128 devices in a mesh: cube: 8 (over x_lo, z), row: 4 (over x_hi, core), col: 4 (over y).
Axes of the slice: x: 4 (x_hi: 2, x_lo: 2; x = x_hi * 2 + x_lo), y: 4, z: 4, core: 2. Of those that a mesh axis runs over, the one named last changes fastest.
Arguments:
- child_update: float32 [32, 2, 4, 128, 128, 128], P(('cube', 'row'), None, None, None, 'col'), may hold values from -13 to 13
- child_map: int32 [2, 16384], replicated, may hold values from -1 to 16383, as said below
- parent_diag: float32 [16384], replicated, may hold values from 0.5 to 2
Outputs:
- updated: float32 [32, 4, 128, 128, 128], P(('cube', 'row'), None, None, 'col')
The draws below stay inside these ranges and needn't reach their ends.
Inputs may be any that keep to these rules, and one draw needn't show every extreme that they name: `child_map`: for each child and each aligned block of 128 child rows, the live rows (entries other than -1) come first and map, strictly increasing, into the same aligned block of 128 parent rows; every block has at least one -1 entry and uses the last parent row of its block.
All inputs are finite; a program needn't handle non-finite values.
Results may differ from the reference program's by a relative error of at most 0.0001.
Values sent between devices are 32-bit elements; how exact they have to be, the bound alone decides.
A program may use at most 192 MiB of HBM per device.

```python
import math
import jax
import jax.numpy as jnp
from jax import lax

FRONT = 16384
K = 1024
TB = 128
RANKS = 512
GRID2 = 32
HALF = 16
TL = 4
CT = 128
CTL = 32
N_COL = 4


def draw_child_update(key, part):
    key_factor = jax.random.fold_in(jax.random.fold_in(key, 7), 0)
    factors = jax.random.normal(key_factor, (2, FRONT, RANKS), jnp.float32)
    gram = jnp.einsum('eik,ejk->eij', factors, factors, precision=lax.Precision.HIGHEST) / RANKS
    gram = gram.reshape(2, TL, 2, HALF, TB, FRONT)
    gram = jnp.transpose(gram, (0, 3, 2, 1, 4, 5)).reshape(GRID2, 2, TL, TB, FRONT)
    gram = gram.reshape(GRID2, 2, TL, TB, CTL, CT // CTL, TB)
    gram = jnp.swapaxes(gram, 4, 5)
    return gram.reshape(GRID2, 2, TL, TB, CT, TB)


def draw_child_map(key, part):
    key_count, key_order = jax.random.split(jax.random.fold_in(key, 11))
    counts = jax.random.randint(key_count, (2, CT), TB * 3 // 8, TB - TB // 16)
    offsets = jnp.arange(TB, dtype=jnp.int32)
    scores = jax.random.randint(key_order, (2, CT, TB), 0, 1 << 20) * TB + offsets
    ranks = jnp.argsort(jnp.argsort(scores, axis=-1), axis=-1).astype(jnp.int32)
    chosen = (ranks < counts[..., None] - 1) | (offsets == TB - 1)
    chosen_rank = jnp.cumsum(chosen.astype(jnp.int32), axis=-1) - 1
    live = jnp.sum(chosen.astype(jnp.int32), axis=-1)
    matches = chosen[..., None, :] & (chosen_rank[..., None, :] == offsets[:, None])
    slot_offset = jnp.sum(jnp.where(matches, offsets[None, :], 0), axis=-1).astype(jnp.int32)
    starts = (jnp.arange(CT, dtype=jnp.int32) * TB)[None, :, None]
    mapped = jnp.where(offsets < live[..., None], starts + slot_offset, -1)
    return mapped.reshape(2, FRONT).astype(jnp.int32)


def setup_inputs(seed: int = 0) -> dict:
    splits = jax.random.split(jax.random.key(seed), 4)
    child_update = draw_child_update(jax.random.fold_in(splits[3], 71), 0)
    child_map = draw_child_map(jax.random.fold_in(splits[3], 71), 0)
    parent_diag = jnp.clip(jnp.exp(jax.random.uniform(splits[2], (FRONT,), jnp.float32, math.log(0.5), math.log(2.0))), 0.5, 2.0)
    return {"child_update": child_update, "child_map": child_map, "parent_diag": parent_diag}


def natural_columns(stored):
    leading = stored.shape[:-2]
    grouped = stored.reshape(leading + (N_COL, CTL, TB))
    grouped = jnp.swapaxes(grouped, -3, -2)
    return grouped.reshape(leading + (FRONT,))

def tile_onehot(tile_map):
    blocks = tile_map.reshape(CT, TB)
    starts = (jnp.arange(CT, dtype=jnp.int32) * TB)[:, None, None]
    offsets = jnp.arange(TB, dtype=jnp.int32)[None, :, None]
    return (blocks[:, None, :] == starts + offsets).astype(jnp.float32)

def reference(child_update, child_map, parent_diag):
    children = child_update.reshape(2, HALF, 2, TL, TB, CT, TB)
    children = jnp.transpose(children, (0, 3, 2, 1, 4, 5, 6)).reshape(2, FRONT, CT, TB)
    children = natural_columns(children)
    front = jnp.diag(parent_diag)
    for sibling in range(2):
        onehot = tile_onehot(child_map[sibling])
        placed = jnp.einsum('tos,tsj->toj', onehot, children[sibling].reshape(CT, TB, FRONT), precision=lax.Precision.HIGHEST)
        placed = jnp.einsum('iuv,uov->iuo', placed.reshape(FRONT, CT, TB), onehot, precision=lax.Precision.HIGHEST)
        front = front + placed.reshape(FRONT, FRONT)
    factor = jnp.linalg.cholesky(front[:K, :K])
    panel = jax.scipy.linalg.solve_triangular(factor, front[:, :K].T, lower=True).T
    trailing = front[:, K:] - jnp.dot(panel.astype(jnp.float32), panel[K:].T.astype(jnp.float32), preferred_element_type=jnp.float32, precision=lax.Precision.HIGHEST)
    whole = jnp.concatenate([panel, trailing], axis=1)
    whole = jnp.transpose(whole.reshape(TL, GRID2, TB, FRONT), (1, 0, 2, 3))
    whole = whole.reshape(GRID2, TL, TB, CTL, N_COL, TB)
    whole = jnp.swapaxes(whole, 3, 4)
    return whole.reshape(GRID2, TL, TB, CT, TB)
```

```python
import functools

import jax
import jax.numpy as jnp
from jax import lax
from jax.experimental import pallas as pl
from jax.experimental.pallas import tpu as pltpu
from jax.sharding import PartitionSpec as P

K = 1024
TB = 128
HI = lax.Precision.HIGHEST
F32 = jnp.float32
MESH = pl.DeviceIdType.MESH
VMEM = pl.BlockSpec(memory_space=pltpu.VMEM)
SMEM = pl.BlockSpec(memory_space=pltpu.SMEM)


def nt(a, b):
    return lax.dot_general(
        a, b, (((1,), (1,)), ((), ())), precision=HI, preferred_element_type=F32
    )


def nn(a, b):
    return lax.dot_general(
        a, b, (((1,), (0,)), ((), ())), precision=HI, preferred_element_type=F32
    )


def place_kernel(raw_ref, got_ref, rmap_ref, cmap_ref, diag_ref, out_ref):
    sub = lax.broadcasted_iota(jnp.int32, (TB, TB), 0)
    lane = lax.broadcasted_iota(jnp.int32, (TB, TB), 1)
    tiles = rmap_ref.shape[1]
    for v in range(2):
        cols = [
            nt(ref[v], (sub == cmap_ref[t, v : v + 1, :]).astype(F32))
            for t, ref in enumerate((raw_ref, got_ref))
        ]
        for j in range(tiles):
            rows = slice(j * TB, (j + 1) * TB)
            total = jnp.where(sub == lane, diag_ref[v * tiles + j : v * tiles + j + 1, :], 0.0)
            for t in range(2):
                hot = (sub == rmap_ref[t, j : j + 1, :]).astype(F32)
                total += nn(hot, cols[t][rows, :])
            out_ref[v, rows, :] = total


def pivot_kernel(piece_ref, out_ref, send, recv, local):
    cube, row, col = lax.axis_index("cube"), lax.axis_index("row"), lax.axis_index("col")
    z, near = lax.rem(cube, 4), cube < 4
    core = lax.rem(row, 2)
    at = lambda cu, ro, co: {"cube": cu, "row": ro, "col": co}
    mates = [at((cube - z) + lax.rem(z + d, 4), row, col) for d in (1, 2, 3)]
    across = [
        at(lax.rem(cube + 4, 8), row, col),
        at(cube, lax.rem(row + 2, 4), col),
        at(lax.rem(cube + 4, 8), lax.rem(row + 2, 4), col),
    ]
    up, down = lax.rem(col + 1, 4), lax.rem(col + 3, 4)
    sides = [at(cube, row, up), at(cube, row, down)]
    other = at(cube, row + 1 - 2 * core, col)
    barrier = pltpu.get_barrier_semaphore()
    for peer in mates + across + sides + [other]:
        pl.semaphore_signal(barrier, inc=1, device_id=peer, device_id_type=MESH)
    pl.semaphore_wait(barrier, 9)

    def copy(c, p, slot, peer):
        return pltpu.make_async_remote_copy(
            src_ref=out_ref.at[c, p],
            dst_ref=out_ref.at[c, p],
            send_sem=send.at[slot],
            recv_sem=recv.at[c, p],
            device_id=peer,
            device_id_type=MESH,
        )

    mine = lax.rem(cube, 2) * 4 + row
    source = cube < 2

    @pl.when(source)
    def _():
        own = pltpu.make_async_copy(piece_ref, out_ref.at[col, mine], local)
        own.start()
        own.wait()
        for i, peer in enumerate(mates):
            copy(col, mine, i, peer).start()

    for zz in range(2):
        p = zz * 4 + row

        @pl.when(near)
        def _():
            @pl.when(z != zz)
            def _():
                copy(col, p, 0, other).wait_recv()

            for i, peer in enumerate(across):
                copy(col, p, 3 + 3 * zz + i, peer).start()

    half = row // 2
    for zz in range(2):
        for hh in range(2):
            p = zz * 4 + hh * 2 + core
            n = zz * 2 + hh

            @pl.when(jnp.logical_or(jnp.logical_not(near), half != hh))
            def _():
                copy(col, p, 0, other).wait_recv()

            copy(col, p, 9 + n, sides[0]).start()
            copy(col, p, 13 + n, sides[1]).start()
            copy(col, p, 17 + n, other).start()
    for zz in range(2):
        for hh in range(2):
            p = zz * 4 + hh * 2 + core
            n = zz * 2 + hh
            copy(down, p, 0, other).wait_recv()
            copy(down, p, 21 + n, other).start()

            @pl.when(core == 0)
            def _():
                copy(down, p, 25 + n, sides[0]).start()

            copy(up, p, 0, other).wait_recv()
            copy(up, p, 29 + n, other).start()

            @pl.when(core == 1)
            def _():
                copy(up, p, 25 + n, sides[1]).start()

    far = lax.rem(col + 2, 4)
    for zz in range(2):
        for hh in range(2):
            p = zz * 4 + hh * 2 + core
            copy(far, p, 0, other).wait_recv()
            copy(far, p, 33 + zz * 2 + hh, other).start()
    for c in range(4):
        for zz in range(2):
            for hh in range(2):
                copy(c, zz * 4 + hh * 2 + 1 - core, 0, other).wait_recv()

    @pl.when(source)
    def _():
        for i in range(3):
            copy(col, mine, i, other).wait_send()

    @pl.when(near)
    def _():
        for i in range(3, 9):
            copy(col, mine, i, other).wait_send()

    for i in range(9, 37):
        copy(col, mine, i, other).wait_send()


def leaf(d_ref, li_ref):
    a_rows = [d_ref[8 * g : 8 * g + 8, :] for g in range(16)]
    lane = lax.broadcasted_iota(jnp.int32, (8, TB), 1)
    sub = lax.broadcasted_iota(jnp.int32, (8, TB), 0)
    b_rows = [(lane == sub + 8 * g).astype(F32) for g in range(16)]
    wide = lambda x: jnp.broadcast_to(x, (8, TB))
    for g0 in range(16):
        j = 8 * g0
        c = [wide(a_rows[g0][:, j + q : j + q + 1]) for q in range(8)]
        e = [[wide(c[q][i : i + 1, :]) if i >= q else None for q in range(8)] for i in range(8)]
        a = [wide(a_rows[g0][q : q + 1, :]) for q in range(8)]
        b = [wide(b_rows[g0][q : q + 1, :]) for q in range(8)]
        more = g0 + 1 < 16
        if more:
            m = [wide(a_rows[g0 + 1][:, j + q : j + q + 1]) for q in range(8)]
        s, t = [None] * 8, [None] * 8
        low = [[None] * 8 for _ in range(8)]
        for q in range(8):
            inv = 1.0 / e[q][q]
            s[q], t[q] = a[q] * inv, b[q] * inv
            for i in range(q + 1, 8):
                low[i][q] = e[i][q] * inv
            for i in range(q + 1, 8):
                for p in range(q + 1, i + 1):
                    e[i][p] = e[i][p] - low[i][q] * e[p][q]
            for i in range(q + 1, 8):
                a[i] = a[i] - low[i][q] * a[q]
                b[i] = b[i] - low[i][q] * b[q]
                if more:
                    m[i] = m[i] - low[i][q] * m[q]
            if more:
                a_rows[g0 + 1] = a_rows[g0 + 1] - m[q] * s[q]
                b_rows[g0 + 1] = b_rows[g0 + 1] - m[q] * t[q]
            li_ref[j + q : j + q + 1, :] = (b[q] * lax.rsqrt(e[q][q]))[0:1, :]
        if g0 + 2 < 16:
            for q in range(7, -1, -1):
                for i in range(q + 1, 8):
                    s[q] = s[q] - low[i][q] * s[i]
                    t[q] = t[q] - low[i][q] * t[i]
            for g in range(g0 + 2, 16):
                m = [wide(a_rows[g][:, j + q : j + q + 1]) for q in range(8)]
                da, db = m[0] * s[0], m[0] * t[0]
                for q in range(1, 8):
                    da, db = da + m[q] * s[q], db + m[q] * t[q]
                a_rows[g] = a_rows[g] - da
                b_rows[g] = b_rows[g] - db


def factor_kernel(col_ref, s_ref, a_ref, y_ref, x_ref, m_ref, li_ref, d_ref):
    blocks = K // TB
    for c in range(4):
        for v in range(2):
            u = 4 * v + c
            for p in range(blocks):
                if p >= u:
                    m_ref[p * TB : (p + 1) * TB, u * TB : (u + 1) * TB] = s_ref[c, p, v]
                else:
                    m_ref[p * TB : (p + 1) * TB, u * TB : (u + 1) * TB] = jnp.zeros((TB, TB), F32)
            m_ref[K:, u * TB : (u + 1) * TB] = a_ref[c, v]

    def step(k, _):
        o = pl.multiple_of(k * TB, TB)
        here = pl.ds(o, TB)
        d_ref[...] = m_ref[here, here]
        leaf(d_ref, li_ref.at[k])
        m_ref[:, here] = nt(m_ref[:, here], li_ref[k])

        def update(j, _):
            q = pl.multiple_of(j * TB, TB)
            there = pl.ds(q, TB)
            m_ref[:, there] = m_ref[:, there] - nt(m_ref[:, here], m_ref[there, here])
            return 0

        lax.fori_loop(k + 1, blocks, update, 0)
        return 0

    lax.fori_loop(0, blocks, step, 0)
    col = col_ref[0]
    for v in range(2):
        y_ref[v] = m_ref[K:, pl.ds(pl.multiple_of((4 * v + col) * TB, TB), TB)]

    def back(i, _):
        k = blocks - 1 - i
        o = pl.multiple_of(k * TB, TB)
        here = pl.ds(o, TB)
        x = nn(m_ref[K:, here], li_ref[k])
        x_ref[:, here] = x

        def update(j, _):
            there = pl.ds(pl.multiple_of(j * TB, TB), TB)
            m_ref[K:, there] = m_ref[K:, there] - nn(x, m_ref[here, there])
            return 0

        lax.fori_loop(0, k, update, 0)
        return 0

    lax.fori_loop(0, blocks, back, 0)


def split(x):
    high = x.astype(jnp.bfloat16)
    return high, (x - high.astype(F32)).astype(jnp.bfloat16)


def finish_kernel(
    at_ref, rinv_ref, kept_ref, got_ref, cinv_ref, g_ref, x_ref, y_ref, diag_ref, out_ref,
    r_ref, wh_ref, wl_ref, xh_ref, xl_ref,
):
    step = pl.program_id(0)
    rows = x_ref.shape[0]

    @pl.when(step == 0)
    def _():
        xh_ref[...], xl_ref[...] = split(x_ref[...])

    for n in range(8):
        for c in range(4):
            for v in range(2):
                u = 4 * v + c
                high, low = split(g_ref[n, c, v])
                wh_ref[n * TB : (n + 1) * TB, u * TB : (u + 1) * TB] = high
                wl_ref[n * TB : (n + 1) * TB, u * TB : (u + 1) * TB] = low
    dims = (((1,), (1,)), ((), ()))
    dot = lambda a, b: lax.dot_general(a, b, dims, preferred_element_type=F32)
    for n in range(8):
        part = slice(n * TB, (n + 1) * TB)
        wh, wl = wh_ref[part, :], wl_ref[part, :]
        r_ref[n * rows : (n + 1) * rows, :] = (
            dot(xl_ref[...], wh) + dot(xh_ref[...], wl)
        ) + dot(xh_ref[...], wh)

    @pl.when(step == 0)
    def _():
        for v in range(2):
            r_ref[v * rows : (v + 1) * rows, :] = -y_ref[v]

    sub = lax.broadcasted_iota(jnp.int32, (TB, TB), 0)
    lane = lax.broadcasted_iota(jnp.int32, (TB, TB), 1)
    base = pl.multiple_of(at_ref[1] * rows + step * TB, TB)
    r_ref[pl.ds(base, TB), :] = r_ref[pl.ds(base, TB), :] - jnp.where(
        sub == lane, diag_ref[pl.ds(step, 1), :], 0.0
    )
    index = [jnp.maximum(cinv_ref[t], 0) for t in range(2)]
    live = [(cinv_ref[t] >= 0).astype(F32) for t in range(2)]
    for j in range(rows // TB):

        def body(o, _):
            value = -r_ref[pl.ds(j * TB + o, 8, stride=rows), :]
            for t, ref in enumerate((kept_ref.at[0, 0], got_ref)):
                s = rinv_ref[t, j * TB + o]
                x = ref[j, jnp.maximum(s, 0)]
                x = jnp.take_along_axis(x, index[t], axis=1)
                value += x * (live[t] * jnp.where(s >= 0, 1.0, 0.0))
            out_ref[0, j, o] = value
            return 0

        lax.fori_loop(0, TB, body, 0, unroll=8)


def inverse(relative):
    offsets = jnp.arange(TB, dtype=jnp.int32)
    hit = relative[..., None, :] == offsets[:, None]
    return jnp.max(jnp.where(hit, offsets, -1), axis=-1)


def on_device(child_update, child_map, parent_diag):
    cube, row, col = lax.axis_index("cube"), lax.axis_index("row"), lax.axis_index("col")
    grid, columns = 32, 4
    position = cube * 4 + row
    sibling = position // (grid // 2)
    block = child_update[0]
    tiles, cols = block.shape[1], block.shape[3]
    rows = tiles * TB
    trade = [(i, i ^ 16) for i in range(grid)]

    panel = jnp.transpose(block[:, :, :, :2, :], (0, 3, 1, 2, 4)).reshape(2, 2, rows, TB)
    raw = lax.dynamic_index_in_dim(panel, sibling, 0, keepdims=False)
    give = lax.dynamic_index_in_dim(panel, 1 - sibling, 0, keepdims=False)
    got = lax.ppermute(give, ("cube", "row"), trade)
    bulk = lax.dynamic_index_in_dim(block, 1 - sibling, 0, keepdims=False)
    bulk, got = lax.optimization_barrier((bulk, got))
    arrived = lax.ppermute(bulk, ("cube", "row"), trade)

    maps = jnp.stack(
        [
            lax.dynamic_index_in_dim(child_map, sibling, 0, keepdims=False),
            lax.dynamic_index_in_dim(child_map, 1 - sibling, 0, keepdims=False),
        ]
    )
    row_maps = lax.dynamic_index_in_dim(
        maps.reshape(2, tiles, grid, TB), position, 2, keepdims=False
    )
    row_tiles = grid * jnp.arange(tiles, dtype=jnp.int32) + position
    row_maps = row_maps - TB * row_tiles[None, :, None]
    col_maps = lax.dynamic_index_in_dim(
        maps.reshape(2, cols, columns, TB), col, 2, keepdims=False
    )
    col_tiles = columns * jnp.arange(cols, dtype=jnp.int32) + col
    col_maps = col_maps - TB * col_tiles[None, :, None]
    diag = lax.dynamic_index_in_dim(
        parent_diag.reshape(tiles, grid, TB), position, 1, keepdims=False
    )
    meets = row_tiles[None, :] == col_tiles[:2, None]
    panel_diag = jnp.where(meets[:, :, None], diag[None], 0.0).reshape(2 * tiles, TB)

    piece = pl.pallas_call(
        place_kernel,
        out_shape=jax.ShapeDtypeStruct((2, rows, TB), F32),
        in_specs=[VMEM] * 5,
        out_specs=VMEM,
    )(raw, got, row_maps, col_maps[:, :2], panel_diag)

    own_rows = lax.all_gather(piece, "col", axis=0)
    pivot = pl.pallas_call(
        pivot_kernel,
        out_shape=jax.ShapeDtypeStruct((4, 8, 2, TB, TB), F32),
        in_specs=[VMEM],
        out_specs=VMEM,
        scratch_shapes=[
            pltpu.SemaphoreType.DMA((37,)),
            pltpu.SemaphoreType.DMA((4, 8)),
            pltpu.SemaphoreType.DMA,
        ],
        compiler_params=pltpu.CompilerParams(collective_id=0, has_side_effects=True),
    )(piece[:, :TB])

    turned = lax.ppermute(
        own_rows, ("row", "col"), [(r * 4 + c, c * 4 + r) for r in range(4) for c in range(4)]
    )
    others = lax.all_gather(turned, "cube", axis=0)

    y, x = pl.pallas_call(
        factor_kernel,
        out_shape=[
            jax.ShapeDtypeStruct((2, rows, TB), F32),
            jax.ShapeDtypeStruct((rows, K), F32),
        ],
        in_specs=[SMEM, VMEM, VMEM],
        out_specs=[VMEM, VMEM],
        scratch_shapes=[
            pltpu.VMEM((K + rows, K), F32),
            pltpu.VMEM((K // TB, TB, TB), F32),
            pltpu.VMEM((TB, TB), F32),
        ],
        cost_estimate=pl.CostEstimate(flops=40_000_000_000, bytes_accessed=8 << 20, transcendentals=0),
    )(col.reshape(1), pivot, own_rows)

    row_inverse = inverse(row_maps).reshape(2, rows)
    solved = jnp.arange(cols) < 2
    col_inverse = jnp.where(solved[None, :, None], -1, inverse(col_maps))
    here = jnp.logical_and(row == col, jnp.logical_or(jnp.arange(tiles) > 0, cube >= 2))
    trailing_diag = jnp.where(here[:, None], diag, 0.0)
    at = jnp.stack([sibling, cube]).astype(jnp.int32)
    return pl.pallas_call(
        finish_kernel,
        out_shape=jax.ShapeDtypeStruct((1, tiles, TB, cols, TB), F32),
        grid_spec=pltpu.PrefetchScalarGridSpec(
            num_scalar_prefetch=2,
            grid=(cols // 8,),
            in_specs=[
                pl.BlockSpec((1, 1, tiles, TB, 8, TB), lambda i, at, _: (0, at[0], 0, 0, i, 0)),
                pl.BlockSpec((tiles, TB, 8, TB), lambda i, *_: (0, 0, i, 0)),
                pl.BlockSpec((2, 8, TB), lambda i, *_: (0, i, 0)),
                pl.BlockSpec((8, 4, 2, TB, TB), lambda i, *_: (0, 0, 0, i, 0)),
                VMEM,
                VMEM,
                VMEM,
            ],
            out_specs=pl.BlockSpec((1, tiles, TB, 8, TB), lambda i, *_: (0, 0, 0, i, 0)),
            scratch_shapes=[
                pltpu.VMEM((8 * rows, TB), F32),
                pltpu.VMEM((8 * TB, K), jnp.bfloat16),
                pltpu.VMEM((8 * TB, K), jnp.bfloat16),
                pltpu.VMEM((rows, K), jnp.bfloat16),
                pltpu.VMEM((rows, K), jnp.bfloat16),
            ],
        ),
    )(at, row_inverse, child_update, arrived, col_inverse, others, x, y, trailing_diag)


def solution(mesh):
    return jax.shard_map(
        on_device,
        mesh=mesh,
        in_specs=(P(("cube", "row"), None, None, None, "col", None), P(), P()),
        out_specs=P(("cube", "row"), None, None, "col", None),
        check_vma=False,
    )
```

```python
import jax
import jax.numpy as jnp
from jax import lax
from jax.experimental import pallas as pl
from jax.experimental.pallas import tpu as pltpu
from jax.sharding import PartitionSpec as P


K = 1024
TB = 128
HI = lax.Precision.HIGHEST
F32 = jnp.float32
MESH = pl.DeviceIdType.MESH
VMEM = pl.BlockSpec(memory_space=pltpu.VMEM)
SMEM = pl.BlockSpec(memory_space=pltpu.SMEM)


def nt(a, b):
    return lax.dot_general(
        a, b, (((1,), (1,)), ((), ())), precision=HI, preferred_element_type=F32
    )


def nn(a, b):
    return lax.dot_general(
        a, b, (((1,), (0,)), ((), ())), precision=HI, preferred_element_type=F32
    )


def place_kernel(raw_ref, got_ref, rmap_ref, cmap_ref, diag_ref, out_ref):
    sub = lax.broadcasted_iota(jnp.int32, (TB, TB), 0)
    lane = lax.broadcasted_iota(jnp.int32, (TB, TB), 1)
    tiles = rmap_ref.shape[2]
    for v in range(2):
        for half in range(2):
            cols = [
                nt(ref[half, v], (sub == cmap_ref[t, v : v + 1, :]).astype(F32))
                for t, ref in enumerate((raw_ref, got_ref))
            ]
            for j in range(tiles):
                rows = slice(j * TB, (j + 1) * TB)
                total = jnp.where(sub == lane, diag_ref[half, v, j : j + 1, :], 0.0)
                for t in range(2):
                    hot = (sub == rmap_ref[t, half, j : j + 1, :]).astype(F32)
                    total += nn(hot, cols[t][rows, :])
                out_ref[half, v, rows, :] = total


def pivot_kernel(piece_ref, out_ref, send, recv, local):
    cube, row, col = lax.axis_index("cube"), lax.axis_index("row"), lax.axis_index("col")
    z = lax.rem(cube, 4)
    core = lax.rem(row, 2)
    at = lambda cu, ro, co: {"cube": cu, "row": ro, "col": co}
    mates = [at((cube - z) + lax.rem(z + d, 4), row, col) for d in (1, 2, 3)]
    across = at(lax.rem(cube + 4, 8), lax.rem(row + 2, 4), col)
    up, down = lax.rem(col + 1, 4), lax.rem(col + 3, 4)
    sides = [at(cube, row, up), at(cube, row, down)]
    other = at(cube, row + 1 - 2 * core, col)
    barrier = pltpu.get_barrier_semaphore()
    for peer in mates + [across] + sides + [other]:
        pl.semaphore_signal(barrier, inc=1, device_id=peer, device_id_type=MESH)
    pl.semaphore_wait(barrier, 7)

    def copy(c, p, slot, peer, width):
        part = out_ref.at[c, p, pl.ds(0, width)]
        return pltpu.make_async_remote_copy(
            src_ref=part,
            dst_ref=part,
            send_sem=send.at[slot],
            recv_sem=recv.at[c, p],
            device_id=peer,
            device_id_type=MESH,
        )

    for zz in range(2):
        mine = zz * 4 + row

        @pl.when(z == zz)
        def _():
            part = pl.ds(0, zz + 1)
            own = pltpu.make_async_copy(piece_ref.at[part], out_ref.at[col, mine, part], local)
            own.start()
            own.wait()
            for i, peer in enumerate(mates):
                copy(col, mine, i, peer, zz + 1).start()

    for zz in range(2):
        p = zz * 4 + row
        n = zz

        @pl.when(z != zz)
        def _():
            copy(col, p, 0, other, zz + 1).wait_recv()

        copy(col, p, 3 + zz, across, zz + 1).start()
        copy(col, p, 5 + n, sides[0], zz + 1).start()
        copy(col, p, 7 + n, sides[1], zz + 1).start()
        copy(col, p, 9 + n, other, zz + 1).start()
    opposite = lax.rem(row + 2, 4)
    for zz in range(2):
        p = zz * 4 + opposite
        n = zz
        copy(col, p, 0, other, zz + 1).wait_recv()
        copy(col, p, 11 + n, sides[0], zz + 1).start()
        copy(col, p, 13 + n, sides[1], zz + 1).start()
        copy(col, p, 15 + n, other, zz + 1).start()
    for i, who in enumerate((row, opposite)):
        for zz in range(2):
            p = zz * 4 + who
            n = i * 2 + zz
            copy(down, p, 0, other, zz + 1).wait_recv()
            copy(down, p, 17 + n, other, zz + 1).start()

            @pl.when(core == 0)
            def _():
                copy(down, p, 21 + n, sides[0], zz + 1).start()

            copy(up, p, 0, other, zz + 1).wait_recv()
            copy(up, p, 25 + n, other, zz + 1).start()

            @pl.when(core == 1)
            def _():
                copy(up, p, 21 + n, sides[1], zz + 1).start()

    far = lax.rem(col + 2, 4)
    for i, who in enumerate((row, opposite)):
        for zz in range(2):
            p = zz * 4 + who
            copy(far, p, 0, other, zz + 1).wait_recv()
            copy(far, p, 29 + i * 2 + zz, other, zz + 1).start()
    for c in range(4):
        for zz in range(2):
            for hh in range(2):
                copy(c, zz * 4 + hh * 2 + 1 - core, 0, other, zz + 1).wait_recv()

    for zz in range(2):

        @pl.when(z == zz)
        def _():
            for i in range(3):
                copy(col, row, i, other, zz + 1).wait_send()

        for i in (3, 5, 7, 9, 11, 13, 15, 17, 19, 21, 23, 25, 27, 29, 31):
            copy(col, row, i + zz, other, zz + 1).wait_send()


def leaf(d_ref, li_ref):
    a_rows = [d_ref[8 * g : 8 * g + 8, :] for g in range(16)]
    lane = lax.broadcasted_iota(jnp.int32, (8, TB), 1)
    sub = lax.broadcasted_iota(jnp.int32, (8, TB), 0)
    b_rows = [(lane == sub + 8 * g).astype(F32) for g in range(16)]
    wide = lambda x: jnp.broadcast_to(x, (8, TB))
    for g0 in range(16):
        j = 8 * g0
        c = [wide(a_rows[g0][:, j + q : j + q + 1]) for q in range(8)]
        e = [[wide(c[q][i : i + 1, :]) if i >= q else None for q in range(8)] for i in range(8)]
        a = [wide(a_rows[g0][q : q + 1, :]) for q in range(8)]
        b = [wide(b_rows[g0][q : q + 1, :]) for q in range(8)]
        more = g0 + 1 < 16
        if more:
            m = [wide(a_rows[g0 + 1][:, j + q : j + q + 1]) for q in range(8)]
        s, t = [None] * 8, [None] * 8
        low = [[None] * 8 for _ in range(8)]
        for q in range(8):
            inv = 1.0 / e[q][q]
            s[q], t[q] = a[q] * inv, b[q] * inv
            for i in range(q + 1, 8):
                low[i][q] = e[i][q] * inv
            for i in range(q + 1, 8):
                for p in range(q + 1, i + 1):
                    e[i][p] = e[i][p] - low[i][q] * e[p][q]
            for i in range(q + 1, 8):
                a[i] = a[i] - low[i][q] * a[q]
                b[i] = b[i] - low[i][q] * b[q]
                if more:
                    m[i] = m[i] - low[i][q] * m[q]
            if more:
                a_rows[g0 + 1] = a_rows[g0 + 1] - m[q] * s[q]
                b_rows[g0 + 1] = b_rows[g0 + 1] - m[q] * t[q]
            li_ref[j + q : j + q + 1, :] = (b[q] * lax.rsqrt(e[q][q]))[0:1, :]
        if g0 + 2 < 16:
            for q in range(7, -1, -1):
                for i in range(q + 1, 8):
                    s[q] = s[q] - low[i][q] * s[i]
                    t[q] = t[q] - low[i][q] * t[i]
            for g in range(g0 + 2, 16):
                m = [wide(a_rows[g][:, j + q : j + q + 1]) for q in range(8)]
                da, db = m[0] * s[0], m[0] * t[0]
                for q in range(1, 8):
                    da, db = da + m[q] * s[q], db + m[q] * t[q]
                a_rows[g] = a_rows[g] - da
                b_rows[g] = b_rows[g] - db


def factor_kernel(col_ref, s_ref, a_ref, y_ref, x_ref, m_ref, li_ref, d_ref):
    blocks = K // TB
    for c in range(4):
        for v in range(2):
            u = 4 * v + c
            for p in range(blocks):
                if p >= u:
                    m_ref[p * TB : (p + 1) * TB, u * TB : (u + 1) * TB] = s_ref[c, p, v]
                else:
                    m_ref[p * TB : (p + 1) * TB, u * TB : (u + 1) * TB] = jnp.zeros((TB, TB), F32)
            m_ref[K:, u * TB : (u + 1) * TB] = a_ref[c, v]

    def step(k, _):
        o = pl.multiple_of(k * TB, TB)
        here = pl.ds(o, TB)
        d_ref[...] = m_ref[here, here]
        leaf(d_ref, li_ref.at[k])
        m_ref[:, here] = nt(m_ref[:, here], li_ref[k])

        def update(j, _):
            q = pl.multiple_of(j * TB, TB)
            there = pl.ds(q, TB)
            m_ref[:, there] = m_ref[:, there] - nt(m_ref[:, here], m_ref[there, here])
            return 0

        lax.fori_loop(k + 1, blocks, update, 0)
        return 0

    lax.fori_loop(0, blocks, step, 0)
    col = col_ref[0]
    for v in range(2):
        y_ref[v] = m_ref[K:, pl.ds(pl.multiple_of((4 * v + col) * TB, TB), TB)]

    def back(i, _):
        k = blocks - 1 - i
        o = pl.multiple_of(k * TB, TB)
        here = pl.ds(o, TB)
        x = nn(m_ref[K:, here], li_ref[k])
        x_ref[:, here] = x

        def update(j, _):
            there = pl.ds(pl.multiple_of(j * TB, TB), TB)
            m_ref[K:, there] = m_ref[K:, there] - nn(x, m_ref[here, there])
            return 0

        lax.fori_loop(0, k, update, 0)
        return 0

    lax.fori_loop(0, blocks, back, 0)


def split(x):
    high = x.astype(jnp.bfloat16)
    return high, (x - high.astype(F32)).astype(jnp.bfloat16)


def place_rows(ref, j, t, rinv_ref, index, live, o):
    s = rinv_ref[t, j * TB + o]
    x = jnp.take_along_axis(ref[j, jnp.maximum(s, 0)], index, axis=1)
    return x * (live * jnp.where(s >= 0, 1.0, 0.0))


def update_kernel(
    at_ref, rinv_ref, kept_ref, cinv_ref, g_ref, x_ref, y_ref, diag_ref, out_ref,
    r_ref, wh_ref, wl_ref, xh_ref, xl_ref,
):
    step = pl.program_id(0)
    rows = x_ref.shape[0]

    @pl.when(step == 0)
    def _():
        xh_ref[...], xl_ref[...] = split(x_ref[...])

    for n in range(8):
        part = slice(n * TB, (n + 1) * TB)
        for m in range(4):
            q = lax.rem(at_ref[2] + n // 4 + 4 - m, 4)
            for v in range(2):
                high, low = split(g_ref[(n % 4) * 2 + n // 4, m, v])
                there = pl.ds(pl.multiple_of((4 * v + q) * TB, TB), TB)
                wh_ref[part, there] = high
                wl_ref[part, there] = low
    dims = (((1,), (1,)), ((), ()))
    dot = lambda a, b: lax.dot_general(a, b, dims, preferred_element_type=F32)
    for n in range(8):
        part = slice(n * TB, (n + 1) * TB)
        wh, wl = wh_ref[part, :], wl_ref[part, :]
        r_ref[n * rows : (n + 1) * rows, :] = (
            dot(xl_ref[...], wh) + dot(xh_ref[...], wl)
        ) + dot(xh_ref[...], wh)

    @pl.when(step == 0)
    def _():
        for v in range(2):
            r_ref[v * rows : (v + 1) * rows, :] = -y_ref[v]

    sub = lax.broadcasted_iota(jnp.int32, (TB, TB), 0)
    lane = lax.broadcasted_iota(jnp.int32, (TB, TB), 1)
    base = pl.multiple_of(at_ref[1] * rows + step * TB, TB)
    r_ref[pl.ds(base, TB), :] = r_ref[pl.ds(base, TB), :] - jnp.where(
        sub == lane, diag_ref[pl.ds(step, 1), :], 0.0
    )
    index, live = jnp.maximum(cinv_ref[0], 0), (cinv_ref[0] >= 0).astype(F32)
    for j in range(rows // TB):

        def body(o, _):
            value = place_rows(kept_ref.at[0, 0], j, 0, rinv_ref, index, live, o)
            out_ref[j, o] = value - r_ref[pl.ds(j * TB + o, 8, stride=rows), :]
            return 0

        lax.fori_loop(0, TB, body, 0, unroll=8)


def finish_kernel(rinv_ref, got_ref, cinv_ref, part_ref, out_ref):
    index, live = jnp.maximum(cinv_ref[1], 0), (cinv_ref[1] >= 0).astype(F32)
    for j in range(got_ref.shape[0]):

        def body(o, _):
            value = place_rows(got_ref, j, 1, rinv_ref, index, live, o)
            out_ref[0, j, o] = value + part_ref[j, o]
            return 0

        lax.fori_loop(0, TB, body, 0, unroll=8)


def inverse(relative):
    offsets = jnp.arange(TB, dtype=jnp.int32)
    hit = relative[..., None, :] == offsets[:, None]
    return jnp.max(jnp.where(hit, offsets, -1), axis=-1)


def on_device(child_update, child_map, parent_diag):
    cube, row, col = lax.axis_index("cube"), lax.axis_index("row"), lax.axis_index("col")
    grid, columns = 32, 4
    position = cube * 4 + row
    sibling = position // (grid // 2)
    block = child_update[0]
    tiles, cols = block.shape[1], block.shape[3]
    rows = tiles * TB
    trade = [(i, i ^ 16) for i in range(grid)]

    raw = jnp.transpose(block[:, :, :, :2, :], (0, 3, 1, 2, 4)).reshape(2, 2, rows, TB)
    got = lax.ppermute(raw, ("cube", "row"), trade)
    bulk = lax.dynamic_index_in_dim(block, 1 - sibling, 0, keepdims=False)
    bulk, got = lax.optimization_barrier((bulk, got))
    arrived = lax.ppermute(bulk, ("cube", "row"), trade)

    maps = jnp.stack(
        [
            lax.dynamic_index_in_dim(child_map, sibling, 0, keepdims=False),
            lax.dynamic_index_in_dim(child_map, 1 - sibling, 0, keepdims=False),
        ]
    )
    within = position % 16
    pair_tiles = (
        grid * jnp.arange(tiles, dtype=jnp.int32)[None, :]
        + 16 * jnp.arange(2, dtype=jnp.int32)[:, None]
        + within
    )
    pair_maps = jnp.swapaxes(
        lax.dynamic_index_in_dim(
            maps.reshape(2, tiles, 2, 16, TB), within, 3, keepdims=False
        ),
        1,
        2,
    )
    pair_maps = pair_maps - TB * pair_tiles[None, :, :, None]
    row_maps = lax.dynamic_index_in_dim(pair_maps, sibling, 1, keepdims=False)
    col_maps = lax.dynamic_index_in_dim(
        maps.reshape(2, cols, columns, TB), col, 2, keepdims=False
    )
    col_tiles = columns * jnp.arange(cols, dtype=jnp.int32) + col
    col_maps = col_maps - TB * col_tiles[None, :, None]
    pair_diag = jnp.swapaxes(
        lax.dynamic_index_in_dim(
            parent_diag.reshape(tiles, 2, 16, TB), within, 2, keepdims=False
        ),
        0,
        1,
    )
    diag = lax.dynamic_index_in_dim(pair_diag, sibling, 0, keepdims=False)
    meets = pair_tiles[:, None, :] == col_tiles[None, :2, None]
    panel_diag = jnp.where(meets[..., None], pair_diag[:, None], 0.0)

    pieces = pl.pallas_call(
        place_kernel,
        out_shape=jax.ShapeDtypeStruct((2, 2, rows, TB), F32),
        in_specs=[VMEM] * 5,
        out_specs=VMEM,
    )(raw, got, pair_maps, col_maps[:, :2], panel_diag)

    even = lax.dynamic_index_in_dim(pieces, col % 2, 0, keepdims=False)
    odd = lax.dynamic_index_in_dim(pieces, 1 - col % 2, 0, keepdims=False)
    quarters = []
    for m in range(4):
        pairs = []
        for s in range(2):
            for z in range(4):
                for half in range(2):
                    for core in range(2):
                        for y in range(4):
                            kind = (m + y) % 4
                            far, h = kind // 2, kind % 2
                            source = ((s * 4 + z) * 4 + half * 2 + core) * 4 + y
                            target = ((s ^ far) * 4 + z) * 4 + (half ^ far) * 2 + h
                            pairs.append((source, target * 4 + half * 2 + core))
        quarters.append(lax.ppermute(even if m % 2 == 0 else odd, ("cube", "row", "col"), pairs))
    turned = jnp.stack(quarters)
    groups = [
        [(s * 4 + z) * 4 + half * 2 + core for z in range(4) for core in range(2)]
        for s in range(2)
        for half in range(2)
    ]
    others = lax.all_gather(turned, ("cube", "row"), axis=0, axis_index_groups=groups)

    own_rows = lax.all_gather(
        lax.dynamic_index_in_dim(pieces, sibling, 0, keepdims=False), "col", axis=0
    )
    pivot = pl.pallas_call(
        pivot_kernel,
        out_shape=jax.ShapeDtypeStruct((4, 8, 2, TB, TB), F32),
        in_specs=[VMEM],
        out_specs=VMEM,
        scratch_shapes=[
            pltpu.SemaphoreType.DMA((33,)),
            pltpu.SemaphoreType.DMA((4, 8)),
            pltpu.SemaphoreType.DMA,
        ],
        compiler_params=pltpu.CompilerParams(collective_id=0, has_side_effects=True),
    )(pieces[0, :, :TB])

    y, x = pl.pallas_call(
        factor_kernel,
        out_shape=[
            jax.ShapeDtypeStruct((2, rows, TB), F32),
            jax.ShapeDtypeStruct((rows, K), F32),
        ],
        in_specs=[SMEM, VMEM, VMEM],
        out_specs=[VMEM, VMEM],
        scratch_shapes=[
            pltpu.VMEM((K + rows, K), F32),
            pltpu.VMEM((K // TB, TB, TB), F32),
            pltpu.VMEM((TB, TB), F32),
        ],
        cost_estimate=pl.CostEstimate(flops=40_000_000_000, bytes_accessed=8 << 20, transcendentals=0),
    )(col.reshape(1), pivot, own_rows)

    row_inverse = inverse(row_maps).reshape(2, rows)
    solved = jnp.arange(cols) < 2
    col_inverse = jnp.where(solved[None, :, None], -1, inverse(col_maps))
    here = jnp.logical_and(row == col, jnp.logical_or(jnp.arange(tiles) > 0, cube >= 2))
    trailing_diag = jnp.where(here[:, None], diag, 0.0)
    crossed = (row // 2 != col // 2).astype(jnp.int32)
    at = jnp.stack([sibling, cube, 2 * crossed]).astype(jnp.int32)
    part = pl.pallas_call(
        update_kernel,
        out_shape=jax.ShapeDtypeStruct((tiles, TB, cols, TB), F32),
        grid_spec=pltpu.PrefetchScalarGridSpec(
            num_scalar_prefetch=2,
            grid=(cols // 8,),
            in_specs=[
                pl.BlockSpec((1, 1, tiles, TB, 8, TB), lambda i, at, _: (0, at[0], 0, 0, i, 0)),
                pl.BlockSpec((2, 8, TB), lambda i, *_: (0, i, 0)),
                pl.BlockSpec((8, 4, 2, TB, TB), lambda i, *_: (0, 0, 0, i, 0)),
                VMEM,
                VMEM,
                VMEM,
            ],
            out_specs=pl.BlockSpec((tiles, TB, 8, TB), lambda i, *_: (0, 0, i, 0)),
            scratch_shapes=[
                pltpu.VMEM((8 * rows, TB), F32),
                pltpu.VMEM((8 * TB, K), jnp.bfloat16),
                pltpu.VMEM((8 * TB, K), jnp.bfloat16),
                pltpu.VMEM((rows, K), jnp.bfloat16),
                pltpu.VMEM((rows, K), jnp.bfloat16),
            ],
        ),
        cost_estimate=pl.CostEstimate(flops=26_000_000_000, bytes_accessed=32 << 20, transcendentals=0),
    )(at, row_inverse, child_update, col_inverse, others, x, y, trailing_diag)
    return pl.pallas_call(
        finish_kernel,
        out_shape=jax.ShapeDtypeStruct((1, tiles, TB, cols, TB), F32),
        grid_spec=pltpu.PrefetchScalarGridSpec(
            num_scalar_prefetch=1,
            grid=(cols // 8,),
            in_specs=[
                pl.BlockSpec((tiles, TB, 8, TB), lambda i, *_: (0, 0, i, 0)),
                pl.BlockSpec((2, 8, TB), lambda i, *_: (0, i, 0)),
                pl.BlockSpec((tiles, TB, 8, TB), lambda i, *_: (0, 0, i, 0)),
            ],
            out_specs=pl.BlockSpec((1, tiles, TB, 8, TB), lambda i, *_: (0, 0, 0, i, 0)),
        ),
    )(row_inverse, arrived, col_inverse, part)


def solution(mesh):
    return jax.shard_map(
        on_device,
        mesh=mesh,
        in_specs=(P(("cube", "row"), None, None, None, "col", None), P(), P()),
        out_specs=P(("cube", "row"), None, None, "col", None),
        check_vma=False,
    )
```

```python
import jax
import jax.numpy as jnp
from jax import lax
from jax.experimental import pallas as pl
from jax.experimental.pallas import tpu as pltpu
from jax.sharding import PartitionSpec as P


K = 1024
TB = 128
HI = lax.Precision.HIGHEST
F32 = jnp.float32
MESH = pl.DeviceIdType.MESH
VMEM = pl.BlockSpec(memory_space=pltpu.VMEM)
SMEM = pl.BlockSpec(memory_space=pltpu.SMEM)


def nt(a, b):
    return lax.dot_general(
        a, b, (((1,), (1,)), ((), ())), precision=HI, preferred_element_type=F32
    )


def nn(a, b):
    return lax.dot_general(
        a, b, (((1,), (0,)), ((), ())), precision=HI, preferred_element_type=F32
    )


def place_kernel(raw_ref, got_ref, rmap_ref, cmap_ref, diag_ref, out_ref):
    sub = lax.broadcasted_iota(jnp.int32, (TB, TB), 0)
    lane = lax.broadcasted_iota(jnp.int32, (TB, TB), 1)
    tiles = rmap_ref.shape[2]
    for v in range(2):
        for half in range(2):
            cols = [
                nt(ref[half, v], (sub == cmap_ref[t, v : v + 1, :]).astype(F32))
                for t, ref in enumerate((raw_ref, got_ref))
            ]
            for j in range(tiles):
                rows = slice(j * TB, (j + 1) * TB)
                total = jnp.where(sub == lane, diag_ref[half, v, j : j + 1, :], 0.0)
                for t in range(2):
                    hot = (sub == rmap_ref[t, half, j : j + 1, :]).astype(F32)
                    total += nn(hot, cols[t][rows, :])
                out_ref[half, v, rows, :] = total


def pivot_kernel(piece_ref, out_ref, send, recv, local):
    cube, row, col = lax.axis_index("cube"), lax.axis_index("row"), lax.axis_index("col")
    z = lax.rem(cube, 4)
    core = lax.rem(row, 2)
    at = lambda cu, ro, co: {"cube": cu, "row": ro, "col": co}
    mates = [at((cube - z) + lax.rem(z + d, 4), row, col) for d in (1, 2, 3)]
    across = at(lax.rem(cube + 4, 8), lax.rem(row + 2, 4), col)
    up, down = lax.rem(col + 1, 4), lax.rem(col + 3, 4)
    sides = [at(cube, row, up), at(cube, row, down)]
    other = at(cube, row + 1 - 2 * core, col)
    barrier = pltpu.get_barrier_semaphore()
    for peer in mates + [across] + sides + [other]:
        pl.semaphore_signal(barrier, inc=1, device_id=peer, device_id_type=MESH)
    pl.semaphore_wait(barrier, 7)

    def copy(c, p, slot, peer, width):
        part = out_ref.at[c, p, pl.ds(0, width)]
        return pltpu.make_async_remote_copy(
            src_ref=part,
            dst_ref=part,
            send_sem=send.at[slot],
            recv_sem=recv.at[c, p],
            device_id=peer,
            device_id_type=MESH,
        )

    for zz in range(2):
        mine = zz * 4 + row

        @pl.when(z == zz)
        def _():
            part = pl.ds(0, zz + 1)
            own = pltpu.make_async_copy(piece_ref.at[part], out_ref.at[col, mine, part], local)
            own.start()
            own.wait()
            for i, peer in enumerate(mates):
                copy(col, mine, i, peer, zz + 1).start()

    for zz in range(2):
        p = zz * 4 + row
        n = zz

        @pl.when(z != zz)
        def _():
            copy(col, p, 0, other, zz + 1).wait_recv()

        copy(col, p, 3 + zz, across, zz + 1).start()
        copy(col, p, 5 + n, sides[0], zz + 1).start()
        copy(col, p, 7 + n, sides[1], zz + 1).start()
        copy(col, p, 9 + n, other, zz + 1).start()
    opposite = lax.rem(row + 2, 4)
    for zz in range(2):
        p = zz * 4 + opposite
        n = zz
        copy(col, p, 0, other, zz + 1).wait_recv()
        copy(col, p, 11 + n, sides[0], zz + 1).start()
        copy(col, p, 13 + n, sides[1], zz + 1).start()
        copy(col, p, 15 + n, other, zz + 1).start()
    for i, who in enumerate((row, opposite)):
        for zz in range(2):
            p = zz * 4 + who
            n = i * 2 + zz
            copy(down, p, 0, other, zz + 1).wait_recv()
            copy(down, p, 17 + n, other, zz + 1).start()

            @pl.when(core == 0)
            def _():
                copy(down, p, 21 + n, sides[0], zz + 1).start()

            copy(up, p, 0, other, zz + 1).wait_recv()
            copy(up, p, 25 + n, other, zz + 1).start()

            @pl.when(core == 1)
            def _():
                copy(up, p, 21 + n, sides[1], zz + 1).start()

    far = lax.rem(col + 2, 4)
    for i, who in enumerate((row, opposite)):
        for zz in range(2):
            p = zz * 4 + who
            copy(far, p, 0, other, zz + 1).wait_recv()
            copy(far, p, 29 + i * 2 + zz, other, zz + 1).start()
    for c in range(4):
        for zz in range(2):
            for hh in range(2):
                copy(c, zz * 4 + hh * 2 + 1 - core, 0, other, zz + 1).wait_recv()

    for zz in range(2):

        @pl.when(z == zz)
        def _():
            for i in range(3):
                copy(col, row, i, other, zz + 1).wait_send()

        for i in (3, 5, 7, 9, 11, 13, 15, 17, 19, 21, 23, 25, 27, 29, 31):
            copy(col, row, i + zz, other, zz + 1).wait_send()


def leaf(d_ref, li_ref):
    a_rows = [d_ref[8 * g : 8 * g + 8, :] for g in range(16)]
    lane = lax.broadcasted_iota(jnp.int32, (8, TB), 1)
    sub = lax.broadcasted_iota(jnp.int32, (8, TB), 0)
    b_rows = [(lane == sub + 8 * g).astype(F32) for g in range(16)]
    wide = lambda x: jnp.broadcast_to(x, (8, TB))
    for g0 in range(16):
        j = 8 * g0
        c = [wide(a_rows[g0][:, j + q : j + q + 1]) for q in range(8)]
        e = [[wide(c[q][i : i + 1, :]) if i >= q else None for q in range(8)] for i in range(8)]
        a = [wide(a_rows[g0][q : q + 1, :]) for q in range(8)]
        b = [wide(b_rows[g0][q : q + 1, :]) for q in range(8)]
        more = g0 + 1 < 16
        if more:
            m = [wide(a_rows[g0 + 1][:, j + q : j + q + 1]) for q in range(8)]
        s, t = [None] * 8, [None] * 8
        low = [[None] * 8 for _ in range(8)]
        for q in range(8):
            inv = 1.0 / e[q][q]
            s[q], t[q] = a[q] * inv, b[q] * inv
            for i in range(q + 1, 8):
                low[i][q] = e[i][q] * inv
            for i in range(q + 1, 8):
                for p in range(q + 1, i + 1):
                    e[i][p] = e[i][p] - low[i][q] * e[p][q]
            for i in range(q + 1, 8):
                a[i] = a[i] - low[i][q] * a[q]
                b[i] = b[i] - low[i][q] * b[q]
                if more:
                    m[i] = m[i] - low[i][q] * m[q]
            if more:
                a_rows[g0 + 1] = a_rows[g0 + 1] - m[q] * s[q]
                b_rows[g0 + 1] = b_rows[g0 + 1] - m[q] * t[q]
            li_ref[j + q : j + q + 1, :] = (b[q] * lax.rsqrt(e[q][q]))[0:1, :]
        if g0 + 2 < 16:
            for q in range(7, -1, -1):
                for i in range(q + 1, 8):
                    s[q] = s[q] - low[i][q] * s[i]
                    t[q] = t[q] - low[i][q] * t[i]
            for g in range(g0 + 2, 16):
                m = [wide(a_rows[g][:, j + q : j + q + 1]) for q in range(8)]
                da, db = m[0] * s[0], m[0] * t[0]
                for q in range(1, 8):
                    da, db = da + m[q] * s[q], db + m[q] * t[q]
                a_rows[g] = a_rows[g] - da
                b_rows[g] = b_rows[g] - db


def factor_kernel(col_ref, s_ref, a_ref, y_ref, x_ref, m_ref, li_ref, d_ref):
    blocks = K // TB
    for c in range(4):
        for v in range(2):
            u = 4 * v + c
            for p in range(u, blocks):
                m_ref[p * TB : (p + 1) * TB, u * TB : (u + 1) * TB] = s_ref[c, p, v]
            m_ref[K:, u * TB : (u + 1) * TB] = a_ref[c, v]

    pair_width = 2 * TB

    def step(k, _):
        here = pl.ds(pl.multiple_of(k * TB, TB), TB)
        d_ref[...] = m_ref[here, here]
        leaf(d_ref, li_ref.at[k])
        m_ref[:, here] = nt(m_ref[:, here], li_ref[k])

        @pl.when(lax.rem(k, 2) == 0)
        def _():
            after = pl.ds(pl.multiple_of((k + 1) * TB, TB), TB)
            m_ref[:, after] = m_ref[:, after] - nt(m_ref[:, here], m_ref[after, here])

        @pl.when(lax.rem(k, 2) == 1)
        def _():
            pair = pl.ds(pl.multiple_of((k - 1) * TB, TB), pair_width)

            def trail(i, _):
                part = pl.ds(pl.multiple_of(i * pair_width, pair_width), pair_width)
                m_ref[:, part] = m_ref[:, part] - nt(m_ref[:, pair], m_ref[part, pair])
                return 0

            lax.fori_loop((k + 1) // 2, blocks // 2, trail, 0)

        return 0

    lax.fori_loop(0, blocks, step, 0)
    col = col_ref[0]
    for v in range(2):
        y_ref[v] = m_ref[K:, pl.ds(pl.multiple_of((4 * v + col) * TB, TB), TB)]

    def back(i, _):
        n = blocks // 2 - 1 - i
        first = pl.ds(pl.multiple_of(n * pair_width, TB), TB)
        last = pl.ds(pl.multiple_of(n * pair_width + TB, TB), TB)
        pair = pl.ds(pl.multiple_of(n * pair_width, pair_width), pair_width)
        x_ref[:, last] = nn(m_ref[K:, last], li_ref[2 * n + 1])
        rest = m_ref[K:, first] - nn(x_ref[:, last], m_ref[last, first])
        x_ref[:, first] = nn(rest, li_ref[2 * n])

        def lead(j, _):
            part = pl.ds(pl.multiple_of(j * pair_width, pair_width), pair_width)
            m_ref[K:, part] = m_ref[K:, part] - nn(x_ref[:, pair], m_ref[pair, part])
            return 0

        lax.fori_loop(0, n, lead, 0)
        return 0

    lax.fori_loop(0, blocks // 2, back, 0)


def split(x):
    high = x.astype(jnp.bfloat16)
    return high, (x - high.astype(F32)).astype(jnp.bfloat16)


def place_rows(t, rinv_ref, cinv_ref, from_ref, part_ref, out_ref):
    groups = range(0, from_ref.shape[-2], 8)
    index = [jnp.maximum(cinv_ref[t, g : g + 8], 0) for g in groups]
    live = [(cinv_ref[t, g : g + 8] >= 0).astype(F32) for g in groups]
    base = pl.program_id(0) * TB

    def body(o, _):
        s = rinv_ref[t, base + o]
        weight = jnp.where(s >= 0, 1.0, 0.0)
        s = jnp.maximum(s, 0)
        for g, at, keep in zip(groups, index, live):
            x = jnp.take_along_axis(from_ref[s, g : g + 8], at, axis=1) * (keep * weight)
            if part_ref is not None:
                x += part_ref[o, g : g + 8]
            out_ref[o, g : g + 8] = x
        return 0

    lax.fori_loop(0, TB, body, 0, unroll=16)


def keep_kernel(at_ref, rinv_ref, kept_ref, cinv_ref, out_ref):
    place_rows(0, rinv_ref, cinv_ref, kept_ref.at[0, 0, 0], None, out_ref.at[0])


def finish_kernel(rinv_ref, got_ref, cinv_ref, part_ref, out_ref):
    place_rows(1, rinv_ref, cinv_ref, got_ref.at[0], part_ref.at[0], out_ref.at[0, 0])


def update_kernel(
    at_ref, kept_ref, g_ref, x_ref, y_ref, diag_ref, out_ref, wh_ref, wl_ref, xh_ref, xl_ref
):
    step = pl.program_id(0)
    tiles = kept_ref.shape[0]

    @pl.when(step == 0)
    def _():
        xh_ref[...], xl_ref[...] = split(x_ref[...])

    for n in range(8):
        part = slice(n * TB, (n + 1) * TB)
        for m in range(4):
            q = lax.rem(at_ref[2] + n // 4 + 4 - m, 4)
            for v in range(2):
                high, low = split(g_ref[(n % 4) * 2 + n // 4, m, v])
                there = pl.ds(pl.multiple_of((4 * v + q) * TB, TB), TB)
                wh_ref[part, there] = high
                wl_ref[part, there] = low
    dims = (((1,), (1,)), ((), ()))
    dot = lambda a, b: lax.dot_general(a, b, dims, preferred_element_type=F32)
    sub = lax.broadcasted_iota(jnp.int32, (TB, TB), 0)
    lane = lax.broadcasted_iota(jnp.int32, (TB, TB), 1)
    diag = jnp.where(sub == lane, diag_ref[pl.ds(step, 1), :], 0.0)
    for n in range(0, 8, 2):
        part = slice(n * TB, (n + 2) * TB)
        wh, wl = wh_ref[part, :], wl_ref[part, :]
        r = (dot(xl_ref[...], wh) + dot(xh_ref[...], wl)) + dot(xh_ref[...], wh)
        for i in range(2):
            for j in range(tiles):
                meets = jnp.logical_and(at_ref[1] == n + i, step == j)
                value = kept_ref[j, :, n + i, :] - r[j * TB : (j + 1) * TB, i * TB : (i + 1) * TB]
                out_ref[j, :, n + i, :] = value + diag * jnp.where(meets, 1.0, 0.0)

    @pl.when(step == 0)
    def _():
        for v in range(2):
            for j in range(tiles):
                out_ref[j, :, v, :] = y_ref[v, j * TB : (j + 1) * TB, :]


def inverse(relative):
    offsets = jnp.arange(TB, dtype=jnp.int32)
    hit = relative[..., None, :] == offsets[:, None]
    return jnp.max(jnp.where(hit, offsets, -1), axis=-1)


def on_device(child_update, child_map, parent_diag):
    cube, row, col = lax.axis_index("cube"), lax.axis_index("row"), lax.axis_index("col")
    grid, columns = 32, 4
    position = cube * 4 + row
    sibling = position // (grid // 2)
    block = child_update[0]
    tiles, cols = block.shape[1], block.shape[3]
    rows = tiles * TB
    trade = [(i, i ^ 16) for i in range(grid)]

    raw = jnp.transpose(block[:, :, :, :2, :], (0, 3, 1, 2, 4)).reshape(2, 2, rows, TB)
    got = lax.ppermute(raw, ("cube", "row"), trade)
    bulk = lax.dynamic_index_in_dim(block, 1 - sibling, 0, keepdims=False)
    bulk, got = lax.optimization_barrier((bulk, got))
    arrived = lax.ppermute(bulk, ("cube", "row"), trade)

    maps = jnp.stack(
        [
            lax.dynamic_index_in_dim(child_map, sibling, 0, keepdims=False),
            lax.dynamic_index_in_dim(child_map, 1 - sibling, 0, keepdims=False),
        ]
    )
    within = position % 16
    pair_tiles = (
        grid * jnp.arange(tiles, dtype=jnp.int32)[None, :]
        + 16 * jnp.arange(2, dtype=jnp.int32)[:, None]
        + within
    )
    pair_maps = jnp.swapaxes(
        lax.dynamic_index_in_dim(
            maps.reshape(2, tiles, 2, 16, TB), within, 3, keepdims=False
        ),
        1,
        2,
    )
    pair_maps = pair_maps - TB * pair_tiles[None, :, :, None]
    row_maps = lax.dynamic_index_in_dim(pair_maps, sibling, 1, keepdims=False)
    col_maps = lax.dynamic_index_in_dim(
        maps.reshape(2, cols, columns, TB), col, 2, keepdims=False
    )
    col_tiles = columns * jnp.arange(cols, dtype=jnp.int32) + col
    col_maps = col_maps - TB * col_tiles[None, :, None]
    pair_diag = jnp.swapaxes(
        lax.dynamic_index_in_dim(
            parent_diag.reshape(tiles, 2, 16, TB), within, 2, keepdims=False
        ),
        0,
        1,
    )
    diag = lax.dynamic_index_in_dim(pair_diag, sibling, 0, keepdims=False)
    meets = pair_tiles[:, None, :] == col_tiles[None, :2, None]
    panel_diag = jnp.where(meets[..., None], pair_diag[:, None], 0.0)

    pieces = pl.pallas_call(
        place_kernel,
        out_shape=jax.ShapeDtypeStruct((2, 2, rows, TB), F32),
        in_specs=[VMEM] * 5,
        out_specs=VMEM,
    )(raw, got, pair_maps, col_maps[:, :2], panel_diag)

    even = lax.dynamic_index_in_dim(pieces, col % 2, 0, keepdims=False)
    odd = lax.dynamic_index_in_dim(pieces, 1 - col % 2, 0, keepdims=False)
    quarters = []
    for m in range(4):
        pairs = []
        for s in range(2):
            for z in range(4):
                for half in range(2):
                    for core in range(2):
                        for y in range(4):
                            kind = (m + y) % 4
                            far, h = kind // 2, kind % 2
                            source = ((s * 4 + z) * 4 + half * 2 + core) * 4 + y
                            target = ((s ^ far) * 4 + z) * 4 + (half ^ far) * 2 + h
                            pairs.append((source, target * 4 + half * 2 + core))
        quarters.append(lax.ppermute(even if m % 2 == 0 else odd, ("cube", "row", "col"), pairs))
    turned = jnp.stack(quarters)
    groups = [
        [(s * 4 + z) * 4 + half * 2 + core for z in range(4) for core in range(2)]
        for s in range(2)
        for half in range(2)
    ]
    others = lax.all_gather(turned, ("cube", "row"), axis=0, axis_index_groups=groups)

    own_rows = lax.all_gather(
        lax.dynamic_index_in_dim(pieces, sibling, 0, keepdims=False), "col", axis=0
    )
    pivot = pl.pallas_call(
        pivot_kernel,
        out_shape=jax.ShapeDtypeStruct((4, 8, 2, TB, TB), F32),
        in_specs=[VMEM],
        out_specs=VMEM,
        scratch_shapes=[
            pltpu.SemaphoreType.DMA((33,)),
            pltpu.SemaphoreType.DMA((4, 8)),
            pltpu.SemaphoreType.DMA,
        ],
        compiler_params=pltpu.CompilerParams(collective_id=0, has_side_effects=True),
    )(pieces[0, :, :TB])

    y, x = pl.pallas_call(
        factor_kernel,
        out_shape=[
            jax.ShapeDtypeStruct((2, rows, TB), F32),
            jax.ShapeDtypeStruct((rows, K), F32),
        ],
        in_specs=[SMEM, VMEM, VMEM],
        out_specs=[VMEM, VMEM],
        scratch_shapes=[
            pltpu.VMEM((K + rows, K), F32),
            pltpu.VMEM((K // TB, TB, TB), F32),
            pltpu.VMEM((TB, TB), F32),
        ],
        cost_estimate=pl.CostEstimate(flops=40_000_000_000, bytes_accessed=8 << 20, transcendentals=0),
    )(col.reshape(1), pivot, own_rows)

    row_inverse = inverse(row_maps).reshape(2, rows)
    solved = jnp.arange(cols) < 2
    col_inverse = jnp.where(solved[None, :, None], -1, inverse(col_maps))
    here = jnp.logical_and(row == col, jnp.logical_or(jnp.arange(tiles) > 0, cube >= 2))
    trailing_diag = jnp.where(here[:, None], diag, 0.0)
    crossed = (row // 2 != col // 2).astype(jnp.int32)
    at = jnp.stack([sibling, cube, 2 * crossed]).astype(jnp.int32)
    by_row = pl.BlockSpec((1, TB, cols, TB), lambda i, *_: (i, 0, 0, 0))
    all_maps = pl.BlockSpec((2, cols, TB), lambda i, *_: (0, 0, 0))
    kept = pl.pallas_call(
        keep_kernel,
        out_shape=jax.ShapeDtypeStruct((tiles, TB, cols, TB), F32),
        grid_spec=pltpu.PrefetchScalarGridSpec(
            num_scalar_prefetch=2,
            grid=(tiles,),
            in_specs=[
                pl.BlockSpec(
                    (1, 1, 1, TB, cols, TB), lambda i, at, _: (0, at[0], i, 0, 0, 0)
                ),
                all_maps,
            ],
            out_specs=by_row,
        ),
    )(at, row_inverse, child_update, col_inverse)
    by_col = pl.BlockSpec((tiles, TB, 8, TB), lambda i, *_: (0, 0, i, 0))
    part = pl.pallas_call(
        update_kernel,
        out_shape=jax.ShapeDtypeStruct((tiles, TB, cols, TB), F32),
        grid_spec=pltpu.PrefetchScalarGridSpec(
            num_scalar_prefetch=1,
            grid=(cols // 8,),
            in_specs=[
                by_col,
                pl.BlockSpec((8, 4, 2, TB, TB), lambda i, *_: (0, 0, 0, i, 0)),
                VMEM,
                VMEM,
                VMEM,
            ],
            out_specs=by_col,
            scratch_shapes=[
                pltpu.VMEM((8 * TB, K), jnp.bfloat16),
                pltpu.VMEM((8 * TB, K), jnp.bfloat16),
                pltpu.VMEM((rows, K), jnp.bfloat16),
                pltpu.VMEM((rows, K), jnp.bfloat16),
            ],
        ),
        cost_estimate=pl.CostEstimate(flops=26_000_000_000, bytes_accessed=32 << 20, transcendentals=0),
    )(at, kept, others, x, y, trailing_diag)
    return pl.pallas_call(
        finish_kernel,
        out_shape=jax.ShapeDtypeStruct((1, tiles, TB, cols, TB), F32),
        grid_spec=pltpu.PrefetchScalarGridSpec(
            num_scalar_prefetch=1,
            grid=(tiles,),
            in_specs=[by_row, all_maps, by_row],
            out_specs=pl.BlockSpec((1, 1, TB, cols, TB), lambda i, *_: (0, i, 0, 0, 0)),
        ),
    )(row_inverse, arrived, col_inverse, part)


def solution(mesh):
    return jax.shard_map(
        on_device,
        mesh=mesh,
        in_specs=(P(("cube", "row"), None, None, None, "col", None), P(), P()),
        out_specs=P(("cube", "row"), None, None, "col", None),
        check_vma=False,
    )
```

```python
import functools

import jax
import jax.numpy as jnp
from jax import lax
from jax.experimental import pallas as pl
from jax.experimental.pallas import tpu as pltpu
from jax.sharding import PartitionSpec as P


K = 1024
TB = 128
HI = lax.Precision.HIGHEST
F32 = jnp.float32
MESH = pl.DeviceIdType.MESH
VMEM = pl.BlockSpec(memory_space=pltpu.VMEM)
SMEM = pl.BlockSpec(memory_space=pltpu.SMEM)


def nt(a, b):
    return lax.dot_general(
        a, b, (((1,), (1,)), ((), ())), precision=HI, preferred_element_type=F32
    )


def nn(a, b):
    return lax.dot_general(
        a, b, (((1,), (0,)), ((), ())), precision=HI, preferred_element_type=F32
    )


def place_kernel(raw_ref, got_ref, rmap_ref, cmap_ref, diag_ref, out_ref):
    sub = lax.broadcasted_iota(jnp.int32, (TB, TB), 0)
    lane = lax.broadcasted_iota(jnp.int32, (TB, TB), 1)
    tiles = rmap_ref.shape[2]
    for v in range(2):
        for half in range(2):
            cols = [
                nt(ref[half, v], (sub == cmap_ref[t, v : v + 1, :]).astype(F32))
                for t, ref in enumerate((raw_ref, got_ref))
            ]
            for j in range(tiles):
                rows = slice(j * TB, (j + 1) * TB)
                total = jnp.where(sub == lane, diag_ref[half, v, j : j + 1, :], 0.0)
                for t in range(2):
                    hot = (sub == rmap_ref[t, half, j : j + 1, :]).astype(F32)
                    total += nn(hot, cols[t][rows, :])
                out_ref[half, v, rows, :] = total


def pivot_kernel(piece_ref, out_ref, send, recv, local):
    cube, row, col = lax.axis_index("cube"), lax.axis_index("row"), lax.axis_index("col")
    z = lax.rem(cube, 4)
    core = lax.rem(row, 2)
    at = lambda cu, ro, co: {"cube": cu, "row": ro, "col": co}
    mates = [at((cube - z) + lax.rem(z + d, 4), row, col) for d in (1, 2, 3)]
    across = at(lax.rem(cube + 4, 8), lax.rem(row + 2, 4), col)
    up, down = lax.rem(col + 1, 4), lax.rem(col + 3, 4)
    sides = [at(cube, row, up), at(cube, row, down)]
    other = at(cube, row + 1 - 2 * core, col)
    barrier = pltpu.get_barrier_semaphore()
    for peer in mates + [across] + sides + [other]:
        pl.semaphore_signal(barrier, inc=1, device_id=peer, device_id_type=MESH)
    pl.semaphore_wait(barrier, 7)

    def copy(c, p, slot, peer, width):
        part = out_ref.at[c, p, pl.ds(0, width)]
        return pltpu.make_async_remote_copy(
            src_ref=part,
            dst_ref=part,
            send_sem=send.at[slot],
            recv_sem=recv.at[c, p],
            device_id=peer,
            device_id_type=MESH,
        )

    for zz in range(2):
        mine = zz * 4 + row

        @pl.when(z == zz)
        def _():
            part = pl.ds(0, zz + 1)
            own = pltpu.make_async_copy(piece_ref.at[part], out_ref.at[col, mine, part], local)
            own.start()
            own.wait()
            for i, peer in enumerate(mates):
                copy(col, mine, i, peer, zz + 1).start()

    for zz in range(2):
        p = zz * 4 + row
        n = zz

        @pl.when(z != zz)
        def _():
            copy(col, p, 0, other, zz + 1).wait_recv()

        copy(col, p, 3 + zz, across, zz + 1).start()
        copy(col, p, 5 + n, sides[0], zz + 1).start()
        copy(col, p, 7 + n, sides[1], zz + 1).start()
        copy(col, p, 9 + n, other, zz + 1).start()
    opposite = lax.rem(row + 2, 4)
    for zz in range(2):
        p = zz * 4 + opposite
        n = zz
        copy(col, p, 0, other, zz + 1).wait_recv()
        copy(col, p, 11 + n, sides[0], zz + 1).start()
        copy(col, p, 13 + n, sides[1], zz + 1).start()
        copy(col, p, 15 + n, other, zz + 1).start()
    for i, who in enumerate((row, opposite)):
        for zz in range(2):
            p = zz * 4 + who
            n = i * 2 + zz
            copy(down, p, 0, other, zz + 1).wait_recv()
            copy(down, p, 17 + n, other, zz + 1).start()

            @pl.when(core == 0)
            def _():
                copy(down, p, 21 + n, sides[0], zz + 1).start()

            copy(up, p, 0, other, zz + 1).wait_recv()
            copy(up, p, 25 + n, other, zz + 1).start()

            @pl.when(core == 1)
            def _():
                copy(up, p, 21 + n, sides[1], zz + 1).start()

    far = lax.rem(col + 2, 4)
    for i, who in enumerate((row, opposite)):
        for zz in range(2):
            p = zz * 4 + who
            copy(far, p, 0, other, zz + 1).wait_recv()
            copy(far, p, 29 + i * 2 + zz, other, zz + 1).start()
    for c in range(4):
        for zz in range(2):
            for hh in range(2):
                copy(c, zz * 4 + hh * 2 + 1 - core, 0, other, zz + 1).wait_recv()

    for zz in range(2):

        @pl.when(z == zz)
        def _():
            for i in range(3):
                copy(col, row, i, other, zz + 1).wait_send()

        for i in (3, 5, 7, 9, 11, 13, 15, 17, 19, 21, 23, 25, 27, 29, 31):
            copy(col, row, i + zz, other, zz + 1).wait_send()


def leaf(d_ref, li_ref):
    a_rows = [d_ref[8 * g : 8 * g + 8, :] for g in range(16)]
    lane = lax.broadcasted_iota(jnp.int32, (8, TB), 1)
    sub = lax.broadcasted_iota(jnp.int32, (8, TB), 0)
    b_rows = [(lane == sub + 8 * g).astype(F32) for g in range(16)]
    wide = lambda x: jnp.broadcast_to(x, (8, TB))
    for g0 in range(16):
        j = 8 * g0
        c = [wide(a_rows[g0][:, j + q : j + q + 1]) for q in range(8)]
        e = [[wide(c[q][i : i + 1, :]) if i >= q else None for q in range(8)] for i in range(8)]
        a = [wide(a_rows[g0][q : q + 1, :]) for q in range(8)]
        b = [wide(b_rows[g0][q : q + 1, :]) for q in range(8)]
        more = g0 + 1 < 16
        if more:
            m = [wide(a_rows[g0 + 1][:, j + q : j + q + 1]) for q in range(8)]
        s, t = [None] * 8, [None] * 8
        low = [[None] * 8 for _ in range(8)]
        for q in range(8):
            inv = 1.0 / e[q][q]
            s[q], t[q] = a[q] * inv, b[q] * inv
            for i in range(q + 1, 8):
                low[i][q] = e[i][q] * inv
            for i in range(q + 1, 8):
                for p in range(q + 1, i + 1):
                    e[i][p] = e[i][p] - low[i][q] * e[p][q]
            for i in range(q + 1, 8):
                a[i] = a[i] - low[i][q] * a[q]
                b[i] = b[i] - low[i][q] * b[q]
                if more:
                    m[i] = m[i] - low[i][q] * m[q]
            if more:
                a_rows[g0 + 1] = a_rows[g0 + 1] - m[q] * s[q]
                b_rows[g0 + 1] = b_rows[g0 + 1] - m[q] * t[q]
            li_ref[j + q : j + q + 1, :] = (b[q] * lax.rsqrt(e[q][q]))[0:1, :]
        if g0 + 2 < 16:
            for q in range(7, -1, -1):
                for i in range(q + 1, 8):
                    s[q] = s[q] - low[i][q] * s[i]
                    t[q] = t[q] - low[i][q] * t[i]
            for g in range(g0 + 2, 16):
                m = [wide(a_rows[g][:, j + q : j + q + 1]) for q in range(8)]
                da, db = m[0] * s[0], m[0] * t[0]
                for q in range(1, 8):
                    da, db = da + m[q] * s[q], db + m[q] * t[q]
                a_rows[g] = a_rows[g] - da
                b_rows[g] = b_rows[g] - db


def factor_kernel(col_ref, s_ref, a_ref, y_ref, x_ref, m_ref, li_ref, d_ref):
    blocks = K // TB
    for c in range(4):
        for v in range(2):
            u = 4 * v + c
            for p in range(u, blocks):
                m_ref[p * TB : (p + 1) * TB, u * TB : (u + 1) * TB] = s_ref[c, p, v]
            m_ref[K:, u * TB : (u + 1) * TB] = a_ref[c, v]

    pair_width = 2 * TB

    def step(k, _):
        here = pl.ds(pl.multiple_of(k * TB, TB), TB)
        d_ref[...] = m_ref[here, here]
        leaf(d_ref, li_ref.at[k])
        m_ref[:, here] = nt(m_ref[:, here], li_ref[k])

        @pl.when(lax.rem(k, 2) == 0)
        def _():
            after = pl.ds(pl.multiple_of((k + 1) * TB, TB), TB)
            m_ref[:, after] = m_ref[:, after] - nt(m_ref[:, here], m_ref[after, here])

        @pl.when(lax.rem(k, 2) == 1)
        def _():
            pair = pl.ds(pl.multiple_of((k - 1) * TB, TB), pair_width)

            def trail(i, _):
                part = pl.ds(pl.multiple_of(i * pair_width, pair_width), pair_width)
                m_ref[:, part] = m_ref[:, part] - nt(m_ref[:, pair], m_ref[part, pair])
                return 0

            lax.fori_loop((k + 1) // 2, blocks // 2, trail, 0)

        return 0

    lax.fori_loop(0, blocks, step, 0)
    col = col_ref[0]
    for v in range(2):
        y_ref[v] = m_ref[K:, pl.ds(pl.multiple_of((4 * v + col) * TB, TB), TB)]

    def back(i, _):
        n = blocks // 2 - 1 - i
        first = pl.ds(pl.multiple_of(n * pair_width, TB), TB)
        last = pl.ds(pl.multiple_of(n * pair_width + TB, TB), TB)
        pair = pl.ds(pl.multiple_of(n * pair_width, pair_width), pair_width)
        x_ref[:, last] = nn(m_ref[K:, last], li_ref[2 * n + 1])
        rest = m_ref[K:, first] - nn(x_ref[:, last], m_ref[last, first])
        x_ref[:, first] = nn(rest, li_ref[2 * n])

        def lead(j, _):
            part = pl.ds(pl.multiple_of(j * pair_width, pair_width), pair_width)
            m_ref[K:, part] = m_ref[K:, part] - nn(x_ref[:, pair], m_ref[pair, part])
            return 0

        lax.fori_loop(0, n, lead, 0)
        return 0

    lax.fori_loop(0, blocks // 2, back, 0)


def split(x):
    high = x.astype(jnp.bfloat16)
    return high, (x - high.astype(F32)).astype(jnp.bfloat16)


def place_rows(tile, t, rinv_ref, cinv_ref, from_ref, less, out_ref):
    groups = range(0, from_ref.shape[-2], 8)
    index = [jnp.maximum(cinv_ref[t, g : g + 8], 0) for g in groups]
    live = [(cinv_ref[t, g : g + 8] >= 0).astype(F32) for g in groups]
    base = tile * TB

    def body(o, _):
        s = rinv_ref[t, base + o]
        weight = jnp.where(s >= 0, 1.0, 0.0)
        s = jnp.maximum(s, 0)
        for g, at, keep in zip(groups, index, live):
            x = jnp.take_along_axis(from_ref[s, g : g + 8], at, axis=1) * (keep * weight)
            out_ref[o, g : g + 8] = x if less is None else x + less(o, g)
        return 0

    lax.fori_loop(0, TB, body, 0, unroll=16)


def keep_kernel(at_ref, rinv_ref, kept_ref, cinv_ref, out_ref):
    place_rows(pl.program_id(0), 0, rinv_ref, cinv_ref, kept_ref.at[0, 0, 0], None, out_ref.at[0, 0])


def finish_kernel(start, rinv_ref, got_ref, cinv_ref, kept_ref, r_ref, out_ref):
    def less(o, g):
        return kept_ref[0, 0, o, g : g + 8] - r_ref.at[0][pl.ds(g * TB + o, 8, stride=TB), :]

    tile = pl.program_id(0) + start
    place_rows(tile, 1, rinv_ref, cinv_ref, got_ref.at[0], less, out_ref.at[0, 0])


def update_kernel(
    at_ref, g_ref, x_ref, y_ref, diag_ref, out_ref, wh_ref, wl_ref, xh_ref, xl_ref
):
    step = pl.program_id(0)
    tiles = out_ref.shape[0]

    @pl.when(step == 0)
    def _():
        xh_ref[...], xl_ref[...] = split(x_ref[...])

    for n in range(8):
        part = slice(n * TB, (n + 1) * TB)
        for m in range(4):
            q = lax.rem(at_ref[2] + n // 4 + 4 - m, 4)
            for v in range(2):
                high, low = split(g_ref[(n % 4) * 2 + n // 4, m, v])
                there = pl.ds(pl.multiple_of((4 * v + q) * TB, TB), TB)
                wh_ref[part, there] = high
                wl_ref[part, there] = low
    dims = (((1,), (1,)), ((), ()))
    dot = lambda a, b: lax.dot_general(a, b, dims, preferred_element_type=F32)
    for n in range(0, 8, 2):
        part = slice(n * TB, (n + 2) * TB)
        wh, wl = wh_ref[part, :], wl_ref[part, :]
        r = (dot(xl_ref[...], wh) + dot(xh_ref[...], wl)) + dot(xh_ref[...], wh)
        for i in range(2):
            for j in range(tiles):
                out_ref[j, (n + i) * TB : (n + i + 1) * TB, :] = r[
                    j * TB : (j + 1) * TB, i * TB : (i + 1) * TB
                ]
    sub = lax.broadcasted_iota(jnp.int32, (TB, TB), 0)
    lane = lax.broadcasted_iota(jnp.int32, (TB, TB), 1)
    here = pl.ds(pl.multiple_of(at_ref[1] * TB, TB), TB)
    out_ref[step, here, :] = out_ref[step, here, :] - jnp.where(
        sub == lane, diag_ref[pl.ds(step, 1), :], 0.0
    )

    @pl.when(step == 0)
    def _():
        for v in range(2):
            for j in range(tiles):
                out_ref[j, v * TB : (v + 1) * TB, :] = -y_ref[v, j * TB : (j + 1) * TB, :]


def inverse(relative):
    offsets = jnp.arange(TB, dtype=jnp.int32)
    hit = relative[..., None, :] == offsets[:, None]
    return jnp.max(jnp.where(hit, offsets, -1), axis=-1)


def on_device(child_update, child_map, parent_diag):
    cube, row, col = lax.axis_index("cube"), lax.axis_index("row"), lax.axis_index("col")
    grid, columns = 32, 4
    position = cube * 4 + row
    sibling = position // (grid // 2)
    block = child_update[0]
    tiles, cols = block.shape[1], block.shape[3]
    rows = tiles * TB
    trade = [(i, i ^ 16) for i in range(grid)]

    raw = jnp.transpose(block[:, :, :, :2, :], (0, 3, 1, 2, 4)).reshape(2, 2, rows, TB)
    got = lax.ppermute(raw, ("cube", "row"), trade)
    early = tiles - 1
    bulk = lax.dynamic_index_in_dim(block, 1 - sibling, 0, keepdims=False)
    first, second, got = lax.optimization_barrier((bulk[:early], bulk[early:], got))
    arrived = []
    for part in (first, second):
        arrived.append(lax.ppermute(part, ("cube", "row"), trade))

    maps = jnp.stack(
        [
            lax.dynamic_index_in_dim(child_map, sibling, 0, keepdims=False),
            lax.dynamic_index_in_dim(child_map, 1 - sibling, 0, keepdims=False),
        ]
    )
    within = position % 16
    pair_tiles = (
        grid * jnp.arange(tiles, dtype=jnp.int32)[None, :]
        + 16 * jnp.arange(2, dtype=jnp.int32)[:, None]
        + within
    )
    pair_maps = jnp.swapaxes(
        lax.dynamic_index_in_dim(
            maps.reshape(2, tiles, 2, 16, TB), within, 3, keepdims=False
        ),
        1,
        2,
    )
    pair_maps = pair_maps - TB * pair_tiles[None, :, :, None]
    row_maps = lax.dynamic_index_in_dim(pair_maps, sibling, 1, keepdims=False)
    col_maps = lax.dynamic_index_in_dim(
        maps.reshape(2, cols, columns, TB), col, 2, keepdims=False
    )
    col_tiles = columns * jnp.arange(cols, dtype=jnp.int32) + col
    col_maps = col_maps - TB * col_tiles[None, :, None]
    pair_diag = jnp.swapaxes(
        lax.dynamic_index_in_dim(
            parent_diag.reshape(tiles, 2, 16, TB), within, 2, keepdims=False
        ),
        0,
        1,
    )
    diag = lax.dynamic_index_in_dim(pair_diag, sibling, 0, keepdims=False)
    meets = pair_tiles[:, None, :] == col_tiles[None, :2, None]
    panel_diag = jnp.where(meets[..., None], pair_diag[:, None], 0.0)

    pieces = pl.pallas_call(
        place_kernel,
        out_shape=jax.ShapeDtypeStruct((2, 2, rows, TB), F32),
        in_specs=[VMEM] * 5,
        out_specs=VMEM,
    )(raw, got, pair_maps, col_maps[:, :2], panel_diag)

    even = lax.dynamic_index_in_dim(pieces, col % 2, 0, keepdims=False)
    odd = lax.dynamic_index_in_dim(pieces, 1 - col % 2, 0, keepdims=False)
    quarters = []
    for m in range(4):
        pairs = []
        for s in range(2):
            for z in range(4):
                for half in range(2):
                    for core in range(2):
                        for y in range(4):
                            kind = (m + y) % 4
                            far, h = kind // 2, kind % 2
                            source = ((s * 4 + z) * 4 + half * 2 + core) * 4 + y
                            target = ((s ^ far) * 4 + z) * 4 + (half ^ far) * 2 + h
                            pairs.append((source, target * 4 + half * 2 + core))
        quarters.append(lax.ppermute(even if m % 2 == 0 else odd, ("cube", "row", "col"), pairs))
    turned = jnp.stack(quarters)
    groups = [
        [(s * 4 + z) * 4 + half * 2 + core for z in range(4) for core in range(2)]
        for s in range(2)
        for half in range(2)
    ]
    others = lax.all_gather(turned, ("cube", "row"), axis=0, axis_index_groups=groups)

    own_rows = lax.all_gather(
        lax.dynamic_index_in_dim(pieces, sibling, 0, keepdims=False), "col", axis=0
    )
    pivot = pl.pallas_call(
        pivot_kernel,
        out_shape=jax.ShapeDtypeStruct((4, 8, 2, TB, TB), F32),
        in_specs=[VMEM],
        out_specs=VMEM,
        scratch_shapes=[
            pltpu.SemaphoreType.DMA((33,)),
            pltpu.SemaphoreType.DMA((4, 8)),
            pltpu.SemaphoreType.DMA,
        ],
        compiler_params=pltpu.CompilerParams(collective_id=0, has_side_effects=True),
    )(pieces[0, :, :TB])

    y, x = pl.pallas_call(
        factor_kernel,
        out_shape=[
            jax.ShapeDtypeStruct((2, rows, TB), F32),
            jax.ShapeDtypeStruct((rows, K), F32),
        ],
        in_specs=[SMEM, VMEM, VMEM],
        out_specs=[VMEM, VMEM],
        scratch_shapes=[
            pltpu.VMEM((K + rows, K), F32),
            pltpu.VMEM((K // TB, TB, TB), F32),
            pltpu.VMEM((TB, TB), F32),
        ],
        cost_estimate=pl.CostEstimate(flops=40_000_000_000, bytes_accessed=8 << 20, transcendentals=0),
    )(col.reshape(1), pivot, own_rows)

    row_inverse = inverse(row_maps).reshape(2, rows)
    solved = jnp.arange(cols) < 2
    col_inverse = jnp.where(solved[None, :, None], -1, inverse(col_maps))
    here = jnp.logical_and(row == col, jnp.logical_or(jnp.arange(tiles) > 0, cube >= 2))
    trailing_diag = jnp.where(here[:, None], diag, 0.0)
    crossed = (row // 2 != col // 2).astype(jnp.int32)
    at = jnp.stack([sibling, cube, 2 * crossed]).astype(jnp.int32)
    whole = jax.ShapeDtypeStruct((1, tiles, TB, cols, TB), F32)
    all_maps = pl.BlockSpec((2, cols, TB), lambda i, *_: (0, 0, 0))
    result = pl.pallas_call(
        keep_kernel,
        out_shape=whole,
        grid_spec=pltpu.PrefetchScalarGridSpec(
            num_scalar_prefetch=2,
            grid=(tiles,),
            in_specs=[
                pl.BlockSpec(
                    (1, 1, 1, TB, cols, TB), lambda i, at, _: (0, at[0], i, 0, 0, 0)
                ),
                all_maps,
            ],
            out_specs=pl.BlockSpec((1, 1, TB, cols, TB), lambda i, *_: (0, i, 0, 0, 0)),
        ),
    )(at, row_inverse, child_update, col_inverse)
    update = pl.pallas_call(
        update_kernel,
        out_shape=jax.ShapeDtypeStruct((tiles, cols * TB, TB), F32),
        grid_spec=pltpu.PrefetchScalarGridSpec(
            num_scalar_prefetch=1,
            grid=(cols // 8,),
            in_specs=[
                pl.BlockSpec((8, 4, 2, TB, TB), lambda i, *_: (0, 0, 0, i, 0)),
                VMEM,
                VMEM,
                VMEM,
            ],
            out_specs=pl.BlockSpec((tiles, 8 * TB, TB), lambda i, *_: (0, i, 0)),
            scratch_shapes=[
                pltpu.VMEM((8 * TB, K), jnp.bfloat16),
                pltpu.VMEM((8 * TB, K), jnp.bfloat16),
                pltpu.VMEM((rows, K), jnp.bfloat16),
                pltpu.VMEM((rows, K), jnp.bfloat16),
            ],
        ),
        cost_estimate=pl.CostEstimate(flops=26_000_000_000, bytes_accessed=32 << 20, transcendentals=0),
    )(at, others, x, y, trailing_diag)
    for start, part in zip((0, early), arrived):
        block_at = lambda i, *_, start=start: (0, i + start, 0, 0, 0)
        result = pl.pallas_call(
            functools.partial(finish_kernel, start),
            out_shape=whole,
            grid_spec=pltpu.PrefetchScalarGridSpec(
                num_scalar_prefetch=1,
                grid=(part.shape[0],),
                in_specs=[
                    pl.BlockSpec((1, TB, cols, TB), lambda i, *_: (i, 0, 0, 0)),
                    all_maps,
                    pl.BlockSpec((1, 1, TB, cols, TB), block_at),
                    pl.BlockSpec((1, cols * TB, TB), lambda i, *_, start=start: (i + start, 0, 0)),
                ],
                out_specs=pl.BlockSpec((1, 1, TB, cols, TB), block_at),
            ),
            input_output_aliases={3: 0},
        )(row_inverse, part, col_inverse, result, update)
    return result


def solution(mesh):
    return jax.shard_map(
        on_device,
        mesh=mesh,
        in_specs=(P(("cube", "row"), None, None, None, "col", None), P(), P()),
        out_specs=P(("cube", "row"), None, None, "col", None),
        check_vma=False,
    )
```

```python
import functools

import jax
import jax.numpy as jnp
from jax import lax
from jax.experimental import pallas as pl
from jax.experimental.pallas import tpu as pltpu
from jax.sharding import PartitionSpec as P


K = 1024
TB = 128
HI = lax.Precision.HIGHEST
F32 = jnp.float32
MESH = pl.DeviceIdType.MESH
VMEM = pl.BlockSpec(memory_space=pltpu.VMEM)
SMEM = pl.BlockSpec(memory_space=pltpu.SMEM)


def nt(a, b):
    return lax.dot_general(
        a, b, (((1,), (1,)), ((), ())), precision=HI, preferred_element_type=F32
    )


def nn(a, b):
    return lax.dot_general(
        a, b, (((1,), (0,)), ((), ())), precision=HI, preferred_element_type=F32
    )


def place_kernel(
    pick_ref, raw_ref, got_ref, rmap_ref, cmap_ref, diag_ref, own_ref, even_ref, odd_ref, piece_ref
):
    sub = lax.broadcasted_iota(jnp.int32, (TB, TB), 0)
    lane = lax.broadcasted_iota(jnp.int32, (TB, TB), 1)
    tiles = rmap_ref.shape[2]
    for v in range(2):
        for half in range(2):
            cols = [
                nt(ref[half, v], (sub == cmap_ref[t, v : v + 1, :]).astype(F32))
                for t, ref in enumerate((raw_ref, got_ref))
            ]
            for j in range(tiles):
                rows = slice(j * TB, (j + 1) * TB)
                total = jnp.where(sub == lane, diag_ref[half, v, j : j + 1, :], 0.0)
                for t in range(2):
                    hot = (sub == rmap_ref[t, half, j : j + 1, :]).astype(F32)
                    total += nn(hot, cols[t][rows, :])
                if half == 0 and j == 0:
                    piece_ref[v] = total
                for out_ref, wanted in ((own_ref, pick_ref[0]), (even_ref, pick_ref[1])):

                    @pl.when(wanted == half)
                    def _():
                        out_ref[v, rows, :] = total

                @pl.when(pick_ref[1] != half)
                def _():
                    odd_ref[v, rows, :] = total


def pivot_kernel(piece_ref, out_ref, send, recv, local):
    cube, row, col = lax.axis_index("cube"), lax.axis_index("row"), lax.axis_index("col")
    z = lax.rem(cube, 4)
    core = lax.rem(row, 2)
    at = lambda cu, ro, co: {"cube": cu, "row": ro, "col": co}
    mates = [at((cube - z) + lax.rem(z + d, 4), row, col) for d in (1, 2, 3)]
    across = at(lax.rem(cube + 4, 8), lax.rem(row + 2, 4), col)
    up, down = lax.rem(col + 1, 4), lax.rem(col + 3, 4)
    sides = [at(cube, row, up), at(cube, row, down)]
    other = at(cube, row + 1 - 2 * core, col)
    barrier = pltpu.get_barrier_semaphore()
    for peer in mates + [across] + sides + [other]:
        pl.semaphore_signal(barrier, inc=1, device_id=peer, device_id_type=MESH)
    pl.semaphore_wait(barrier, 7)

    def copy(c, p, slot, peer, width):
        part = out_ref.at[c, p, pl.ds(0, width)]
        return pltpu.make_async_remote_copy(
            src_ref=part,
            dst_ref=part,
            send_sem=send.at[slot],
            recv_sem=recv.at[c, p],
            device_id=peer,
            device_id_type=MESH,
        )

    for zz in range(2):
        mine = zz * 4 + row

        @pl.when(z == zz)
        def _():
            part = pl.ds(0, zz + 1)
            own = pltpu.make_async_copy(piece_ref.at[part], out_ref.at[col, mine, part], local)
            own.start()
            own.wait()
            for i, peer in enumerate(mates):
                copy(col, mine, i, peer, zz + 1).start()

    for zz in range(2):
        p = zz * 4 + row
        n = zz

        @pl.when(z != zz)
        def _():
            copy(col, p, 0, other, zz + 1).wait_recv()

        copy(col, p, 3 + zz, across, zz + 1).start()
        copy(col, p, 5 + n, sides[0], zz + 1).start()
        copy(col, p, 7 + n, sides[1], zz + 1).start()
        copy(col, p, 9 + n, other, zz + 1).start()
    opposite = lax.rem(row + 2, 4)
    for zz in range(2):
        p = zz * 4 + opposite
        n = zz
        copy(col, p, 0, other, zz + 1).wait_recv()
        copy(col, p, 11 + n, sides[0], zz + 1).start()
        copy(col, p, 13 + n, sides[1], zz + 1).start()
        copy(col, p, 15 + n, other, zz + 1).start()
    for i, who in enumerate((row, opposite)):
        for zz in range(2):
            p = zz * 4 + who
            n = i * 2 + zz
            copy(down, p, 0, other, zz + 1).wait_recv()
            copy(down, p, 17 + n, other, zz + 1).start()

            @pl.when(core == 0)
            def _():
                copy(down, p, 21 + n, sides[0], zz + 1).start()

            copy(up, p, 0, other, zz + 1).wait_recv()
            copy(up, p, 25 + n, other, zz + 1).start()

            @pl.when(core == 1)
            def _():
                copy(up, p, 21 + n, sides[1], zz + 1).start()

    far = lax.rem(col + 2, 4)
    for i, who in enumerate((row, opposite)):
        for zz in range(2):
            p = zz * 4 + who
            copy(far, p, 0, other, zz + 1).wait_recv()
            copy(far, p, 29 + i * 2 + zz, other, zz + 1).start()
    for c in range(4):
        for zz in range(2):
            for hh in range(2):
                copy(c, zz * 4 + hh * 2 + 1 - core, 0, other, zz + 1).wait_recv()

    for zz in range(2):

        @pl.when(z == zz)
        def _():
            for i in range(3):
                copy(col, row, i, other, zz + 1).wait_send()

        for i in (3, 5, 7, 9, 11, 13, 15, 17, 19, 21, 23, 25, 27, 29, 31):
            copy(col, row, i + zz, other, zz + 1).wait_send()


def leaf(d_ref, li_ref):
    a_rows = [d_ref[8 * g : 8 * g + 8, :] for g in range(16)]
    lane = lax.broadcasted_iota(jnp.int32, (8, TB), 1)
    sub = lax.broadcasted_iota(jnp.int32, (8, TB), 0)
    b_rows = [(lane == sub + 8 * g).astype(F32) for g in range(16)]
    wide = lambda x: jnp.broadcast_to(x, (8, TB))
    for g0 in range(16):
        j = 8 * g0
        c = [wide(a_rows[g0][:, j + q : j + q + 1]) for q in range(8)]
        e = [[wide(c[q][i : i + 1, :]) if i >= q else None for q in range(8)] for i in range(8)]
        a = [wide(a_rows[g0][q : q + 1, :]) for q in range(8)]
        b = [wide(b_rows[g0][q : q + 1, :]) for q in range(8)]
        more = g0 + 1 < 16
        if more:
            m = [wide(a_rows[g0 + 1][:, j + q : j + q + 1]) for q in range(8)]
        s, t = [None] * 8, [None] * 8
        low = [[None] * 8 for _ in range(8)]
        for q in range(8):
            inv = 1.0 / e[q][q]
            s[q], t[q] = a[q] * inv, b[q] * inv
            for i in range(q + 1, 8):
                low[i][q] = e[i][q] * inv
            for i in range(q + 1, 8):
                for p in range(q + 1, i + 1):
                    e[i][p] = e[i][p] - low[i][q] * e[p][q]
            for i in range(q + 1, 8):
                a[i] = a[i] - low[i][q] * a[q]
                b[i] = b[i] - low[i][q] * b[q]
                if more:
                    m[i] = m[i] - low[i][q] * m[q]
            if more:
                a_rows[g0 + 1] = a_rows[g0 + 1] - m[q] * s[q]
                b_rows[g0 + 1] = b_rows[g0 + 1] - m[q] * t[q]
            li_ref[j + q : j + q + 1, :] = (b[q] * lax.rsqrt(e[q][q]))[0:1, :]
        if g0 + 2 < 16:
            for q in range(7, -1, -1):
                for i in range(q + 1, 8):
                    s[q] = s[q] - low[i][q] * s[i]
                    t[q] = t[q] - low[i][q] * t[i]
            for g in range(g0 + 2, 16):
                m = [wide(a_rows[g][:, j + q : j + q + 1]) for q in range(8)]
                da, db = m[0] * s[0], m[0] * t[0]
                for q in range(1, 8):
                    da, db = da + m[q] * s[q], db + m[q] * t[q]
                a_rows[g] = a_rows[g] - da
                b_rows[g] = b_rows[g] - db


def factor_kernel(s_ref, m_ref, li_ref, d_ref):
    blocks, pair_width = K // TB, 2 * TB
    for c in range(4):
        for v in range(2):
            u = 4 * v + c
            for p in range(u, blocks):
                m_ref[p * TB : (p + 1) * TB, u * TB : (u + 1) * TB] = s_ref[c, p, v]

    def step(k, _):
        here = pl.ds(pl.multiple_of(k * TB, TB), TB)
        d_ref[...] = m_ref[here, here]
        leaf(d_ref, li_ref.at[k])
        m_ref[:, here] = nt(m_ref[:, here], li_ref[k])

        @pl.when(lax.rem(k, 2) == 0)
        def _():
            after = pl.ds(pl.multiple_of((k + 1) * TB, TB), TB)
            m_ref[:, after] = m_ref[:, after] - nt(m_ref[:, here], m_ref[after, here])

        @pl.when(lax.rem(k, 2) == 1)
        def _():
            pair = pl.ds(pl.multiple_of((k - 1) * TB, TB), pair_width)

            def trail(i, _):
                part = pl.ds(pl.multiple_of(i * pair_width, pair_width), pair_width)
                m_ref[:, part] = m_ref[:, part] - nt(m_ref[:, pair], m_ref[part, pair])
                return 0

            lax.fori_loop((k + 1) // 2, blocks // 2, trail, 0)

        return 0

    lax.fori_loop(0, blocks, step, 0)


def solve_kernel(col_ref, l_ref, li_ref, own_ref, low_ref, high_ref, far_ref, y_ref, x_ref, m_ref):
    blocks, pair_width = K // TB, 2 * TB
    col = col_ref[0]
    for part, ref in enumerate((own_ref, high_ref, far_ref, low_ref)):
        for v in range(2):
            u = 4 * v + lax.rem(col + part, 4)
            m_ref[:, pl.ds(pl.multiple_of(u * TB, TB), TB)] = ref[v]

    def places(n):
        at = n * pair_width
        return (
            pl.ds(pl.multiple_of(at, TB), TB),
            pl.ds(pl.multiple_of(at + TB, TB), TB),
            pl.ds(pl.multiple_of(at, pair_width), pair_width),
        )

    def forth(n, _):
        first, last, pair = places(n)
        m_ref[:, first] = nt(m_ref[:, first], li_ref[2 * n])
        rest = m_ref[:, last] - nt(m_ref[:, first], l_ref[last, first])
        m_ref[:, last] = nt(rest, li_ref[2 * n + 1])

        def trail(i, _):
            part = places(i)[2]
            m_ref[:, part] = m_ref[:, part] - nt(m_ref[:, pair], l_ref[part, pair])
            return 0

        lax.fori_loop(n + 1, blocks // 2, trail, 0)
        return 0

    lax.fori_loop(0, blocks // 2, forth, 0)
    for v in range(2):
        y_ref[v] = m_ref[:, pl.ds(pl.multiple_of((4 * v + col) * TB, TB), TB)]

    def back(i, _):
        n = blocks // 2 - 1 - i
        first, last, pair = places(n)
        x_ref[:, last] = nn(m_ref[:, last], li_ref[2 * n + 1])
        rest = m_ref[:, first] - nn(x_ref[:, last], l_ref[last, first])
        x_ref[:, first] = nn(rest, li_ref[2 * n])

        def lead(j, _):
            part = places(j)[2]
            m_ref[:, part] = m_ref[:, part] - nn(x_ref[:, pair], l_ref[pair, part])
            return 0

        lax.fori_loop(0, n, lead, 0)
        return 0

    lax.fori_loop(0, blocks // 2, back, 0)


def split(x):
    high = x.astype(jnp.bfloat16)
    return high, (x - high.astype(F32)).astype(jnp.bfloat16)


def place_rows(tile, t, rinv_ref, cinv_ref, from_ref, less, out_ref):
    groups = range(0, from_ref.shape[-2], 8)
    index = [jnp.maximum(cinv_ref[t, g : g + 8], 0) for g in groups]
    live = [(cinv_ref[t, g : g + 8] >= 0).astype(F32) for g in groups]
    base = tile * TB

    def body(o, _):
        s = rinv_ref[t, base + o]
        weight = jnp.where(s >= 0, 1.0, 0.0)
        s = jnp.maximum(s, 0)
        for g, at, keep in zip(groups, index, live):
            x = jnp.take_along_axis(from_ref[s, g : g + 8], at, axis=1) * (keep * weight)
            out_ref[o, g : g + 8] = x if less is None else x + less(o, g)
        return 0

    lax.fori_loop(0, TB, body, 0, unroll=16)


def keep_kernel(at_ref, rinv_ref, kept_ref, cinv_ref, out_ref):
    place_rows(pl.program_id(0), 0, rinv_ref, cinv_ref, kept_ref.at[0, 0, 0], None, out_ref.at[0, 0])


def finish_kernel(start, rinv_ref, got_ref, cinv_ref, kept_ref, ra_ref, rb_ref, out_ref):
    cut = ra_ref.shape[1] // TB

    def less(o, g):
        ref, at = (ra_ref, g) if g < cut else (rb_ref, g - cut)
        return kept_ref[0, 0, o, g : g + 8] - ref.at[0][pl.ds(at * TB + o, 8, stride=TB), :]

    tile = pl.program_id(0) + start
    place_rows(tile, 1, rinv_ref, cinv_ref, got_ref.at[0], less, out_ref.at[0, 0])


def update_kernel(
    start, at_ref, g_ref, x_ref, y_ref, diag_ref, out_ref, wh_ref, wl_ref, xh_ref, xl_ref
):
    step = pl.program_id(0) + start
    tiles = out_ref.shape[0]

    @pl.when(step == start)
    def _():
        xh_ref[...], xl_ref[...] = split(x_ref[...])

    for n in range(8):
        part = slice(n * TB, (n + 1) * TB)
        for m in range(4):
            q = lax.rem(at_ref[2] + n // 4 + 4 - m, 4)
            for v in range(2):
                high, low = split(g_ref[(n % 4) * 2 + n // 4, m, v])
                there = pl.ds(pl.multiple_of((4 * v + q) * TB, TB), TB)
                wh_ref[part, there] = high
                wl_ref[part, there] = low
    dims = (((1,), (1,)), ((), ()))
    dot = lambda a, b: lax.dot_general(a, b, dims, preferred_element_type=F32)
    for n in range(0, 8, 2):
        part = slice(n * TB, (n + 2) * TB)
        wh, wl = wh_ref[part, :], wl_ref[part, :]
        r = (dot(xl_ref[...], wh) + dot(xh_ref[...], wl)) + dot(xh_ref[...], wh)
        for i in range(2):
            for j in range(tiles):
                out_ref[j, (n + i) * TB : (n + i + 1) * TB, :] = r[
                    j * TB : (j + 1) * TB, i * TB : (i + 1) * TB
                ]
    sub = lax.broadcasted_iota(jnp.int32, (TB, TB), 0)
    lane = lax.broadcasted_iota(jnp.int32, (TB, TB), 1)
    here = pl.ds(pl.multiple_of(at_ref[1] * TB, TB), TB)
    out_ref[step, here, :] = out_ref[step, here, :] - jnp.where(
        sub == lane, diag_ref[pl.ds(step, 1), :], 0.0
    )

    @pl.when(step == 0)
    def _():
        for v in range(2):
            for j in range(tiles):
                out_ref[j, v * TB : (v + 1) * TB, :] = -y_ref[v, j * TB : (j + 1) * TB, :]


def inverse(relative):
    offsets = jnp.arange(TB, dtype=jnp.int32)
    hit = relative[..., None, :] == offsets[:, None]
    return jnp.max(jnp.where(hit, offsets, -1), axis=-1)


def on_device(child_update, child_map, parent_diag):
    cube, row, col = lax.axis_index("cube"), lax.axis_index("row"), lax.axis_index("col")
    grid, columns = 32, 4
    position = cube * 4 + row
    sibling = position // (grid // 2)
    block = child_update[0]
    tiles, cols = block.shape[1], block.shape[3]
    rows = tiles * TB
    trade = [(i, i ^ 16) for i in range(grid)]

    raw = jnp.transpose(block[:, :, :, :2, :], (0, 3, 1, 2, 4)).reshape(2, 2, rows, TB)
    got = lax.ppermute(raw, ("cube", "row"), trade)
    early = tiles - 1
    bulk = lax.dynamic_index_in_dim(block, 1 - sibling, 0, keepdims=False)
    first, got = lax.optimization_barrier((bulk[:early], got))
    second = bulk[early:]
    arrived = []
    for part in (first, second):
        arrived.append(lax.ppermute(part, ("cube", "row"), trade))

    maps = jnp.stack(
        [
            lax.dynamic_index_in_dim(child_map, sibling, 0, keepdims=False),
            lax.dynamic_index_in_dim(child_map, 1 - sibling, 0, keepdims=False),
        ]
    )
    within = position % 16
    pair_tiles = (
        grid * jnp.arange(tiles, dtype=jnp.int32)[None, :]
        + 16 * jnp.arange(2, dtype=jnp.int32)[:, None]
        + within
    )
    pair_maps = jnp.swapaxes(
        lax.dynamic_index_in_dim(
            maps.reshape(2, tiles, 2, 16, TB), within, 3, keepdims=False
        ),
        1,
        2,
    )
    pair_maps = pair_maps - TB * pair_tiles[None, :, :, None]
    row_maps = lax.dynamic_index_in_dim(pair_maps, sibling, 1, keepdims=False)
    col_maps = lax.dynamic_index_in_dim(
        maps.reshape(2, cols, columns, TB), col, 2, keepdims=False
    )
    col_tiles = columns * jnp.arange(cols, dtype=jnp.int32) + col
    col_maps = col_maps - TB * col_tiles[None, :, None]
    pair_diag = jnp.swapaxes(
        lax.dynamic_index_in_dim(
            parent_diag.reshape(tiles, 2, 16, TB), within, 2, keepdims=False
        ),
        0,
        1,
    )
    diag = lax.dynamic_index_in_dim(pair_diag, sibling, 0, keepdims=False)
    meets = pair_tiles[:, None, :] == col_tiles[None, :2, None]
    panel_diag = jnp.where(meets[..., None], pair_diag[:, None], 0.0)

    strip = jax.ShapeDtypeStruct((2, rows, TB), F32)
    own, even, odd, piece = pl.pallas_call(
        place_kernel,
        out_shape=[strip, strip, strip, jax.ShapeDtypeStruct((2, TB, TB), F32)],
        in_specs=[SMEM] + [VMEM] * 5,
        out_specs=[VMEM] * 4,
    )(
        jnp.stack([sibling, col % 2]).astype(jnp.int32),
        raw, got, pair_maps, col_maps[:, :2], panel_diag,
    )

    quarters = []
    for m in range(4):
        pairs = []
        for s in range(2):
            for z in range(4):
                for half in range(2):
                    for core in range(2):
                        for y in range(4):
                            kind = (m + y) % 4
                            far, h = kind // 2, kind % 2
                            source = ((s * 4 + z) * 4 + half * 2 + core) * 4 + y
                            target = ((s ^ far) * 4 + z) * 4 + (half ^ far) * 2 + h
                            pairs.append((source, target * 4 + half * 2 + core))
        quarters.append(lax.ppermute(even if m % 2 == 0 else odd, ("cube", "row", "col"), pairs))
    groups = [
        [(s * 4 + z) * 4 + half * 2 + core for z in range(4) for core in range(2)]
        for s in range(2)
        for half in range(2)
    ]
    others = []
    for part in (slice(0, early * TB), slice(early * TB, rows)):
        turned = jnp.stack([quarter[:, part] for quarter in quarters])
        others.append(
            lax.all_gather(turned, ("cube", "row"), axis=0, axis_index_groups=groups)
        )

    pivot = pl.pallas_call(
        pivot_kernel,
        out_shape=jax.ShapeDtypeStruct((4, 8, 2, TB, TB), F32),
        in_specs=[VMEM],
        out_specs=VMEM,
        scratch_shapes=[
            pltpu.SemaphoreType.DMA((33,)),
            pltpu.SemaphoreType.DMA((4, 8)),
            pltpu.SemaphoreType.DMA,
        ],
        compiler_params=pltpu.CompilerParams(collective_id=0, has_side_effects=True),
    )(piece)

    own, pivot = lax.optimization_barrier((own, pivot))
    strips = []
    for hop in (1, 3, 2):
        strips.append(lax.ppermute(own, "col", [(c, (c + hop) % 4) for c in range(4)]))

    lower, inverses = pl.pallas_call(
        factor_kernel,
        out_shape=[jax.ShapeDtypeStruct((K, K), F32), jax.ShapeDtypeStruct((K // TB, TB, TB), F32)],
        in_specs=[VMEM],
        out_specs=[VMEM, VMEM],
        scratch_shapes=[pltpu.VMEM((TB, TB), F32)],
    )(pivot)
    y, x = pl.pallas_call(
        solve_kernel,
        out_shape=[
            jax.ShapeDtypeStruct((2, rows, TB), F32),
            jax.ShapeDtypeStruct((rows, K), F32),
        ],
        in_specs=[SMEM] + [VMEM] * 6,
        out_specs=[VMEM, VMEM],
        scratch_shapes=[pltpu.VMEM((rows, K), F32)],
    )(col.reshape(1), lower, inverses, own, *strips)

    row_inverse = inverse(row_maps).reshape(2, rows)
    solved = jnp.arange(cols) < 2
    col_inverse = jnp.where(solved[None, :, None], -1, inverse(col_maps))
    here = jnp.logical_and(row == col, jnp.logical_or(jnp.arange(tiles) > 0, cube >= 2))
    trailing_diag = jnp.where(here[:, None], diag, 0.0)
    crossed = (row // 2 != col // 2).astype(jnp.int32)
    at = jnp.stack([sibling, cube, 2 * crossed]).astype(jnp.int32)
    whole = jax.ShapeDtypeStruct((1, tiles, TB, cols, TB), F32)
    all_maps = pl.BlockSpec((2, cols, TB), lambda i, *_: (0, 0, 0))
    result = pl.pallas_call(
        keep_kernel,
        out_shape=whole,
        grid_spec=pltpu.PrefetchScalarGridSpec(
            num_scalar_prefetch=2,
            grid=(tiles,),
            in_specs=[
                pl.BlockSpec(
                    (1, 1, 1, TB, cols, TB), lambda i, at, _: (0, at[0], i, 0, 0, 0)
                ),
                all_maps,
            ],
            out_specs=pl.BlockSpec((1, 1, TB, cols, TB), lambda i, *_: (0, i, 0, 0, 0)),
        ),
    )(at, row_inverse, child_update, col_inverse)
    updates = []
    for start, gathered in zip((0, early), others):
        steps = gathered.shape[3] // TB
        updates.append(
            pl.pallas_call(
                functools.partial(update_kernel, start),
                out_shape=jax.ShapeDtypeStruct((tiles, steps * 8 * TB, TB), F32),
                grid_spec=pltpu.PrefetchScalarGridSpec(
                    num_scalar_prefetch=1,
                    grid=(steps,),
                    in_specs=[
                        pl.BlockSpec((8, 4, 2, TB, TB), lambda i, *_: (0, 0, 0, i, 0)),
                        VMEM,
                        VMEM,
                        VMEM,
                    ],
                    out_specs=pl.BlockSpec((tiles, 8 * TB, TB), lambda i, *_: (0, i, 0)),
                    scratch_shapes=[
                        pltpu.VMEM((8 * TB, K), jnp.bfloat16),
                        pltpu.VMEM((8 * TB, K), jnp.bfloat16),
                        pltpu.VMEM((rows, K), jnp.bfloat16),
                        pltpu.VMEM((rows, K), jnp.bfloat16),
                    ],
                ),
            )(at, gathered, x, y, trailing_diag)
        )
    for start, part in zip((0, early), arrived):
        block_at = lambda i, *_, start=start: (0, i + start, 0, 0, 0)
        result = pl.pallas_call(
            functools.partial(finish_kernel, start),
            out_shape=whole,
            grid_spec=pltpu.PrefetchScalarGridSpec(
                num_scalar_prefetch=1,
                grid=(part.shape[0],),
                in_specs=[
                    pl.BlockSpec((1, TB, cols, TB), lambda i, *_: (i, 0, 0, 0)),
                    all_maps,
                    pl.BlockSpec((1, 1, TB, cols, TB), block_at),
                    *(
                        pl.BlockSpec(
                            (1,) + update.shape[1:], lambda i, *_, start=start: (i + start, 0, 0)
                        )
                        for update in updates
                    ),
                ],
                out_specs=pl.BlockSpec((1, 1, TB, cols, TB), block_at),
            ),
            input_output_aliases={3: 0},
        )(row_inverse, part, col_inverse, result, *updates)
    return result


def solution(mesh):
    return jax.shard_map(
        on_device,
        mesh=mesh,
        in_specs=(P(("cube", "row"), None, None, None, "col", None), P(), P()),
        out_specs=P(("cube", "row"), None, None, "col", None),
        check_vma=False,
    )
```

```python
import functools

import jax
import jax.numpy as jnp
from jax import lax
from jax.experimental import pallas as pl
from jax.experimental.pallas import tpu as pltpu
from jax.sharding import PartitionSpec as P


K = 1024
TB = 128
HI = lax.Precision.HIGHEST
F32 = jnp.float32
MESH = pl.DeviceIdType.MESH
VMEM = pl.BlockSpec(memory_space=pltpu.VMEM)
ANY = pl.BlockSpec(memory_space=pl.ANY)
SMEM = pl.BlockSpec(memory_space=pltpu.SMEM)


def nt(a, b):
    return lax.dot_general(
        a, b, (((1,), (1,)), ((), ())), precision=HI, preferred_element_type=F32
    )


def nn(a, b):
    return lax.dot_general(
        a, b, (((1,), (0,)), ((), ())), precision=HI, preferred_element_type=F32
    )


def place_kernel(
    pick_ref, raw_ref, got_ref, rmap_ref, cmap_ref, diag_ref, own_ref, even_ref, odd_ref, piece_ref, hold_ref
):
    sub = lax.broadcasted_iota(jnp.int32, (TB, TB), 0)
    lane = lax.broadcasted_iota(jnp.int32, (TB, TB), 1)
    tiles = rmap_ref.shape[2]
    for v in range(2):
        for half in range(2):
            cols = [
                nt(ref[half, v], (sub == cmap_ref[t, v : v + 1, :]).astype(F32))
                for t, ref in enumerate((raw_ref, got_ref))
            ]
            for j in range(tiles):
                rows = slice(j * TB, (j + 1) * TB)
                total = jnp.where(sub == lane, diag_ref[half, v, j : j + 1, :], 0.0)
                for t in range(2):
                    hot = (sub == rmap_ref[t, half, j : j + 1, :]).astype(F32)
                    total += nn(hot, cols[t][rows, :])
                if half == 0 and j == 0:
                    piece_ref[v] = total
                hold_ref[jnp.where(pick_ref[0] == half, 0, 3), v, rows, :] = total
                hold_ref[jnp.where(pick_ref[1] == half, 1, 2), v, rows, :] = total
    for n, out_ref in enumerate((own_ref, even_ref, odd_ref)):
        out_ref[...] = hold_ref[n]


def pivot_kernel(
    piece_ref, even_ref, odd_ref, out_ref, turned_ref, send, recv, local, send_turned, recv_turned
):
    cube, row, col = lax.axis_index("cube"), lax.axis_index("row"), lax.axis_index("col")
    z = lax.rem(cube, 4)
    core, half = lax.rem(row, 2), row // 2
    at = lambda cu, ro, co: {"cube": cu, "row": ro, "col": co}
    mates = [at((cube - z) + lax.rem(z + d, 4), row, col) for d in (1, 2, 3)]
    across = at(lax.rem(cube + 4, 8), lax.rem(row + 2, 4), col)
    up, down = lax.rem(col + 1, 4), lax.rem(col + 3, 4)
    sides = [at(cube, row, up), at(cube, row, down)]
    other = at(cube, row + 1 - 2 * core, col)
    barrier = pltpu.get_barrier_semaphore()
    for peer in mates + [across] + sides + [other]:
        pl.semaphore_signal(barrier, inc=1, device_id=peer, device_id_type=MESH)
    side = cube // 4
    alone = row == col

    def to_kind(kind):
        far, h = kind // 2, lax.rem(kind, 2)
        x = lax.rem(side + far, 2) * 4 + z
        return at(x, lax.rem(half + far, 2) * 2 + h, row)

    crossed = lax.rem(half + col // 2, 2)
    sender = lambda y: at(
        lax.rem(side + crossed, 2) * 4 + z, col, y
    )
    for y in range(4):

        @pl.when(jnp.logical_not(jnp.logical_and(alone, col == y)))
        def _():
            pl.semaphore_signal(barrier, inc=1, device_id=sender(y), device_id_type=MESH)

    @pl.when(alone)
    def _():
        pl.semaphore_wait(barrier, 10)

    @pl.when(jnp.logical_not(alone))
    def _():
        pl.semaphore_wait(barrier, 11)

    def quarter(m):
        return pltpu.make_async_remote_copy(
            src_ref=(odd_ref if m % 2 else even_ref),
            dst_ref=turned_ref.at[m],
            send_sem=send_turned.at[m],
            recv_sem=recv_turned.at[m],
            device_id=to_kind(lax.rem(m + col, 4)),
            device_id_type=MESH,
        )

    def stays(m):
        return jnp.logical_and(alone, lax.rem(m + col, 4) == core)

    def keep_quarter(m):
        return pltpu.make_async_copy(
            odd_ref if m % 2 else even_ref, turned_ref.at[m], send_turned.at[m]
        )

    def copy(c, p, slot, peer, width):
        part = out_ref.at[c, p, pl.ds(0, width)]
        return pltpu.make_async_remote_copy(
            src_ref=part,
            dst_ref=part,
            send_sem=send.at[slot],
            recv_sem=recv.at[c, p],
            device_id=peer,
            device_id_type=MESH,
        )

    for zz in range(2):
        mine = zz * 4 + row

        @pl.when(z == zz)
        def _():
            part = pl.ds(0, zz + 1)
            own = pltpu.make_async_copy(piece_ref.at[part], out_ref.at[col, mine, part], local)
            own.start()
            own.wait()
            for i, peer in enumerate(mates):
                copy(col, mine, i, peer, zz + 1).start()

    for zz in range(2):
        p = zz * 4 + row
        n = zz

        @pl.when(z != zz)
        def _():
            copy(col, p, 0, other, zz + 1).wait_recv()

        copy(col, p, 3 + zz, across, zz + 1).start()
        copy(col, p, 5 + n, sides[0], zz + 1).start()
        copy(col, p, 7 + n, sides[1], zz + 1).start()
        copy(col, p, 9 + n, other, zz + 1).start()
    opposite = lax.rem(row + 2, 4)
    for zz in range(2):
        p = zz * 4 + opposite
        n = zz
        copy(col, p, 0, other, zz + 1).wait_recv()
        copy(col, p, 11 + n, sides[0], zz + 1).start()
        copy(col, p, 13 + n, sides[1], zz + 1).start()
        copy(col, p, 15 + n, other, zz + 1).start()
    for m in range(4):

        @pl.when(stays(m))
        def _():
            keep_quarter(m).start()

        @pl.when(jnp.logical_not(stays(m)))
        def _():
            quarter(m).start()

    for i, who in enumerate((row, opposite)):
        for zz in range(2):
            p = zz * 4 + who
            n = i * 2 + zz
            copy(down, p, 0, other, zz + 1).wait_recv()
            copy(down, p, 17 + n, other, zz + 1).start()

            @pl.when(core == 0)
            def _():
                copy(down, p, 21 + n, sides[0], zz + 1).start()

            copy(up, p, 0, other, zz + 1).wait_recv()
            copy(up, p, 25 + n, other, zz + 1).start()

            @pl.when(core == 1)
            def _():
                copy(up, p, 21 + n, sides[1], zz + 1).start()

    far = lax.rem(col + 2, 4)
    for i, who in enumerate((row, opposite)):
        for zz in range(2):
            p = zz * 4 + who
            copy(far, p, 0, other, zz + 1).wait_recv()
            copy(far, p, 29 + i * 2 + zz, other, zz + 1).start()
    for c in range(4):
        for zz in range(2):
            for hh in range(2):
                copy(c, zz * 4 + hh * 2 + 1 - core, 0, other, zz + 1).wait_recv()

    for zz in range(2):

        @pl.when(z == zz)
        def _():
            for i in range(3):
                copy(col, row, i, other, zz + 1).wait_send()

        for i in (3, 5, 7, 9, 11, 13, 15, 17, 19, 21, 23, 25, 27, 29, 31):
            copy(col, row, i + zz, other, zz + 1).wait_send()

    for m in range(4):

        @pl.when(stays(m))
        def _():
            keep_quarter(m).wait()

        @pl.when(jnp.logical_not(stays(m)))
        def _():
            quarter(m).wait()


def leaf(d_ref, li_ref):
    a_rows = [d_ref[8 * g : 8 * g + 8, :] for g in range(16)]
    lane = lax.broadcasted_iota(jnp.int32, (8, TB), 1)
    sub = lax.broadcasted_iota(jnp.int32, (8, TB), 0)
    b_rows = [(lane == sub + 8 * g).astype(F32) for g in range(16)]
    wide = lambda x: jnp.broadcast_to(x, (8, TB))
    for g0 in range(16):
        j = 8 * g0
        c = [wide(a_rows[g0][:, j + q : j + q + 1]) for q in range(8)]
        e = [[wide(c[q][i : i + 1, :]) if i >= q else None for q in range(8)] for i in range(8)]
        a = [wide(a_rows[g0][q : q + 1, :]) for q in range(8)]
        b = [wide(b_rows[g0][q : q + 1, :]) for q in range(8)]
        more = g0 + 1 < 16
        if more:
            m = [wide(a_rows[g0 + 1][:, j + q : j + q + 1]) for q in range(8)]
        s, t = [None] * 8, [None] * 8
        low = [[None] * 8 for _ in range(8)]
        for q in range(8):
            inv = 1.0 / e[q][q]
            s[q], t[q] = a[q] * inv, b[q] * inv
            for i in range(q + 1, 8):
                low[i][q] = e[i][q] * inv
            for i in range(q + 1, 8):
                for p in range(q + 1, i + 1):
                    e[i][p] = e[i][p] - low[i][q] * e[p][q]
            for i in range(q + 1, 8):
                a[i] = a[i] - low[i][q] * a[q]
                b[i] = b[i] - low[i][q] * b[q]
                if more:
                    m[i] = m[i] - low[i][q] * m[q]
            if more:
                a_rows[g0 + 1] = a_rows[g0 + 1] - m[q] * s[q]
                b_rows[g0 + 1] = b_rows[g0 + 1] - m[q] * t[q]
            li_ref[j + q : j + q + 1, :] = (b[q] * lax.rsqrt(e[q][q]))[0:1, :]
        if g0 + 2 < 16:
            for q in range(7, -1, -1):
                for i in range(q + 1, 8):
                    s[q] = s[q] - low[i][q] * s[i]
                    t[q] = t[q] - low[i][q] * t[i]
            for g in range(g0 + 2, 16):
                m = [wide(a_rows[g][:, j + q : j + q + 1]) for q in range(8)]
                da, db = m[0] * s[0], m[0] * t[0]
                for q in range(1, 8):
                    da, db = da + m[q] * s[q], db + m[q] * t[q]
                a_rows[g] = a_rows[g] - da
                b_rows[g] = b_rows[g] - db


def factor_kernel(s_ref, m_ref, li_ref, d_ref):
    blocks, pair_width = K // TB, 2 * TB
    for c in range(4):
        for v in range(2):
            u = 4 * v + c
            for p in range(u, blocks):
                m_ref[p * TB : (p + 1) * TB, u * TB : (u + 1) * TB] = s_ref[c, p, v]

    def step(k, _):
        here = pl.ds(pl.multiple_of(k * TB, TB), TB)
        d_ref[...] = m_ref[here, here]
        leaf(d_ref, li_ref.at[k])
        m_ref[:, here] = nt(m_ref[:, here], li_ref[k])

        @pl.when(lax.rem(k, 2) == 0)
        def _():
            after = pl.ds(pl.multiple_of((k + 1) * TB, TB), TB)
            m_ref[:, after] = m_ref[:, after] - nt(m_ref[:, here], m_ref[after, here])

        @pl.when(lax.rem(k, 2) == 1)
        def _():
            pair = pl.ds(pl.multiple_of((k - 1) * TB, TB), pair_width)

            def trail(i, _):
                part = pl.ds(pl.multiple_of(i * pair_width, pair_width), pair_width)
                m_ref[:, part] = m_ref[:, part] - nt(m_ref[:, pair], m_ref[part, pair])
                return 0

            lax.fori_loop((k + 1) // 2, blocks // 2, trail, 0)

        return 0

    lax.fori_loop(0, blocks, step, 0)


def solve_kernel(col_ref, l_ref, li_ref, own_ref, low_ref, high_ref, far_ref, y_ref, x_ref, m_ref):
    blocks, pair_width = K // TB, 2 * TB
    col = col_ref[0]
    for part, ref in enumerate((own_ref, high_ref, far_ref, low_ref)):
        for v in range(2):
            u = 4 * v + lax.rem(col + part, 4)
            m_ref[:, pl.ds(pl.multiple_of(u * TB, TB), TB)] = ref[v]

    def places(n):
        at = n * pair_width
        return (
            pl.ds(pl.multiple_of(at, TB), TB),
            pl.ds(pl.multiple_of(at + TB, TB), TB),
            pl.ds(pl.multiple_of(at, pair_width), pair_width),
        )

    def forth(n, _):
        first, last, pair = places(n)
        m_ref[:, first] = nt(m_ref[:, first], li_ref[2 * n])
        rest = m_ref[:, last] - nt(m_ref[:, first], l_ref[last, first])
        m_ref[:, last] = nt(rest, li_ref[2 * n + 1])

        def trail(i, _):
            part = places(i)[2]
            m_ref[:, part] = m_ref[:, part] - nt(m_ref[:, pair], l_ref[part, pair])
            return 0

        lax.fori_loop(n + 1, blocks // 2, trail, 0)
        return 0

    lax.fori_loop(0, blocks // 2, forth, 0)
    for v in range(2):
        y_ref[v] = m_ref[:, pl.ds(pl.multiple_of((4 * v + col) * TB, TB), TB)]

    def back(i, _):
        n = blocks // 2 - 1 - i
        first, last, pair = places(n)
        x_ref[:, last] = nn(m_ref[:, last], li_ref[2 * n + 1])
        rest = m_ref[:, first] - nn(x_ref[:, last], l_ref[last, first])
        x_ref[:, first] = nn(rest, li_ref[2 * n])

        def lead(j, _):
            part = places(j)[2]
            m_ref[:, part] = m_ref[:, part] - nn(x_ref[:, pair], l_ref[pair, part])
            return 0

        lax.fori_loop(0, n, lead, 0)
        return 0

    lax.fori_loop(0, blocks // 2, back, 0)


def split(x):
    high = x.astype(jnp.bfloat16)
    return high, (x - high.astype(F32)).astype(jnp.bfloat16)


def place_rows(tile, t, rinv_ref, cinv_ref, from_ref, less, out_ref):
    groups = range(0, from_ref.shape[-2], 8)
    index = [jnp.maximum(cinv_ref[t, g : g + 8], 0) for g in groups]
    live = [(cinv_ref[t, g : g + 8] >= 0).astype(F32) for g in groups]
    base = tile * TB

    def body(o, _):
        s = rinv_ref[t, base + o]
        weight = jnp.where(s >= 0, 1.0, 0.0)
        s = jnp.maximum(s, 0)
        for g, at, keep in zip(groups, index, live):
            x = jnp.take_along_axis(from_ref[s, g : g + 8], at, axis=1) * (keep * weight)
            out_ref[o, g : g + 8] = x if less is None else x + less(o, g)
        return 0

    lax.fori_loop(0, TB, body, 0, unroll=16)


def keep_kernel(
    at_ref, rinv_ref, kept_ref, sent_ref, cinv_ref, out_ref, early_ref, late_ref
):
    step, steps = pl.program_id(0), pl.num_programs(0)

    @pl.when(step < steps - 1)
    def _():
        early_ref[0] = sent_ref[0, 0, 0]

    @pl.when(step == steps - 1)
    def _():
        late_ref[0] = sent_ref[0, 0, 0]

    place_rows(step, 0, rinv_ref, cinv_ref, kept_ref.at[0, 0, 0], None, out_ref.at[0, 0])


def finish_kernel(start, rinv_ref, got_ref, cinv_ref, kept_ref, r_ref, out_ref):
    def less(o, g):
        return kept_ref[0, 0, o, g : g + 8] - r_ref.at[0][pl.ds(g * TB + o, 8, stride=TB), :]

    tile = pl.program_id(0) + start
    place_rows(tile, 1, rinv_ref, cinv_ref, got_ref.at[0], less, out_ref.at[0, 0])


def update_kernel(
    at_ref, g_ref, x_ref, y_ref, diag_ref, out_ref, wh_ref, wl_ref, xh_ref, xl_ref
):
    step = pl.program_id(0)
    tiles = out_ref.shape[0]

    @pl.when(step == 0)
    def _():
        xh_ref[...], xl_ref[...] = split(x_ref[...])

    for n in range(8):
        part = slice(n * TB, (n + 1) * TB)
        for m in range(4):
            q = lax.rem(at_ref[2] + n // 4 + 4 - m, 4)
            for v in range(2):
                high, low = split(g_ref[(n % 4) * 2 + n // 4, m, v])
                there = pl.ds(pl.multiple_of((4 * v + q) * TB, TB), TB)
                wh_ref[part, there] = high
                wl_ref[part, there] = low
    dims = (((1,), (1,)), ((), ()))
    dot = lambda a, b: lax.dot_general(a, b, dims, preferred_element_type=F32)
    for n in range(0, 8, 2):
        part = slice(n * TB, (n + 2) * TB)
        wh, wl = wh_ref[part, :], wl_ref[part, :]
        r = (dot(xl_ref[...], wh) + dot(xh_ref[...], wl)) + dot(xh_ref[...], wh)
        for i in range(2):
            for j in range(tiles):
                out_ref[j, (n + i) * TB : (n + i + 1) * TB, :] = r[
                    j * TB : (j + 1) * TB, i * TB : (i + 1) * TB
                ]
    sub = lax.broadcasted_iota(jnp.int32, (TB, TB), 0)
    lane = lax.broadcasted_iota(jnp.int32, (TB, TB), 1)
    here = pl.ds(pl.multiple_of(at_ref[1] * TB, TB), TB)
    out_ref[step, here, :] = out_ref[step, here, :] - jnp.where(
        sub == lane, diag_ref[pl.ds(step, 1), :], 0.0
    )

    @pl.when(step == 0)
    def _():
        for v in range(2):
            for j in range(tiles):
                out_ref[j, v * TB : (v + 1) * TB, :] = -y_ref[v, j * TB : (j + 1) * TB, :]


def inverse(relative):
    offsets = jnp.arange(TB, dtype=jnp.int32)
    hit = relative[..., None, :] == offsets[:, None]
    return jnp.max(jnp.where(hit, offsets, -1), axis=-1)


def on_device(child_update, child_map, parent_diag):
    cube, row, col = lax.axis_index("cube"), lax.axis_index("row"), lax.axis_index("col")
    grid, columns = 32, 4
    position = cube * 4 + row
    sibling = position // (grid // 2)
    block = child_update[0]
    tiles, cols = block.shape[1], block.shape[3]
    rows = tiles * TB
    trade = [(i, i ^ 16) for i in range(grid)]

    raw = jnp.transpose(block[:, :, :, :2, :], (0, 3, 1, 2, 4)).reshape(2, 2, rows, TB)
    got = lax.ppermute(raw, ("cube", "row"), trade)
    early = tiles - 1
    maps = jnp.stack(
        [
            lax.dynamic_index_in_dim(child_map, sibling, 0, keepdims=False),
            lax.dynamic_index_in_dim(child_map, 1 - sibling, 0, keepdims=False),
        ]
    )
    within = position % 16
    pair_tiles = (
        grid * jnp.arange(tiles, dtype=jnp.int32)[None, :]
        + 16 * jnp.arange(2, dtype=jnp.int32)[:, None]
        + within
    )
    pair_maps = jnp.swapaxes(
        lax.dynamic_index_in_dim(
            maps.reshape(2, tiles, 2, 16, TB), within, 3, keepdims=False
        ),
        1,
        2,
    )
    pair_maps = pair_maps - TB * pair_tiles[None, :, :, None]
    row_maps = lax.dynamic_index_in_dim(pair_maps, sibling, 1, keepdims=False)
    col_maps = lax.dynamic_index_in_dim(
        maps.reshape(2, cols, columns, TB), col, 2, keepdims=False
    )
    col_tiles = columns * jnp.arange(cols, dtype=jnp.int32) + col
    col_maps = col_maps - TB * col_tiles[None, :, None]
    pair_diag = jnp.swapaxes(
        lax.dynamic_index_in_dim(
            parent_diag.reshape(tiles, 2, 16, TB), within, 2, keepdims=False
        ),
        0,
        1,
    )
    diag = lax.dynamic_index_in_dim(pair_diag, sibling, 0, keepdims=False)
    meets = pair_tiles[:, None, :] == col_tiles[None, :2, None]
    panel_diag = jnp.where(meets[..., None], pair_diag[:, None], 0.0)

    row_inverse = inverse(row_maps).reshape(2, rows)
    solved = jnp.arange(cols) < 2
    col_inverse = jnp.where(solved[None, :, None], -1, inverse(col_maps))
    here = jnp.logical_and(row == col, jnp.logical_or(jnp.arange(tiles) > 0, cube >= 2))
    trailing_diag = jnp.where(here[:, None], diag, 0.0)
    crossed = (row // 2 != col // 2).astype(jnp.int32)
    at = jnp.stack([sibling, cube, 2 * crossed]).astype(jnp.int32)
    whole = jax.ShapeDtypeStruct((1, tiles, TB, cols, TB), F32)
    all_maps = pl.BlockSpec((2, cols, TB), lambda i, *_: (0, 0, 0))
    result, first, second = pl.pallas_call(
        keep_kernel,
        out_shape=[
            whole,
            jax.ShapeDtypeStruct((early, TB, cols, TB), F32),
            jax.ShapeDtypeStruct((tiles - early, TB, cols, TB), F32),
        ],
        grid_spec=pltpu.PrefetchScalarGridSpec(
            num_scalar_prefetch=2,
            grid=(tiles,),
            in_specs=[
                pl.BlockSpec(
                    (1, 1, 1, TB, cols, TB), lambda i, at, _: (0, at[0], i, 0, 0, 0)
                ),
                pl.BlockSpec((1, 1, 1, TB, cols, TB), lambda i, at, _: (0, 1 - at[0], i, 0, 0, 0)),
                all_maps,
            ],
            out_specs=[
                pl.BlockSpec((1, 1, TB, cols, TB), lambda i, *_: (0, i, 0, 0, 0)),
                pl.BlockSpec((1, TB, cols, TB), lambda i, *_: (jnp.minimum(i, early - 1), 0, 0, 0)),
                pl.BlockSpec((1, TB, cols, TB), lambda i, *_: (0, 0, 0, 0)),
            ],
        ),
    )(at, row_inverse, child_update, child_update, col_inverse)
    first, second, got = lax.optimization_barrier((first, second, got))
    arrived = []
    for part in (first, second):
        arrived.append(lax.ppermute(part, ("cube", "row"), trade))

    strip = jax.ShapeDtypeStruct((2, rows, TB), F32)
    own, even, odd, piece = pl.pallas_call(
        place_kernel,
        out_shape=[strip, strip, strip, jax.ShapeDtypeStruct((2, TB, TB), F32)],
        in_specs=[SMEM] + [VMEM] * 5,
        out_specs=[VMEM] * 4,
        scratch_shapes=[pltpu.VMEM((4, 2, rows, TB), F32)],
    )(
        jnp.stack([sibling, col % 2]).astype(jnp.int32),
        raw, got, pair_maps, col_maps[:, :2], panel_diag,
    )

    pivot, turned = pl.pallas_call(
        pivot_kernel,
        out_shape=[
            jax.ShapeDtypeStruct((4, 8, 2, TB, TB), F32),
            jax.ShapeDtypeStruct((4, 2, rows, TB), F32),
        ],
        in_specs=[VMEM, ANY, ANY],
        out_specs=[VMEM, ANY],
        scratch_shapes=[
            pltpu.SemaphoreType.DMA((33,)),
            pltpu.SemaphoreType.DMA((4, 8)),
            pltpu.SemaphoreType.DMA,
            pltpu.SemaphoreType.DMA((4,)),
            pltpu.SemaphoreType.DMA((4,)),
        ],
        compiler_params=pltpu.CompilerParams(collective_id=0, has_side_effects=True),
    )(piece, even, odd)

    groups = [
        [(s * 4 + z) * 4 + half * 2 + core for z in range(4) for core in range(2)]
        for s in range(2)
        for half in range(2)
    ]
    others = lax.all_gather(turned, ("cube", "row"), axis=0, axis_index_groups=groups)
    own, pivot = lax.optimization_barrier((own, pivot))
    strips = []
    for hop in (1, 3, 2):
        strips.append(lax.ppermute(own, "col", [(c, (c + hop) % 4) for c in range(4)]))

    lower, inverses = pl.pallas_call(
        factor_kernel,
        out_shape=[jax.ShapeDtypeStruct((K, K), F32), jax.ShapeDtypeStruct((K // TB, TB, TB), F32)],
        in_specs=[VMEM],
        out_specs=[VMEM, VMEM],
        scratch_shapes=[pltpu.VMEM((TB, TB), F32)],
    )(pivot)
    y, x = pl.pallas_call(
        solve_kernel,
        out_shape=[
            jax.ShapeDtypeStruct((2, rows, TB), F32),
            jax.ShapeDtypeStruct((rows, K), F32),
        ],
        in_specs=[SMEM] + [VMEM] * 6,
        out_specs=[VMEM, VMEM],
        scratch_shapes=[pltpu.VMEM((rows, K), F32)],
    )(col.reshape(1), lower, inverses, own, *strips)

    update = pl.pallas_call(
        update_kernel,
        out_shape=jax.ShapeDtypeStruct((tiles, cols * TB, TB), F32),
        grid_spec=pltpu.PrefetchScalarGridSpec(
            num_scalar_prefetch=1,
            grid=(cols // 8,),
            in_specs=[
                pl.BlockSpec((8, 4, 2, TB, TB), lambda i, *_: (0, 0, 0, i, 0)),
                VMEM,
                VMEM,
                VMEM,
            ],
            out_specs=pl.BlockSpec((tiles, 8 * TB, TB), lambda i, *_: (0, i, 0)),
            scratch_shapes=[
                pltpu.VMEM((8 * TB, K), jnp.bfloat16),
                pltpu.VMEM((8 * TB, K), jnp.bfloat16),
                pltpu.VMEM((rows, K), jnp.bfloat16),
                pltpu.VMEM((rows, K), jnp.bfloat16),
            ],
        ),
    )(at, others, x, y, trailing_diag)
    for start, part in zip((0, early), arrived):
        block_at = lambda i, *_, start=start: (0, i + start, 0, 0, 0)
        result = pl.pallas_call(
            functools.partial(finish_kernel, start),
            out_shape=whole,
            grid_spec=pltpu.PrefetchScalarGridSpec(
                num_scalar_prefetch=1,
                grid=(part.shape[0],),
                in_specs=[
                    pl.BlockSpec((1, TB, cols, TB), lambda i, *_: (i, 0, 0, 0)),
                    all_maps,
                    pl.BlockSpec((1, 1, TB, cols, TB), block_at),
                    pl.BlockSpec((1, cols * TB, TB), lambda i, *_, start=start: (i + start, 0, 0)),
                ],
                out_specs=pl.BlockSpec((1, 1, TB, cols, TB), block_at),
            ),
            input_output_aliases={3: 0},
        )(row_inverse, part, col_inverse, result, update)
    return result


def solution(mesh):
    return jax.shard_map(
        on_device,
        mesh=mesh,
        in_specs=(P(("cube", "row"), None, None, None, "col", None), P(), P()),
        out_specs=P(("cube", "row"), None, None, "col", None),
        check_vma=False,
    )
```

```python
import functools

import jax
import jax.numpy as jnp
from jax import lax
from jax.experimental import pallas as pl
from jax.experimental.pallas import tpu as pltpu
from jax.sharding import PartitionSpec as P


K = 1024
TB = 128
HI = lax.Precision.HIGHEST
F32 = jnp.float32
MESH = pl.DeviceIdType.MESH
VMEM = pl.BlockSpec(memory_space=pltpu.VMEM)
ANY = pl.BlockSpec(memory_space=pl.ANY)
SMEM = pl.BlockSpec(memory_space=pltpu.SMEM)


def nt(a, b):
    return lax.dot_general(
        a, b, (((1,), (1,)), ((), ())), precision=HI, preferred_element_type=F32
    )


def nn(a, b):
    return lax.dot_general(
        a, b, (((1,), (0,)), ((), ())), precision=HI, preferred_element_type=F32
    )


def place_kernel(
    pick_ref, raw_ref, got_ref, rmap_ref, cmap_ref, diag_ref, own_ref, even_ref, odd_ref, piece_ref, hold_ref
):
    sub = lax.broadcasted_iota(jnp.int32, (TB, TB), 0)
    lane = lax.broadcasted_iota(jnp.int32, (TB, TB), 1)
    tiles = rmap_ref.shape[2]
    for v in range(2):
        for half in range(2):
            cols = [
                nt(ref[half, v], (sub == cmap_ref[t, v : v + 1, :]).astype(F32))
                for t, ref in enumerate((raw_ref, got_ref))
            ]
            for j in range(tiles):
                rows = slice(j * TB, (j + 1) * TB)
                total = jnp.where(sub == lane, diag_ref[half, v, j : j + 1, :], 0.0)
                for t in range(2):
                    hot = (sub == rmap_ref[t, half, j : j + 1, :]).astype(F32)
                    total += nn(hot, cols[t][rows, :])
                if half == 0 and j == 0:
                    piece_ref[v] = total
                hold_ref[jnp.where(pick_ref[0] == half, 0, 3), v, rows, :] = total
                hold_ref[jnp.where(pick_ref[1] == half, 1, 2), v, rows, :] = total
    for n, out_ref in enumerate((own_ref, even_ref, odd_ref)):
        out_ref[...] = hold_ref[n]


def pivot_kernel(
    piece_ref, even_ref, odd_ref, out_ref, turned_ref, send, recv, local, send_turned, recv_turned,
    relay_ref, send_relay, recv_relay,
):
    cube, row, col = lax.axis_index("cube"), lax.axis_index("row"), lax.axis_index("col")
    z = lax.rem(cube, 4)
    core, half = lax.rem(row, 2), row // 2
    at = lambda cu, ro, co: {"cube": cu, "row": ro, "col": co}
    mates = [at((cube - z) + lax.rem(z + d, 4), row, col) for d in (1, 2, 3)]
    across = at(lax.rem(cube + 4, 8), lax.rem(row + 2, 4), col)
    up, down = lax.rem(col + 1, 4), lax.rem(col + 3, 4)
    sides = [at(cube, row, up), at(cube, row, down)]
    other = at(cube, row + 1 - 2 * core, col)
    barrier = pltpu.get_barrier_semaphore()
    for peer in mates + [across] + sides + [other]:
        pl.semaphore_signal(barrier, inc=1, device_id=peer, device_id_type=MESH)
    side = cube // 4
    alone = row == col

    def to_kind(kind):
        far, h = kind // 2, lax.rem(kind, 2)
        x = lax.rem(side + far, 2) * 4 + z
        return at(x, lax.rem(half + far, 2) * 2 + h, row)

    crossed = lax.rem(half + col // 2, 2)
    sender = lambda y: at(
        lax.rem(side + crossed, 2) * 4 + z, col, y
    )
    twice = lax.rem(col + 4 - row, 4) == 2
    served = lax.rem(col + 1 + 2 * lax.rem(col + 1, 2), 4)
    served_crossed = lax.rem(half + served // 2, 2)
    served_slot = lax.rem(2 * served_crossed + core + 8 - served - 2, 4)
    for d in (0, 1, 3):
        y = lax.rem(col + d, 4)

        @pl.when(jnp.logical_not(jnp.logical_and(alone, d == 0)))
        def _():
            pl.semaphore_signal(barrier, inc=1, device_id=sender(y), device_id_type=MESH)

    pl.semaphore_signal(
        barrier,
        inc=1,
        device_id=at(
            lax.rem(side + served_crossed, 2) * 4 + z, served, lax.rem(served + 2, 4)
        ),
        device_id_type=MESH,
    )

    @pl.when(alone)
    def _():
        pl.semaphore_wait(barrier, 10)

    @pl.when(jnp.logical_not(alone))
    def _():
        pl.semaphore_wait(barrier, 11)

    def quarter(m):
        return pltpu.make_async_remote_copy(
            src_ref=(odd_ref if m % 2 else even_ref),
            dst_ref=turned_ref.at[m],
            send_sem=send_turned.at[m],
            recv_sem=recv_turned.at[m],
            device_id=to_kind(lax.rem(m + col, 4)),
            device_id_type=MESH,
        )

    def to_relay(m):
        target = to_kind(lax.rem(m + col, 4))
        return pltpu.make_async_remote_copy(
            src_ref=(odd_ref if m % 2 else even_ref),
            dst_ref=relay_ref,
            send_sem=send_turned.at[m],
            recv_sem=recv_relay,
            device_id=at(target["cube"], target["row"], lax.rem(row + 3 - 2 * lax.rem(row, 2), 4)),
            device_id_type=MESH,
        )

    onward = pltpu.make_async_remote_copy(
        src_ref=relay_ref,
        dst_ref=turned_ref.at[served_slot],
        send_sem=send_relay,
        recv_sem=recv_turned.at[served_slot],
        device_id=at(cube, row, served),
        device_id_type=MESH,
    )

    def stays(m):
        return jnp.logical_and(alone, lax.rem(m + col, 4) == core)

    def keep_quarter(m):
        return pltpu.make_async_copy(
            odd_ref if m % 2 else even_ref, turned_ref.at[m], send_turned.at[m]
        )

    def copy(c, p, slot, peer, width):
        part = out_ref.at[c, p, pl.ds(0, width)]
        return pltpu.make_async_remote_copy(
            src_ref=part,
            dst_ref=part,
            send_sem=send.at[slot],
            recv_sem=recv.at[c, p],
            device_id=peer,
            device_id_type=MESH,
        )

    for zz in range(2):
        mine = zz * 4 + row

        @pl.when(z == zz)
        def _():
            part = pl.ds(0, zz + 1)
            own = pltpu.make_async_copy(piece_ref.at[part], out_ref.at[col, mine, part], local)
            own.start()
            own.wait()
            for i, peer in enumerate(mates):
                copy(col, mine, i, peer, zz + 1).start()

    for zz in range(2):
        p = zz * 4 + row
        n = zz

        @pl.when(z != zz)
        def _():
            copy(col, p, 0, other, zz + 1).wait_recv()

        copy(col, p, 3 + zz, across, zz + 1).start()
        copy(col, p, 5 + n, sides[0], zz + 1).start()
        copy(col, p, 7 + n, sides[1], zz + 1).start()
        copy(col, p, 9 + n, other, zz + 1).start()
    opposite = lax.rem(row + 2, 4)
    for zz in range(2):
        p = zz * 4 + opposite
        n = zz
        copy(col, p, 0, other, zz + 1).wait_recv()
        copy(col, p, 11 + n, sides[0], zz + 1).start()
        copy(col, p, 13 + n, sides[1], zz + 1).start()
        copy(col, p, 15 + n, other, zz + 1).start()
    for m in range(4):

        @pl.when(stays(m))
        def _():
            keep_quarter(m).start()

        @pl.when(twice)
        def _():
            to_relay(m).start()

        @pl.when(jnp.logical_not(jnp.logical_or(stays(m), twice)))
        def _():
            quarter(m).start()

    for i, who in enumerate((row, opposite)):
        for zz in range(2):
            p = zz * 4 + who
            n = i * 2 + zz
            copy(down, p, 0, other, zz + 1).wait_recv()
            copy(down, p, 17 + n, other, zz + 1).start()

            @pl.when(core == 0)
            def _():
                copy(down, p, 21 + n, sides[0], zz + 1).start()

            copy(up, p, 0, other, zz + 1).wait_recv()
            copy(up, p, 25 + n, other, zz + 1).start()

            @pl.when(core == 1)
            def _():
                copy(up, p, 21 + n, sides[1], zz + 1).start()

    to_relay(0).wait_recv()
    onward.start()
    far = lax.rem(col + 2, 4)
    for i, who in enumerate((row, opposite)):
        for zz in range(2):
            p = zz * 4 + who
            copy(far, p, 0, other, zz + 1).wait_recv()
            copy(far, p, 29 + i * 2 + zz, other, zz + 1).start()
    for c in range(4):
        for zz in range(2):
            for hh in range(2):
                copy(c, zz * 4 + hh * 2 + 1 - core, 0, other, zz + 1).wait_recv()

    for zz in range(2):

        @pl.when(z == zz)
        def _():
            for i in range(3):
                copy(col, row, i, other, zz + 1).wait_send()

        for i in (3, 5, 7, 9, 11, 13, 15, 17, 19, 21, 23, 25, 27, 29, 31):
            copy(col, row, i + zz, other, zz + 1).wait_send()

    for m in range(4):

        @pl.when(stays(m))
        def _():
            keep_quarter(m).wait()

        @pl.when(jnp.logical_not(stays(m)))
        def _():
            quarter(m).wait()

    onward.wait_send()


def leaf(d_ref, li_ref):
    a_rows = [d_ref[8 * g : 8 * g + 8, :] for g in range(16)]
    lane = lax.broadcasted_iota(jnp.int32, (8, TB), 1)
    sub = lax.broadcasted_iota(jnp.int32, (8, TB), 0)
    b_rows = [(lane == sub + 8 * g).astype(F32) for g in range(16)]
    wide = lambda x: jnp.broadcast_to(x, (8, TB))
    for g0 in range(16):
        j = 8 * g0
        c = [wide(a_rows[g0][:, j + q : j + q + 1]) for q in range(8)]
        e = [[wide(c[q][i : i + 1, :]) if i >= q else None for q in range(8)] for i in range(8)]
        a = [wide(a_rows[g0][q : q + 1, :]) for q in range(8)]
        b = [wide(b_rows[g0][q : q + 1, :]) for q in range(8)]
        more = g0 + 1 < 16
        if more:
            m = [wide(a_rows[g0 + 1][:, j + q : j + q + 1]) for q in range(8)]
        s, t = [None] * 8, [None] * 8
        low = [[None] * 8 for _ in range(8)]
        for q in range(8):
            inv = 1.0 / e[q][q]
            s[q], t[q] = a[q] * inv, b[q] * inv
            for i in range(q + 1, 8):
                low[i][q] = e[i][q] * inv
            for i in range(q + 1, 8):
                for p in range(q + 1, i + 1):
                    e[i][p] = e[i][p] - low[i][q] * e[p][q]
            for i in range(q + 1, 8):
                a[i] = a[i] - low[i][q] * a[q]
                b[i] = b[i] - low[i][q] * b[q]
                if more:
                    m[i] = m[i] - low[i][q] * m[q]
            if more:
                a_rows[g0 + 1] = a_rows[g0 + 1] - m[q] * s[q]
                b_rows[g0 + 1] = b_rows[g0 + 1] - m[q] * t[q]
            li_ref[j + q : j + q + 1, :] = (b[q] * lax.rsqrt(e[q][q]))[0:1, :]
        if g0 + 2 < 16:
            for q in range(7, -1, -1):
                for i in range(q + 1, 8):
                    s[q] = s[q] - low[i][q] * s[i]
                    t[q] = t[q] - low[i][q] * t[i]
            for g in range(g0 + 2, 16):
                m = [wide(a_rows[g][:, j + q : j + q + 1]) for q in range(8)]
                da, db = m[0] * s[0], m[0] * t[0]
                for q in range(1, 8):
                    da, db = da + m[q] * s[q], db + m[q] * t[q]
                a_rows[g] = a_rows[g] - da
                b_rows[g] = b_rows[g] - db


def factor_kernel(s_ref, m_ref, li_ref, d_ref):
    blocks, pair_width = K // TB, 2 * TB
    for c in range(4):
        for v in range(2):
            u = 4 * v + c
            for p in range(u, blocks):
                m_ref[p * TB : (p + 1) * TB, u * TB : (u + 1) * TB] = s_ref[c, p, v]

    def step(k, _):
        here = pl.ds(pl.multiple_of(k * TB, TB), TB)
        d_ref[...] = m_ref[here, here]
        leaf(d_ref, li_ref.at[k])
        m_ref[:, here] = nt(m_ref[:, here], li_ref[k])

        @pl.when(lax.rem(k, 2) == 0)
        def _():
            after = pl.ds(pl.multiple_of((k + 1) * TB, TB), TB)
            m_ref[:, after] = m_ref[:, after] - nt(m_ref[:, here], m_ref[after, here])

        @pl.when(lax.rem(k, 2) == 1)
        def _():
            pair = pl.ds(pl.multiple_of((k - 1) * TB, TB), pair_width)

            def trail(i, _):
                part = pl.ds(pl.multiple_of(i * pair_width, pair_width), pair_width)
                m_ref[:, part] = m_ref[:, part] - nt(m_ref[:, pair], m_ref[part, pair])
                return 0

            lax.fori_loop((k + 1) // 2, blocks // 2, trail, 0)

        return 0

    lax.fori_loop(0, blocks, step, 0)


def solve_kernel(col_ref, l_ref, li_ref, own_ref, low_ref, high_ref, far_ref, y_ref, x_ref, m_ref):
    blocks, pair_width = K // TB, 2 * TB
    col = col_ref[0]
    for part, ref in enumerate((own_ref, high_ref, far_ref, low_ref)):
        for v in range(2):
            u = 4 * v + lax.rem(col + part, 4)
            m_ref[:, pl.ds(pl.multiple_of(u * TB, TB), TB)] = ref[v]

    def places(n):
        at = n * pair_width
        return (
            pl.ds(pl.multiple_of(at, TB), TB),
            pl.ds(pl.multiple_of(at + TB, TB), TB),
            pl.ds(pl.multiple_of(at, pair_width), pair_width),
        )

    def forth(n, _):
        first, last, pair = places(n)
        m_ref[:, first] = nt(m_ref[:, first], li_ref[2 * n])
        rest = m_ref[:, last] - nt(m_ref[:, first], l_ref[last, first])
        m_ref[:, last] = nt(rest, li_ref[2 * n + 1])

        def trail(i, _):
            part = places(i)[2]
            m_ref[:, part] = m_ref[:, part] - nt(m_ref[:, pair], l_ref[part, pair])
            return 0

        lax.fori_loop(n + 1, blocks // 2, trail, 0)
        return 0

    lax.fori_loop(0, blocks // 2, forth, 0)
    for v in range(2):
        y_ref[v] = m_ref[:, pl.ds(pl.multiple_of((4 * v + col) * TB, TB), TB)]

    def back(i, _):
        n = blocks // 2 - 1 - i
        first, last, pair = places(n)
        x_ref[:, last] = nn(m_ref[:, last], li_ref[2 * n + 1])
        rest = m_ref[:, first] - nn(x_ref[:, last], l_ref[last, first])
        x_ref[:, first] = nn(rest, li_ref[2 * n])

        def lead(j, _):
            part = places(j)[2]
            m_ref[:, part] = m_ref[:, part] - nn(x_ref[:, pair], l_ref[pair, part])
            return 0

        lax.fori_loop(0, n, lead, 0)
        return 0

    lax.fori_loop(0, blocks // 2, back, 0)


def split(x):
    high = x.astype(jnp.bfloat16)
    return high, (x - high.astype(F32)).astype(jnp.bfloat16)


def place_rows(tile, t, rinv_ref, cinv_ref, load, less, out_ref):
    groups = range(0, out_ref.shape[-2], 8)
    index = [jnp.maximum(cinv_ref[t, g : g + 8], 0) for g in groups]
    live = [(cinv_ref[t, g : g + 8] >= 0).astype(F32) for g in groups]
    base = tile * TB

    def body(o, _):
        s = rinv_ref[t, base + o]
        weight = jnp.where(s >= 0, 1.0, 0.0)
        s = jnp.maximum(s, 0)
        for g, at, keep in zip(groups, index, live):
            x = jnp.take_along_axis(load(s, g), at, axis=1) * (keep * weight)
            out_ref[o, g : g + 8] = x if less is None else x + less(o, g)
        return 0

    lax.fori_loop(0, TB, body, 0, unroll=16)


def keep_kernel(
    at_ref, rinv_ref, kept_ref, sent_ref, cinv_ref, out_ref, early_ref, late_ref, thin_ref
):
    step, steps = pl.program_id(0), pl.num_programs(0)

    @pl.when(step < steps - 1)
    def _():
        early_ref[0] = sent_ref[0, 0, 0, :, 8:, :]

    @pl.when(step == steps - 1)
    def _():
        late_ref[0] = sent_ref[0, 0, 0, :, 8:, :]

    for v in range(2, 8):
        thin_ref[v - 2] = sent_ref[0, 0, 0, :, v, :]

    def load(s, g):
        return kept_ref[0, 0, 0, s, g : g + 8]

    place_rows(step, 0, rinv_ref, cinv_ref, load, None, out_ref.at[0, 0])


def finish_kernel(
    start, rinv_ref, got_ref, thin_ref, cinv_ref, kept_ref, r_ref, out_ref, first_ref
):
    @pl.when(pl.program_id(0) == 0)
    def _():
        first_ref[: 2 * TB, :] = jnp.zeros((2 * TB, TB), F32)

    for v in range(2, 8):
        first_ref[v * TB : (v + 1) * TB, :] = thin_ref[v - 2]

    def load(s, g):
        if g == 0:
            return first_ref[pl.ds(s, 8, stride=TB), :]
        return got_ref[0, s, g - 8 : g]

    def less(o, g):
        return kept_ref[0, 0, o, g : g + 8] - r_ref.at[0][pl.ds(g * TB + o, 8, stride=TB), :]

    tile = pl.program_id(0) + start
    place_rows(tile, 1, rinv_ref, cinv_ref, load, less, out_ref.at[0, 0])


def update_kernel(
    at_ref, g_ref, x_ref, y_ref, diag_ref, out_ref, wh_ref, wl_ref, xh_ref, xl_ref
):
    step = pl.program_id(0)
    tiles = out_ref.shape[0]

    @pl.when(step == 0)
    def _():
        xh_ref[...], xl_ref[...] = split(x_ref[...])

    for n in range(8):
        part = slice(n * TB, (n + 1) * TB)
        for m in range(4):
            q = lax.rem(at_ref[2] + n // 4 + 4 - m, 4)
            for v in range(2):
                high, low = split(g_ref[(n % 4) * 2 + n // 4, m, v])
                there = pl.ds(pl.multiple_of((4 * v + q) * TB, TB), TB)
                wh_ref[part, there] = high
                wl_ref[part, there] = low
    dims = (((1,), (1,)), ((), ()))
    dot = lambda a, b: lax.dot_general(a, b, dims, preferred_element_type=F32)
    for n in range(0, 8, 2):
        part = slice(n * TB, (n + 2) * TB)
        wh, wl = wh_ref[part, :], wl_ref[part, :]
        r = (dot(xl_ref[...], wh) + dot(xh_ref[...], wl)) + dot(xh_ref[...], wh)
        for i in range(2):
            for j in range(tiles):
                out_ref[j, (n + i) * TB : (n + i + 1) * TB, :] = r[
                    j * TB : (j + 1) * TB, i * TB : (i + 1) * TB
                ]
    sub = lax.broadcasted_iota(jnp.int32, (TB, TB), 0)
    lane = lax.broadcasted_iota(jnp.int32, (TB, TB), 1)
    here = pl.ds(pl.multiple_of(at_ref[1] * TB, TB), TB)
    out_ref[step, here, :] = out_ref[step, here, :] - jnp.where(
        sub == lane, diag_ref[pl.ds(step, 1), :], 0.0
    )

    @pl.when(step == 0)
    def _():
        for v in range(2):
            for j in range(tiles):
                out_ref[j, v * TB : (v + 1) * TB, :] = -y_ref[v, j * TB : (j + 1) * TB, :]


def inverse(relative):
    offsets = jnp.arange(TB, dtype=jnp.int32)
    hit = relative[..., None, :] == offsets[:, None]
    return jnp.max(jnp.where(hit, offsets, -1), axis=-1)


def on_device(child_update, child_map, parent_diag):
    cube, row, col = lax.axis_index("cube"), lax.axis_index("row"), lax.axis_index("col")
    grid, columns = 32, 4
    position = cube * 4 + row
    sibling = position // (grid // 2)
    block = child_update[0]
    tiles, cols = block.shape[1], block.shape[3]
    rows = tiles * TB
    trade = [(i, i ^ 16) for i in range(grid)]

    raw = jnp.transpose(block[:, :, :, :2, :], (0, 3, 1, 2, 4)).reshape(2, 2, rows, TB)
    got = lax.ppermute(raw, ("cube", "row"), trade)
    early = tiles - 1
    maps = jnp.stack(
        [
            lax.dynamic_index_in_dim(child_map, sibling, 0, keepdims=False),
            lax.dynamic_index_in_dim(child_map, 1 - sibling, 0, keepdims=False),
        ]
    )
    within = position % 16
    pair_tiles = (
        grid * jnp.arange(tiles, dtype=jnp.int32)[None, :]
        + 16 * jnp.arange(2, dtype=jnp.int32)[:, None]
        + within
    )
    pair_maps = jnp.swapaxes(
        lax.dynamic_index_in_dim(
            maps.reshape(2, tiles, 2, 16, TB), within, 3, keepdims=False
        ),
        1,
        2,
    )
    pair_maps = pair_maps - TB * pair_tiles[None, :, :, None]
    row_maps = lax.dynamic_index_in_dim(pair_maps, sibling, 1, keepdims=False)
    col_maps = lax.dynamic_index_in_dim(
        maps.reshape(2, cols, columns, TB), col, 2, keepdims=False
    )
    col_tiles = columns * jnp.arange(cols, dtype=jnp.int32) + col
    col_maps = col_maps - TB * col_tiles[None, :, None]
    pair_diag = jnp.swapaxes(
        lax.dynamic_index_in_dim(
            parent_diag.reshape(tiles, 2, 16, TB), within, 2, keepdims=False
        ),
        0,
        1,
    )
    diag = lax.dynamic_index_in_dim(pair_diag, sibling, 0, keepdims=False)
    meets = pair_tiles[:, None, :] == col_tiles[None, :2, None]
    panel_diag = jnp.where(meets[..., None], pair_diag[:, None], 0.0)

    row_inverse = inverse(row_maps).reshape(2, rows)
    solved = jnp.arange(cols) < 2
    col_inverse = jnp.where(solved[None, :, None], -1, inverse(col_maps))
    here = jnp.logical_and(row == col, jnp.logical_or(jnp.arange(tiles) > 0, cube >= 2))
    trailing_diag = jnp.where(here[:, None], diag, 0.0)
    crossed = (row // 2 != col // 2).astype(jnp.int32)
    at = jnp.stack([sibling, cube, 2 * crossed]).astype(jnp.int32)
    whole = jax.ShapeDtypeStruct((1, tiles, TB, cols, TB), F32)
    all_maps = pl.BlockSpec((2, cols, TB), lambda i, *_: (0, 0, 0))
    result, first, second, thin = pl.pallas_call(
        keep_kernel,
        out_shape=[
            whole,
            jax.ShapeDtypeStruct((early, TB, cols - 8, TB), F32),
            jax.ShapeDtypeStruct((tiles - early, TB, cols - 8, TB), F32),
            jax.ShapeDtypeStruct((6, rows, TB), F32),
        ],
        grid_spec=pltpu.PrefetchScalarGridSpec(
            num_scalar_prefetch=2,
            grid=(tiles,),
            in_specs=[
                pl.BlockSpec(
                    (1, 1, 1, TB, cols, TB), lambda i, at, _: (0, at[0], i, 0, 0, 0)
                ),
                pl.BlockSpec((1, 1, 1, TB, cols, TB), lambda i, at, _: (0, 1 - at[0], i, 0, 0, 0)),
                all_maps,
            ],
            out_specs=[
                pl.BlockSpec((1, 1, TB, cols, TB), lambda i, *_: (0, i, 0, 0, 0)),
                pl.BlockSpec(
                    (1, TB, cols - 8, TB), lambda i, *_: (jnp.minimum(i, early - 1), 0, 0, 0)
                ),
                pl.BlockSpec((1, TB, cols - 8, TB), lambda i, *_: (0, 0, 0, 0)),
                pl.BlockSpec((6, TB, TB), lambda i, *_: (0, i, 0)),
            ],
        ),
    )(at, row_inverse, child_update, child_update, col_inverse)
    first, second, thin, got = lax.optimization_barrier((first, second, thin, got))
    arrived = []
    for part in (thin, first, second):
        arrived.append(lax.ppermute(part, ("cube", "row"), trade))

    strip = jax.ShapeDtypeStruct((2, rows, TB), F32)
    own, even, odd, piece = pl.pallas_call(
        place_kernel,
        out_shape=[strip, strip, strip, jax.ShapeDtypeStruct((2, TB, TB), F32)],
        in_specs=[SMEM] + [VMEM] * 5,
        out_specs=[VMEM] * 4,
        scratch_shapes=[pltpu.VMEM((4, 2, rows, TB), F32)],
    )(
        jnp.stack([sibling, col % 2]).astype(jnp.int32),
        raw, got, pair_maps, col_maps[:, :2], panel_diag,
    )

    pivot, turned = pl.pallas_call(
        pivot_kernel,
        out_shape=[
            jax.ShapeDtypeStruct((4, 8, 2, TB, TB), F32),
            jax.ShapeDtypeStruct((4, 2, rows, TB), F32),
        ],
        in_specs=[VMEM, ANY, ANY],
        out_specs=[VMEM, ANY],
        scratch_shapes=[
            pltpu.SemaphoreType.DMA((33,)),
            pltpu.SemaphoreType.DMA((4, 8)),
            pltpu.SemaphoreType.DMA,
            pltpu.SemaphoreType.DMA((4,)),
            pltpu.SemaphoreType.DMA((4,)),
            pltpu.VMEM((2, rows, TB), F32),
            pltpu.SemaphoreType.DMA,
            pltpu.SemaphoreType.DMA,
        ],
        compiler_params=pltpu.CompilerParams(collective_id=0, has_side_effects=True),
    )(piece, even, odd)

    groups = [
        [(s * 4 + z) * 4 + half * 2 + core for z in range(4) for core in range(2)]
        for s in range(2)
        for half in range(2)
    ]
    others = lax.all_gather(turned, ("cube", "row"), axis=0, axis_index_groups=groups)
    own, pivot = lax.optimization_barrier((own, pivot))
    strips = []
    for hop in (1, 3, 2):
        strips.append(lax.ppermute(own, "col", [(c, (c + hop) % 4) for c in range(4)]))

    lower, inverses = pl.pallas_call(
        factor_kernel,
        out_shape=[jax.ShapeDtypeStruct((K, K), F32), jax.ShapeDtypeStruct((K // TB, TB, TB), F32)],
        in_specs=[VMEM],
        out_specs=[VMEM, VMEM],
        scratch_shapes=[pltpu.VMEM((TB, TB), F32)],
    )(pivot)
    y, x = pl.pallas_call(
        solve_kernel,
        out_shape=[
            jax.ShapeDtypeStruct((2, rows, TB), F32),
            jax.ShapeDtypeStruct((rows, K), F32),
        ],
        in_specs=[SMEM] + [VMEM] * 6,
        out_specs=[VMEM, VMEM],
        scratch_shapes=[pltpu.VMEM((rows, K), F32)],
    )(col.reshape(1), lower, inverses, own, *strips)

    update = pl.pallas_call(
        update_kernel,
        out_shape=jax.ShapeDtypeStruct((tiles, cols * TB, TB), F32),
        grid_spec=pltpu.PrefetchScalarGridSpec(
            num_scalar_prefetch=1,
            grid=(cols // 8,),
            in_specs=[
                pl.BlockSpec((8, 4, 2, TB, TB), lambda i, *_: (0, 0, 0, i, 0)),
                VMEM,
                VMEM,
                VMEM,
            ],
            out_specs=pl.BlockSpec((tiles, 8 * TB, TB), lambda i, *_: (0, i, 0)),
            scratch_shapes=[
                pltpu.VMEM((8 * TB, K), jnp.bfloat16),
                pltpu.VMEM((8 * TB, K), jnp.bfloat16),
                pltpu.VMEM((rows, K), jnp.bfloat16),
                pltpu.VMEM((rows, K), jnp.bfloat16),
            ],
        ),
    )(at, others, x, y, trailing_diag)
    thin, *arrived = arrived
    for start, part in zip((0, early), arrived):
        block_at = lambda i, *_, start=start: (0, i + start, 0, 0, 0)
        result = pl.pallas_call(
            functools.partial(finish_kernel, start),
            out_shape=whole,
            grid_spec=pltpu.PrefetchScalarGridSpec(
                num_scalar_prefetch=1,
                grid=(part.shape[0],),
                in_specs=[
                    pl.BlockSpec((1, TB, cols - 8, TB), lambda i, *_: (i, 0, 0, 0)),
                    pl.BlockSpec((6, TB, TB), lambda i, *_, start=start: (0, i + start, 0)),
                    all_maps,
                    pl.BlockSpec((1, 1, TB, cols, TB), block_at),
                    pl.BlockSpec((1, cols * TB, TB), lambda i, *_, start=start: (i + start, 0, 0)),
                ],
                out_specs=pl.BlockSpec((1, 1, TB, cols, TB), block_at),
                scratch_shapes=[pltpu.VMEM((8 * TB, TB), F32)],
            ),
            input_output_aliases={4: 0},
        )(row_inverse, part, thin, col_inverse, result, update)
    return result


def solution(mesh):
    return jax.shard_map(
        on_device,
        mesh=mesh,
        in_specs=(P(("cube", "row"), None, None, None, "col", None), P(), P()),
        out_specs=P(("cube", "row"), None, None, "col", None),
        check_vma=False,
    )
```

```python
import jax
import jax.numpy as jnp
from jax import lax
from jax.experimental import pallas as pl
from jax.experimental.pallas import tpu as pltpu
from jax.sharding import PartitionSpec as P


K = 1024
TB = 128
HI = lax.Precision.HIGHEST
F32 = jnp.float32
MESH = pl.DeviceIdType.MESH
VMEM = pl.BlockSpec(memory_space=pltpu.VMEM)
ANY = pl.BlockSpec(memory_space=pl.ANY)
SMEM = pl.BlockSpec(memory_space=pltpu.SMEM)


def nt(a, b):
    return lax.dot_general(
        a, b, (((1,), (1,)), ((), ())), precision=HI, preferred_element_type=F32
    )


def nn(a, b):
    return lax.dot_general(
        a, b, (((1,), (0,)), ((), ())), precision=HI, preferred_element_type=F32
    )


def place_kernel(
    pick_ref, raw_ref, got_ref, rmap_ref, cmap_ref, diag_ref, own_ref, even_ref, odd_ref, piece_ref, hold_ref
):
    sub = lax.broadcasted_iota(jnp.int32, (TB, TB), 0)
    lane = lax.broadcasted_iota(jnp.int32, (TB, TB), 1)
    tiles = rmap_ref.shape[2]
    for v in range(2):
        for half in range(2):
            cols = [
                nt(ref[half, v], (sub == cmap_ref[t, v : v + 1, :]).astype(F32))
                for t, ref in enumerate((raw_ref, got_ref))
            ]
            for j in range(tiles):
                rows = slice(j * TB, (j + 1) * TB)
                total = jnp.where(sub == lane, diag_ref[half, v, j : j + 1, :], 0.0)
                for t in range(2):
                    hot = (sub == rmap_ref[t, half, j : j + 1, :]).astype(F32)
                    total += nn(hot, cols[t][rows, :])
                if half == 0 and j == 0:
                    piece_ref[v] = total
                hold_ref[jnp.where(pick_ref[0] == half, 0, 3), v, rows, :] = total
                hold_ref[jnp.where(pick_ref[1] == half, 1, 2), v, rows, :] = total
    for n, out_ref in enumerate((own_ref, even_ref, odd_ref)):
        out_ref[...] = hold_ref[n]


def pivot_kernel(
    piece_ref, even_ref, odd_ref, out_ref, turned_ref, send, recv, local, send_turned, recv_turned
):
    cube, row, col = lax.axis_index("cube"), lax.axis_index("row"), lax.axis_index("col")
    z = lax.rem(cube, 4)
    core, half = lax.rem(row, 2), row // 2
    at = lambda cu, ro, co: {"cube": cu, "row": ro, "col": co}
    mates = [at((cube - z) + lax.rem(z + d, 4), row, col) for d in (1, 2, 3)]
    across = at(lax.rem(cube + 4, 8), lax.rem(row + 2, 4), col)
    up, down = lax.rem(col + 1, 4), lax.rem(col + 3, 4)
    sides = [at(cube, row, up), at(cube, row, down)]
    other = at(cube, row + 1 - 2 * core, col)
    barrier = pltpu.get_barrier_semaphore()
    for peer in mates + [across] + sides + [other]:
        pl.semaphore_signal(barrier, inc=1, device_id=peer, device_id_type=MESH)
    side = cube // 4
    alone = row == col

    def to_kind(kind):
        far, h = kind // 2, lax.rem(kind, 2)
        x = lax.rem(side + far, 2) * 4 + z
        return at(x, lax.rem(half + far, 2) * 2 + h, row)

    crossed = lax.rem(half + col // 2, 2)
    sender = lambda y: at(
        lax.rem(side + crossed, 2) * 4 + z, col, y
    )
    for y in range(4):

        @pl.when(jnp.logical_not(jnp.logical_and(alone, col == y)))
        def _():
            pl.semaphore_signal(barrier, inc=1, device_id=sender(y), device_id_type=MESH)

    @pl.when(alone)
    def _():
        pl.semaphore_wait(barrier, 10)

    @pl.when(jnp.logical_not(alone))
    def _():
        pl.semaphore_wait(barrier, 11)

    def quarter(m):
        return pltpu.make_async_remote_copy(
            src_ref=(odd_ref if m % 2 else even_ref),
            dst_ref=turned_ref.at[m],
            send_sem=send_turned.at[m],
            recv_sem=recv_turned.at[m],
            device_id=to_kind(lax.rem(m + col, 4)),
            device_id_type=MESH,
        )

    def stays(m):
        return jnp.logical_and(alone, lax.rem(m + col, 4) == core)

    def keep_quarter(m):
        return pltpu.make_async_copy(
            odd_ref if m % 2 else even_ref, turned_ref.at[m], send_turned.at[m]
        )

    def copy(c, p, slot, peer, width):
        part = out_ref.at[c, p, pl.ds(0, width)]
        return pltpu.make_async_remote_copy(
            src_ref=part,
            dst_ref=part,
            send_sem=send.at[slot],
            recv_sem=recv.at[c, p],
            device_id=peer,
            device_id_type=MESH,
        )

    for zz in range(2):
        mine = zz * 4 + row

        @pl.when(z == zz)
        def _():
            part = pl.ds(0, zz + 1)
            own = pltpu.make_async_copy(piece_ref.at[part], out_ref.at[col, mine, part], local)
            own.start()
            own.wait()
            for i, peer in enumerate(mates):
                copy(col, mine, i, peer, zz + 1).start()

    for zz in range(2):
        p = zz * 4 + row
        n = zz

        @pl.when(z != zz)
        def _():
            copy(col, p, 0, other, zz + 1).wait_recv()

        copy(col, p, 3 + zz, across, zz + 1).start()
        copy(col, p, 5 + n, sides[0], zz + 1).start()
        copy(col, p, 7 + n, sides[1], zz + 1).start()
        copy(col, p, 9 + n, other, zz + 1).start()
    opposite = lax.rem(row + 2, 4)
    for zz in range(2):
        p = zz * 4 + opposite
        n = zz
        copy(col, p, 0, other, zz + 1).wait_recv()
        copy(col, p, 11 + n, sides[0], zz + 1).start()
        copy(col, p, 13 + n, sides[1], zz + 1).start()
        copy(col, p, 15 + n, other, zz + 1).start()
    for m in range(4):

        @pl.when(stays(m))
        def _():
            keep_quarter(m).start()

        @pl.when(jnp.logical_not(stays(m)))
        def _():
            quarter(m).start()

    for i, who in enumerate((row, opposite)):
        for zz in range(2):
            p = zz * 4 + who
            n = i * 2 + zz
            copy(down, p, 0, other, zz + 1).wait_recv()
            copy(down, p, 17 + n, other, zz + 1).start()

            @pl.when(core == 0)
            def _():
                copy(down, p, 21 + n, sides[0], zz + 1).start()

            copy(up, p, 0, other, zz + 1).wait_recv()
            copy(up, p, 25 + n, other, zz + 1).start()

            @pl.when(core == 1)
            def _():
                copy(up, p, 21 + n, sides[1], zz + 1).start()

    far = lax.rem(col + 2, 4)
    for i, who in enumerate((row, opposite)):
        for zz in range(2):
            p = zz * 4 + who
            copy(far, p, 0, other, zz + 1).wait_recv()
            copy(far, p, 29 + i * 2 + zz, other, zz + 1).start()
    for c in range(4):
        for zz in range(2):
            for hh in range(2):
                copy(c, zz * 4 + hh * 2 + 1 - core, 0, other, zz + 1).wait_recv()

    for zz in range(2):

        @pl.when(z == zz)
        def _():
            for i in range(3):
                copy(col, row, i, other, zz + 1).wait_send()

        for i in (3, 5, 7, 9, 11, 13, 15, 17, 19, 21, 23, 25, 27, 29, 31):
            copy(col, row, i + zz, other, zz + 1).wait_send()

    for m in range(4):

        @pl.when(stays(m))
        def _():
            keep_quarter(m).wait()

        @pl.when(jnp.logical_not(stays(m)))
        def _():
            quarter(m).wait()


def leaf(d_ref, li_ref):
    a_rows = [d_ref[8 * g : 8 * g + 8, :] for g in range(16)]
    lane = lax.broadcasted_iota(jnp.int32, (8, TB), 1)
    sub = lax.broadcasted_iota(jnp.int32, (8, TB), 0)
    b_rows = [(lane == sub + 8 * g).astype(F32) for g in range(16)]
    wide = lambda x: jnp.broadcast_to(x, (8, TB))
    for g0 in range(16):
        j = 8 * g0
        c = [wide(a_rows[g0][:, j + q : j + q + 1]) for q in range(8)]
        e = [[wide(c[q][i : i + 1, :]) if i >= q else None for q in range(8)] for i in range(8)]
        a = [wide(a_rows[g0][q : q + 1, :]) for q in range(8)]
        b = [wide(b_rows[g0][q : q + 1, :]) for q in range(8)]
        more = g0 + 1 < 16
        if more:
            m = [wide(a_rows[g0 + 1][:, j + q : j + q + 1]) for q in range(8)]
        s, t = [None] * 8, [None] * 8
        low = [[None] * 8 for _ in range(8)]
        for q in range(8):
            inv = 1.0 / e[q][q]
            s[q], t[q] = a[q] * inv, b[q] * inv
            for i in range(q + 1, 8):
                low[i][q] = e[i][q] * inv
            for i in range(q + 1, 8):
                for p in range(q + 1, i + 1):
                    e[i][p] = e[i][p] - low[i][q] * e[p][q]
            for i in range(q + 1, 8):
                a[i] = a[i] - low[i][q] * a[q]
                b[i] = b[i] - low[i][q] * b[q]
                if more:
                    m[i] = m[i] - low[i][q] * m[q]
            if more:
                a_rows[g0 + 1] = a_rows[g0 + 1] - m[q] * s[q]
                b_rows[g0 + 1] = b_rows[g0 + 1] - m[q] * t[q]
            li_ref[j + q : j + q + 1, :] = (b[q] * lax.rsqrt(e[q][q]))[0:1, :]
        if g0 + 2 < 16:
            for q in range(7, -1, -1):
                for i in range(q + 1, 8):
                    s[q] = s[q] - low[i][q] * s[i]
                    t[q] = t[q] - low[i][q] * t[i]
            for g in range(g0 + 2, 16):
                m = [wide(a_rows[g][:, j + q : j + q + 1]) for q in range(8)]
                da, db = m[0] * s[0], m[0] * t[0]
                for q in range(1, 8):
                    da, db = da + m[q] * s[q], db + m[q] * t[q]
                a_rows[g] = a_rows[g] - da
                b_rows[g] = b_rows[g] - db


def factor_kernel(s_ref, m_ref, li_ref, d_ref):
    blocks, pair_width = K // TB, 2 * TB
    for c in range(4):
        for v in range(2):
            u = 4 * v + c
            for p in range(u, blocks):
                m_ref[p * TB : (p + 1) * TB, u * TB : (u + 1) * TB] = s_ref[c, p, v]

    def step(k, _):
        here = pl.ds(pl.multiple_of(k * TB, TB), TB)
        d_ref[...] = m_ref[here, here]
        leaf(d_ref, li_ref.at[k])
        m_ref[:, here] = nt(m_ref[:, here], li_ref[k])

        @pl.when(lax.rem(k, 2) == 0)
        def _():
            after = pl.ds(pl.multiple_of((k + 1) * TB, TB), TB)
            m_ref[:, after] = m_ref[:, after] - nt(m_ref[:, here], m_ref[after, here])

        @pl.when(lax.rem(k, 2) == 1)
        def _():
            pair = pl.ds(pl.multiple_of((k - 1) * TB, TB), pair_width)

            def trail(i, _):
                part = pl.ds(pl.multiple_of(i * pair_width, pair_width), pair_width)
                m_ref[:, part] = m_ref[:, part] - nt(m_ref[:, pair], m_ref[part, pair])
                return 0

            lax.fori_loop((k + 1) // 2, blocks // 2, trail, 0)

        return 0

    lax.fori_loop(0, blocks, step, 0)


def solve_kernel(col_ref, l_ref, li_ref, own_ref, low_ref, high_ref, far_ref, y_ref, x_ref, m_ref):
    blocks, pair_width = K // TB, 2 * TB
    col = col_ref[0]
    for part, ref in enumerate((own_ref, high_ref, far_ref, low_ref)):
        for v in range(2):
            u = 4 * v + lax.rem(col + part, 4)
            m_ref[:, pl.ds(pl.multiple_of(u * TB, TB), TB)] = ref[v]

    def places(n):
        at = n * pair_width
        return (
            pl.ds(pl.multiple_of(at, TB), TB),
            pl.ds(pl.multiple_of(at + TB, TB), TB),
            pl.ds(pl.multiple_of(at, pair_width), pair_width),
        )

    def forth(n, _):
        first, last, pair = places(n)
        m_ref[:, first] = nt(m_ref[:, first], li_ref[2 * n])
        rest = m_ref[:, last] - nt(m_ref[:, first], l_ref[last, first])
        m_ref[:, last] = nt(rest, li_ref[2 * n + 1])

        def trail(i, _):
            part = places(i)[2]
            m_ref[:, part] = m_ref[:, part] - nt(m_ref[:, pair], l_ref[part, pair])
            return 0

        lax.fori_loop(n + 1, blocks // 2, trail, 0)
        return 0

    lax.fori_loop(0, blocks // 2, forth, 0)
    for v in range(2):
        y_ref[v] = m_ref[:, pl.ds(pl.multiple_of((4 * v + col) * TB, TB), TB)]

    def back(i, _):
        n = blocks // 2 - 1 - i
        first, last, pair = places(n)
        x_ref[:, last] = nn(m_ref[:, last], li_ref[2 * n + 1])
        rest = m_ref[:, first] - nn(x_ref[:, last], l_ref[last, first])
        x_ref[:, first] = nn(rest, li_ref[2 * n])

        def lead(j, _):
            part = places(j)[2]
            m_ref[:, part] = m_ref[:, part] - nn(x_ref[:, pair], l_ref[pair, part])
            return 0

        lax.fori_loop(0, n, lead, 0)
        return 0

    lax.fori_loop(0, blocks // 2, back, 0)


def split(x):
    high = x.astype(jnp.bfloat16)
    return high, (x - high.astype(F32)).astype(jnp.bfloat16)


def place_rows(tile, t, rinv_ref, cinv_ref, load, less, out_ref):
    groups = range(0, out_ref.shape[-2], 8)
    index = [jnp.maximum(cinv_ref[t, g : g + 8], 0) for g in groups]
    live = [(cinv_ref[t, g : g + 8] >= 0).astype(F32) for g in groups]
    base = tile * TB

    def body(o, _):
        s = rinv_ref[t, base + o]
        weight = jnp.where(s >= 0, 1.0, 0.0)
        s = jnp.maximum(s, 0)
        for g, at, keep in zip(groups, index, live):
            x = jnp.take_along_axis(load(s, g), at, axis=1) * (keep * weight)
            out_ref[o, g : g + 8] = x if less is None else x + less(o, g)
        return 0

    lax.fori_loop(0, TB, body, 0, unroll=16)


def keep_kernel(
    at_ref, rinv_ref, kept_ref, sent_ref, cinv_ref, out_ref, main_ref, thin_ref
):
    main_ref[0] = sent_ref[0, 0, 0, :, 8:, :]
    for v in range(2, 8):
        thin_ref[v - 2] = sent_ref[0, 0, 0, :, v, :]

    def load(s, g):
        return kept_ref[0, 0, 0, s, g : g + 8]

    place_rows(pl.program_id(0), 0, rinv_ref, cinv_ref, load, None, out_ref.at[0, 0])


def finish_kernel(
    rinv_ref, got_ref, thin_ref, cinv_ref, kept_ref, r_ref, out_ref, first_ref
):
    @pl.when(pl.program_id(0) == 0)
    def _():
        first_ref[: 2 * TB, :] = jnp.zeros((2 * TB, TB), F32)

    for v in range(2, 8):
        first_ref[v * TB : (v + 1) * TB, :] = thin_ref[v - 2]

    def load(s, g):
        if g == 0:
            return first_ref[pl.ds(s, 8, stride=TB), :]
        return got_ref[0, s, g - 8 : g]

    def less(o, g):
        return kept_ref[0, 0, o, g : g + 8] - r_ref.at[0][pl.ds(g * TB + o, 8, stride=TB), :]

    place_rows(pl.program_id(0), 1, rinv_ref, cinv_ref, load, less, out_ref.at[0, 0])


def update_kernel(
    at_ref, g_ref, x_ref, y_ref, diag_ref, out_ref, wh_ref, wl_ref, xh_ref, xl_ref
):
    step = pl.program_id(0)
    tiles = out_ref.shape[0]

    @pl.when(step == 0)
    def _():
        xh_ref[...], xl_ref[...] = split(x_ref[...])

    for n in range(8):
        part = slice(n * TB, (n + 1) * TB)
        for m in range(4):
            q = lax.rem(at_ref[2] + n // 4 + 4 - m, 4)
            for v in range(2):
                high, low = split(g_ref[(n % 4) * 2 + n // 4, m, v])
                there = pl.ds(pl.multiple_of((4 * v + q) * TB, TB), TB)
                wh_ref[part, there] = high
                wl_ref[part, there] = low
    dims = (((1,), (1,)), ((), ()))
    dot = lambda a, b: lax.dot_general(a, b, dims, preferred_element_type=F32)
    for n in range(0, 8, 2):
        part = slice(n * TB, (n + 2) * TB)
        wh, wl = wh_ref[part, :], wl_ref[part, :]
        r = (dot(xl_ref[...], wh) + dot(xh_ref[...], wl)) + dot(xh_ref[...], wh)
        for i in range(2):
            for j in range(tiles):
                out_ref[j, (n + i) * TB : (n + i + 1) * TB, :] = r[
                    j * TB : (j + 1) * TB, i * TB : (i + 1) * TB
                ]
    sub = lax.broadcasted_iota(jnp.int32, (TB, TB), 0)
    lane = lax.broadcasted_iota(jnp.int32, (TB, TB), 1)
    here = pl.ds(pl.multiple_of(at_ref[1] * TB, TB), TB)
    out_ref[step, here, :] = out_ref[step, here, :] - jnp.where(
        sub == lane, diag_ref[pl.ds(step, 1), :], 0.0
    )

    @pl.when(step == 0)
    def _():
        for v in range(2):
            for j in range(tiles):
                out_ref[j, v * TB : (v + 1) * TB, :] = -y_ref[v, j * TB : (j + 1) * TB, :]


def inverse(relative):
    offsets = jnp.arange(TB, dtype=jnp.int32)
    hit = relative[..., None, :] == offsets[:, None]
    return jnp.max(jnp.where(hit, offsets, -1), axis=-1)


def on_device(child_update, child_map, parent_diag):
    cube, row, col = lax.axis_index("cube"), lax.axis_index("row"), lax.axis_index("col")
    grid, columns = 32, 4
    position = cube * 4 + row
    sibling = position // (grid // 2)
    block = child_update[0]
    tiles, cols = block.shape[1], block.shape[3]
    rows = tiles * TB
    trade = [(i, i ^ 16) for i in range(grid)]

    raw = jnp.transpose(block[:, :, :, :2, :], (0, 3, 1, 2, 4)).reshape(2, 2, rows, TB)
    got = lax.ppermute(raw, ("cube", "row"), trade)
    maps = jnp.stack(
        [
            lax.dynamic_index_in_dim(child_map, sibling, 0, keepdims=False),
            lax.dynamic_index_in_dim(child_map, 1 - sibling, 0, keepdims=False),
        ]
    )
    within = position % 16
    pair_tiles = (
        grid * jnp.arange(tiles, dtype=jnp.int32)[None, :]
        + 16 * jnp.arange(2, dtype=jnp.int32)[:, None]
        + within
    )
    pair_maps = jnp.swapaxes(
        lax.dynamic_index_in_dim(
            maps.reshape(2, tiles, 2, 16, TB), within, 3, keepdims=False
        ),
        1,
        2,
    )
    pair_maps = pair_maps - TB * pair_tiles[None, :, :, None]
    row_maps = lax.dynamic_index_in_dim(pair_maps, sibling, 1, keepdims=False)
    col_maps = lax.dynamic_index_in_dim(
        maps.reshape(2, cols, columns, TB), col, 2, keepdims=False
    )
    col_tiles = columns * jnp.arange(cols, dtype=jnp.int32) + col
    col_maps = col_maps - TB * col_tiles[None, :, None]
    pair_diag = jnp.swapaxes(
        lax.dynamic_index_in_dim(
            parent_diag.reshape(tiles, 2, 16, TB), within, 2, keepdims=False
        ),
        0,
        1,
    )
    diag = lax.dynamic_index_in_dim(pair_diag, sibling, 0, keepdims=False)
    meets = pair_tiles[:, None, :] == col_tiles[None, :2, None]
    panel_diag = jnp.where(meets[..., None], pair_diag[:, None], 0.0)

    row_inverse = inverse(row_maps).reshape(2, rows)
    solved = jnp.arange(cols) < 2
    col_inverse = jnp.where(solved[None, :, None], -1, inverse(col_maps))
    here = jnp.logical_and(row == col, jnp.logical_or(jnp.arange(tiles) > 0, cube >= 2))
    trailing_diag = jnp.where(here[:, None], diag, 0.0)
    crossed = (row // 2 != col // 2).astype(jnp.int32)
    at = jnp.stack([sibling, cube, 2 * crossed]).astype(jnp.int32)
    whole = jax.ShapeDtypeStruct((1, tiles, TB, cols, TB), F32)
    all_maps = pl.BlockSpec((2, cols, TB), lambda i, *_: (0, 0, 0))
    result, main, thin = pl.pallas_call(
        keep_kernel,
        out_shape=[
            whole,
            jax.ShapeDtypeStruct((tiles, TB, cols - 8, TB), F32),
            jax.ShapeDtypeStruct((6, rows, TB), F32),
        ],
        grid_spec=pltpu.PrefetchScalarGridSpec(
            num_scalar_prefetch=2,
            grid=(tiles,),
            in_specs=[
                pl.BlockSpec(
                    (1, 1, 1, TB, cols, TB), lambda i, at, _: (0, at[0], i, 0, 0, 0)
                ),
                pl.BlockSpec((1, 1, 1, TB, cols, TB), lambda i, at, _: (0, 1 - at[0], i, 0, 0, 0)),
                all_maps,
            ],
            out_specs=[
                pl.BlockSpec((1, 1, TB, cols, TB), lambda i, *_: (0, i, 0, 0, 0)),
                pl.BlockSpec((1, TB, cols - 8, TB), lambda i, *_: (i, 0, 0, 0)),
                pl.BlockSpec((6, TB, TB), lambda i, *_: (0, i, 0)),
            ],
        ),
    )(at, row_inverse, child_update, child_update, col_inverse)
    main, thin, got = lax.optimization_barrier((main, thin, got))
    arrived = []
    for part in (thin, main):
        arrived.append(lax.ppermute(part, ("cube", "row"), trade))

    strip = jax.ShapeDtypeStruct((2, rows, TB), F32)
    own, even, odd, piece = pl.pallas_call(
        place_kernel,
        out_shape=[strip, strip, strip, jax.ShapeDtypeStruct((2, TB, TB), F32)],
        in_specs=[SMEM] + [VMEM] * 5,
        out_specs=[VMEM] * 4,
        scratch_shapes=[pltpu.VMEM((4, 2, rows, TB), F32)],
    )(
        jnp.stack([sibling, col % 2]).astype(jnp.int32),
        raw, got, pair_maps, col_maps[:, :2], panel_diag,
    )

    pivot, turned = pl.pallas_call(
        pivot_kernel,
        out_shape=[
            jax.ShapeDtypeStruct((4, 8, 2, TB, TB), F32),
            jax.ShapeDtypeStruct((4, 2, rows, TB), F32),
        ],
        in_specs=[VMEM, ANY, ANY],
        out_specs=[VMEM, ANY],
        scratch_shapes=[
            pltpu.SemaphoreType.DMA((33,)),
            pltpu.SemaphoreType.DMA((4, 8)),
            pltpu.SemaphoreType.DMA,
            pltpu.SemaphoreType.DMA((4,)),
            pltpu.SemaphoreType.DMA((4,)),
        ],
        compiler_params=pltpu.CompilerParams(collective_id=0, has_side_effects=True),
    )(piece, even, odd)

    groups = [
        [(s * 4 + z) * 4 + half * 2 + core for z in range(4) for core in range(2)]
        for s in range(2)
        for half in range(2)
    ]
    others = lax.all_gather(turned, ("cube", "row"), axis=0, axis_index_groups=groups)
    own, pivot = lax.optimization_barrier((own, pivot))
    strips = []
    for hop in (1, 3, 2):
        strips.append(lax.ppermute(own, "col", [(c, (c + hop) % 4) for c in range(4)]))

    lower, inverses = pl.pallas_call(
        factor_kernel,
        out_shape=[jax.ShapeDtypeStruct((K, K), F32), jax.ShapeDtypeStruct((K // TB, TB, TB), F32)],
        in_specs=[VMEM],
        out_specs=[VMEM, VMEM],
        scratch_shapes=[pltpu.VMEM((TB, TB), F32)],
    )(pivot)
    y, x = pl.pallas_call(
        solve_kernel,
        out_shape=[
            jax.ShapeDtypeStruct((2, rows, TB), F32),
            jax.ShapeDtypeStruct((rows, K), F32),
        ],
        in_specs=[SMEM] + [VMEM] * 6,
        out_specs=[VMEM, VMEM],
        scratch_shapes=[pltpu.VMEM((rows, K), F32)],
    )(col.reshape(1), lower, inverses, own, *strips)

    update = pl.pallas_call(
        update_kernel,
        out_shape=jax.ShapeDtypeStruct((tiles, cols * TB, TB), F32),
        grid_spec=pltpu.PrefetchScalarGridSpec(
            num_scalar_prefetch=1,
            grid=(cols // 8,),
            in_specs=[
                pl.BlockSpec((8, 4, 2, TB, TB), lambda i, *_: (0, 0, 0, i, 0)),
                VMEM,
                VMEM,
                VMEM,
            ],
            out_specs=pl.BlockSpec((tiles, 8 * TB, TB), lambda i, *_: (0, i, 0)),
            scratch_shapes=[
                pltpu.VMEM((8 * TB, K), jnp.bfloat16),
                pltpu.VMEM((8 * TB, K), jnp.bfloat16),
                pltpu.VMEM((rows, K), jnp.bfloat16),
                pltpu.VMEM((rows, K), jnp.bfloat16),
            ],
        ),
    )(at, others, x, y, trailing_diag)
    own_block = pl.BlockSpec((1, 1, TB, cols, TB), lambda i, *_: (0, i, 0, 0, 0))
    return pl.pallas_call(
        finish_kernel,
        out_shape=whole,
        grid_spec=pltpu.PrefetchScalarGridSpec(
            num_scalar_prefetch=1,
            grid=(tiles,),
            in_specs=[
                pl.BlockSpec((1, TB, cols - 8, TB), lambda i, *_: (i, 0, 0, 0)),
                pl.BlockSpec((6, TB, TB), lambda i, *_: (0, i, 0)),
                all_maps,
                own_block,
                pl.BlockSpec((1, cols * TB, TB), lambda i, *_: (i, 0, 0)),
            ],
            out_specs=own_block,
            scratch_shapes=[pltpu.VMEM((8 * TB, TB), F32)],
        ),
    )(row_inverse, arrived[1], arrived[0], col_inverse, result, update)


def solution(mesh):
    return jax.shard_map(
        on_device,
        mesh=mesh,
        in_specs=(P(("cube", "row"), None, None, None, "col", None), P(), P()),
        out_specs=P(("cube", "row"), None, None, "col", None),
        check_vma=False,
    )
```

```python
import jax
import jax.numpy as jnp
from jax import lax
from jax.experimental import pallas as pl
from jax.experimental.pallas import tpu as pltpu
from jax.sharding import PartitionSpec as P


K = 1024
TB = 128
HI = lax.Precision.HIGHEST
F32 = jnp.float32
MESH = pl.DeviceIdType.MESH
VMEM = pl.BlockSpec(memory_space=pltpu.VMEM)
ANY = pl.BlockSpec(memory_space=pl.ANY)
SMEM = pl.BlockSpec(memory_space=pltpu.SMEM)


def nt(a, b):
    return lax.dot_general(
        a, b, (((1,), (1,)), ((), ())), precision=HI, preferred_element_type=F32
    )


def nn(a, b):
    return lax.dot_general(
        a, b, (((1,), (0,)), ((), ())), precision=HI, preferred_element_type=F32
    )


def place_kernel(
    pick_ref, raw_ref, got_ref, rmap_ref, cmap_ref, diag_ref, own_ref, even_ref, odd_ref, piece_ref, hold_ref
):
    sub = lax.broadcasted_iota(jnp.int32, (TB, TB), 0)
    lane = lax.broadcasted_iota(jnp.int32, (TB, TB), 1)
    tiles = rmap_ref.shape[2]
    for v in range(2):
        for half in range(2):
            cols = [
                nt(ref[half, v], (sub == cmap_ref[t, v : v + 1, :]).astype(F32))
                for t, ref in enumerate((raw_ref, got_ref))
            ]
            for j in range(tiles):
                rows = slice(j * TB, (j + 1) * TB)
                total = jnp.where(sub == lane, diag_ref[half, v, j : j + 1, :], 0.0)
                for t in range(2):
                    hot = (sub == rmap_ref[t, half, j : j + 1, :]).astype(F32)
                    total += nn(hot, cols[t][rows, :])
                if half == 0 and j == 0:
                    piece_ref[v] = total
                hold_ref[jnp.where(pick_ref[0] == half, 0, 3), v, rows, :] = total
                hold_ref[jnp.where(pick_ref[1] == half, 1, 2), v, rows, :] = total
    for n, out_ref in enumerate((own_ref, even_ref, odd_ref)):
        out_ref[...] = hold_ref[n]


def pivot_kernel(
    piece_ref, even_ref, odd_ref, out_ref, turned_ref, send, recv, local, send_turned, recv_turned
):
    cube, row, col = lax.axis_index("cube"), lax.axis_index("row"), lax.axis_index("col")
    z = lax.rem(cube, 4)
    core, half = lax.rem(row, 2), row // 2
    at = lambda cu, ro, co: {"cube": cu, "row": ro, "col": co}
    mates = [at((cube - z) + lax.rem(z + d, 4), row, col) for d in (1, 2, 3)]
    across = at(lax.rem(cube + 4, 8), lax.rem(row + 2, 4), col)
    up, down = lax.rem(col + 1, 4), lax.rem(col + 3, 4)
    sides = [at(cube, row, up), at(cube, row, down)]
    other = at(cube, row + 1 - 2 * core, col)
    barrier = pltpu.get_barrier_semaphore()
    for peer in mates + [across] + sides + [other]:
        pl.semaphore_signal(barrier, inc=1, device_id=peer, device_id_type=MESH)
    side = cube // 4
    alone = row == col

    def to_kind(kind):
        far, h = kind // 2, lax.rem(kind, 2)
        x = lax.rem(side + far, 2) * 4 + z
        return at(x, lax.rem(half + far, 2) * 2 + h, row)

    crossed = lax.rem(half + col // 2, 2)
    sender = lambda y: at(
        lax.rem(side + crossed, 2) * 4 + z, col, y
    )
    for y in range(4):

        @pl.when(jnp.logical_not(jnp.logical_and(alone, col == y)))
        def _():
            pl.semaphore_signal(barrier, inc=1, device_id=sender(y), device_id_type=MESH)

    @pl.when(alone)
    def _():
        pl.semaphore_wait(barrier, 10)

    @pl.when(jnp.logical_not(alone))
    def _():
        pl.semaphore_wait(barrier, 11)

    def quarter(m):
        return pltpu.make_async_remote_copy(
            src_ref=(odd_ref if m % 2 else even_ref),
            dst_ref=turned_ref.at[m],
            send_sem=send_turned.at[m],
            recv_sem=recv_turned.at[m],
            device_id=to_kind(lax.rem(m + col, 4)),
            device_id_type=MESH,
        )

    def stays(m):
        return jnp.logical_and(alone, lax.rem(m + col, 4) == core)

    def keep_quarter(m):
        return pltpu.make_async_copy(
            odd_ref if m % 2 else even_ref, turned_ref.at[m], send_turned.at[m]
        )

    def copy(c, p, slot, peer, width):
        part = out_ref.at[c, p, pl.ds(0, width)]
        return pltpu.make_async_remote_copy(
            src_ref=part,
            dst_ref=part,
            send_sem=send.at[slot],
            recv_sem=recv.at[c, p],
            device_id=peer,
            device_id_type=MESH,
        )

    for zz in range(2):
        mine = zz * 4 + row

        @pl.when(z == zz)
        def _():
            part = pl.ds(0, zz + 1)
            own = pltpu.make_async_copy(piece_ref.at[part], out_ref.at[col, mine, part], local)
            own.start()
            own.wait()
            for i, peer in enumerate(mates):
                copy(col, mine, i, peer, zz + 1).start()

    for m in range(4):

        @pl.when(stays(m))
        def _():
            keep_quarter(m).start()

        @pl.when(jnp.logical_not(stays(m)))
        def _():
            quarter(m).start()

    for zz in range(2):
        p = zz * 4 + row
        n = zz

        @pl.when(z != zz)
        def _():
            copy(col, p, 0, other, zz + 1).wait_recv()

        copy(col, p, 3 + zz, across, zz + 1).start()
        copy(col, p, 5 + n, sides[0], zz + 1).start()
        copy(col, p, 7 + n, sides[1], zz + 1).start()
        copy(col, p, 9 + n, other, zz + 1).start()
    opposite = lax.rem(row + 2, 4)
    for zz in range(2):
        p = zz * 4 + opposite
        n = zz
        copy(col, p, 0, other, zz + 1).wait_recv()
        copy(col, p, 11 + n, sides[0], zz + 1).start()
        copy(col, p, 13 + n, sides[1], zz + 1).start()
        copy(col, p, 15 + n, other, zz + 1).start()
    for i, who in enumerate((row, opposite)):
        for zz in range(2):
            p = zz * 4 + who
            n = i * 2 + zz
            copy(down, p, 0, other, zz + 1).wait_recv()
            copy(down, p, 17 + n, other, zz + 1).start()

            @pl.when(core == 0)
            def _():
                copy(down, p, 21 + n, sides[0], zz + 1).start()

            copy(up, p, 0, other, zz + 1).wait_recv()
            copy(up, p, 25 + n, other, zz + 1).start()

            @pl.when(core == 1)
            def _():
                copy(up, p, 21 + n, sides[1], zz + 1).start()

    far = lax.rem(col + 2, 4)
    for i, who in enumerate((row, opposite)):
        for zz in range(2):
            p = zz * 4 + who
            copy(far, p, 0, other, zz + 1).wait_recv()
            copy(far, p, 29 + i * 2 + zz, other, zz + 1).start()
    for c in range(4):
        for zz in range(2):
            for hh in range(2):
                copy(c, zz * 4 + hh * 2 + 1 - core, 0, other, zz + 1).wait_recv()

    for zz in range(2):

        @pl.when(z == zz)
        def _():
            for i in range(3):
                copy(col, row, i, other, zz + 1).wait_send()

        for i in (3, 5, 7, 9, 11, 13, 15, 17, 19, 21, 23, 25, 27, 29, 31):
            copy(col, row, i + zz, other, zz + 1).wait_send()

    for m in range(4):

        @pl.when(stays(m))
        def _():
            keep_quarter(m).wait()

        @pl.when(jnp.logical_not(stays(m)))
        def _():
            quarter(m).wait()


def leaf(d_ref, li_ref):
    a_rows = [d_ref[8 * g : 8 * g + 8, :] for g in range(16)]
    lane = lax.broadcasted_iota(jnp.int32, (8, TB), 1)
    sub = lax.broadcasted_iota(jnp.int32, (8, TB), 0)
    b_rows = [(lane == sub + 8 * g).astype(F32) for g in range(16)]
    wide = lambda x: jnp.broadcast_to(x, (8, TB))
    for g0 in range(16):
        j = 8 * g0
        c = [wide(a_rows[g0][:, j + q : j + q + 1]) for q in range(8)]
        e = [[wide(c[q][i : i + 1, :]) if i >= q else None for q in range(8)] for i in range(8)]
        a = [wide(a_rows[g0][q : q + 1, :]) for q in range(8)]
        b = [wide(b_rows[g0][q : q + 1, :]) for q in range(8)]
        more = g0 + 1 < 16
        if more:
            m = [wide(a_rows[g0 + 1][:, j + q : j + q + 1]) for q in range(8)]
        s, t = [None] * 8, [None] * 8
        low = [[None] * 8 for _ in range(8)]
        for q in range(8):
            inv = 1.0 / e[q][q]
            s[q], t[q] = a[q] * inv, b[q] * inv
            for i in range(q + 1, 8):
                low[i][q] = e[i][q] * inv
            for i in range(q + 1, 8):
                for p in range(q + 1, i + 1):
                    e[i][p] = e[i][p] - low[i][q] * e[p][q]
            for i in range(q + 1, 8):
                a[i] = a[i] - low[i][q] * a[q]
                b[i] = b[i] - low[i][q] * b[q]
                if more:
                    m[i] = m[i] - low[i][q] * m[q]
            if more:
                a_rows[g0 + 1] = a_rows[g0 + 1] - m[q] * s[q]
                b_rows[g0 + 1] = b_rows[g0 + 1] - m[q] * t[q]
            li_ref[j + q : j + q + 1, :] = (b[q] * lax.rsqrt(e[q][q]))[0:1, :]
        if g0 + 2 < 16:
            for q in range(7, -1, -1):
                for i in range(q + 1, 8):
                    s[q] = s[q] - low[i][q] * s[i]
                    t[q] = t[q] - low[i][q] * t[i]
            for g in range(g0 + 2, 16):
                m = [wide(a_rows[g][:, j + q : j + q + 1]) for q in range(8)]
                da, db = m[0] * s[0], m[0] * t[0]
                for q in range(1, 8):
                    da, db = da + m[q] * s[q], db + m[q] * t[q]
                a_rows[g] = a_rows[g] - da
                b_rows[g] = b_rows[g] - db


def factor_kernel(s_ref, m_ref, li_ref, d_ref):
    blocks, pair_width = K // TB, 2 * TB
    for c in range(4):
        for v in range(2):
            u = 4 * v + c
            for p in range(u, blocks):
                m_ref[p * TB : (p + 1) * TB, u * TB : (u + 1) * TB] = s_ref[c, p, v]

    def step(k, _):
        here = pl.ds(pl.multiple_of(k * TB, TB), TB)
        d_ref[...] = m_ref[here, here]
        leaf(d_ref, li_ref.at[k])
        m_ref[:, here] = nt(m_ref[:, here], li_ref[k])

        @pl.when(lax.rem(k, 2) == 0)
        def _():
            after = pl.ds(pl.multiple_of((k + 1) * TB, TB), TB)
            m_ref[:, after] = m_ref[:, after] - nt(m_ref[:, here], m_ref[after, here])

        @pl.when(lax.rem(k, 2) == 1)
        def _():
            pair = pl.ds(pl.multiple_of((k - 1) * TB, TB), pair_width)

            def trail(i, _):
                part = pl.ds(pl.multiple_of(i * pair_width, pair_width), pair_width)
                m_ref[:, part] = m_ref[:, part] - nt(m_ref[:, pair], m_ref[part, pair])
                return 0

            lax.fori_loop((k + 1) // 2, blocks // 2, trail, 0)

        return 0

    lax.fori_loop(0, blocks, step, 0)


def solve_kernel(col_ref, l_ref, li_ref, own_ref, low_ref, high_ref, far_ref, y_ref, x_ref, m_ref):
    blocks, pair_width = K // TB, 2 * TB
    col = col_ref[0]
    for part, ref in enumerate((own_ref, high_ref, far_ref, low_ref)):
        for v in range(2):
            u = 4 * v + lax.rem(col + part, 4)
            m_ref[:, pl.ds(pl.multiple_of(u * TB, TB), TB)] = ref[v]

    def places(n):
        at = n * pair_width
        return (
            pl.ds(pl.multiple_of(at, TB), TB),
            pl.ds(pl.multiple_of(at + TB, TB), TB),
            pl.ds(pl.multiple_of(at, pair_width), pair_width),
        )

    def forth(n, _):
        first, last, pair = places(n)
        m_ref[:, first] = nt(m_ref[:, first], li_ref[2 * n])
        rest = m_ref[:, last] - nt(m_ref[:, first], l_ref[last, first])
        m_ref[:, last] = nt(rest, li_ref[2 * n + 1])

        def trail(i, _):
            part = places(i)[2]
            m_ref[:, part] = m_ref[:, part] - nt(m_ref[:, pair], l_ref[part, pair])
            return 0

        lax.fori_loop(n + 1, blocks // 2, trail, 0)
        return 0

    lax.fori_loop(0, blocks // 2, forth, 0)
    for v in range(2):
        y_ref[v] = m_ref[:, pl.ds(pl.multiple_of((4 * v + col) * TB, TB), TB)]

    def back(i, _):
        n = blocks // 2 - 1 - i
        first, last, pair = places(n)
        x_ref[:, last] = nn(m_ref[:, last], li_ref[2 * n + 1])
        rest = m_ref[:, first] - nn(x_ref[:, last], l_ref[last, first])
        x_ref[:, first] = nn(rest, li_ref[2 * n])

        def lead(j, _):
            part = places(j)[2]
            m_ref[:, part] = m_ref[:, part] - nn(x_ref[:, pair], l_ref[pair, part])
            return 0

        lax.fori_loop(0, n, lead, 0)
        return 0

    lax.fori_loop(0, blocks // 2, back, 0)


def split(x):
    high = x.astype(jnp.bfloat16)
    return high, (x - high.astype(F32)).astype(jnp.bfloat16)


def place_rows(tile, first, t, rinv_ref, cinv_ref, load, less, out_ref):
    groups = range(0, out_ref.shape[-2], 8)
    index = [jnp.maximum(cinv_ref[t, g : g + 8], 0) for g in groups]
    live = [(cinv_ref[t, g : g + 8] >= 0).astype(F32) for g in groups]
    count = out_ref.shape[0]

    def body(o, _):
        s = rinv_ref[t, tile * TB + first + o]
        weight = jnp.where(s >= 0, 1.0, 0.0)
        s = jnp.maximum(s, 0)
        for g, at, keep in zip(groups, index, live):
            x = jnp.take_along_axis(load(s, g), at, axis=1) * (keep * weight)
            out_ref[o, g : g + 8] = x if less is None else x + less(o, g)
        return 0

    lax.fori_loop(0, count, body, 0, unroll=16)


def keep_kernel(
    at_ref, rinv_ref, kept_ref, sent_ref, cinv_ref, out_ref, main_ref, thin_ref
):
    main_ref[0] = sent_ref[0, 0, 0, :, 8:, :]
    for v in range(2, 8):
        thin_ref[v - 2] = sent_ref[0, 0, 0, :, v, :]

    def load(s, g):
        return kept_ref[0, 0, 0, s, g : g + 8]

    place_rows(pl.program_id(0), 0, 0, rinv_ref, cinv_ref, load, None, out_ref.at[0, 0])


def finish_kernel(
    rinv_ref, got_ref, thin_ref, cinv_ref, kept_ref, r_ref, out_ref, first_ref
):
    @pl.when(pl.program_id(0) == 0)
    def _():
        first_ref[: 2 * TB, :] = jnp.zeros((2 * TB, TB), F32)

    tile, first = pl.program_id(0) // 2, lax.rem(pl.program_id(0), 2) * (TB // 2)
    for v in range(2, 8):
        first_ref[v * TB : (v + 1) * TB, :] = thin_ref[v - 2]

    def load(s, g):
        if g == 0:
            return first_ref[pl.ds(s, 8, stride=TB), :]
        return got_ref[0, s, g - 8 : g]

    def less(o, g):
        return kept_ref[0, 0, o, g : g + 8] - r_ref.at[0][pl.ds(g * TB + first + o, 8, stride=TB), :]

    place_rows(tile, first, 1, rinv_ref, cinv_ref, load, less, out_ref.at[0, 0])


def update_kernel(
    at_ref, g_ref, x_ref, y_ref, diag_ref, out_ref, wh_ref, wl_ref, xh_ref, xl_ref
):
    step = pl.program_id(0)
    tiles = out_ref.shape[0]

    @pl.when(step == 0)
    def _():
        xh_ref[...], xl_ref[...] = split(x_ref[...])

    for n in range(8):
        part = slice(n * TB, (n + 1) * TB)
        for m in range(4):
            q = lax.rem(at_ref[2] + n // 4 + 4 - m, 4)
            for v in range(2):
                high, low = split(g_ref[(n % 4) * 2 + n // 4, m, v])
                there = pl.ds(pl.multiple_of((4 * v + q) * TB, TB), TB)
                wh_ref[part, there] = high
                wl_ref[part, there] = low
    dims = (((1,), (1,)), ((), ()))
    dot = lambda a, b: lax.dot_general(a, b, dims, preferred_element_type=F32)
    for n in range(0, 8, 2):
        part = slice(n * TB, (n + 2) * TB)
        wh, wl = wh_ref[part, :], wl_ref[part, :]
        r = (dot(xl_ref[...], wh) + dot(xh_ref[...], wl)) + dot(xh_ref[...], wh)
        for i in range(2):
            for j in range(tiles):
                out_ref[j, (n + i) * TB : (n + i + 1) * TB, :] = r[
                    j * TB : (j + 1) * TB, i * TB : (i + 1) * TB
                ]
    sub = lax.broadcasted_iota(jnp.int32, (TB, TB), 0)
    lane = lax.broadcasted_iota(jnp.int32, (TB, TB), 1)
    here = pl.ds(pl.multiple_of(at_ref[1] * TB, TB), TB)
    out_ref[step, here, :] = out_ref[step, here, :] - jnp.where(
        sub == lane, diag_ref[pl.ds(step, 1), :], 0.0
    )

    @pl.when(step == 0)
    def _():
        for v in range(2):
            for j in range(tiles):
                out_ref[j, v * TB : (v + 1) * TB, :] = -y_ref[v, j * TB : (j + 1) * TB, :]


def inverse(relative):
    offsets = jnp.arange(TB, dtype=jnp.int32)
    hit = relative[..., None, :] == offsets[:, None]
    return jnp.max(jnp.where(hit, offsets, -1), axis=-1)


def on_device(child_update, child_map, parent_diag):
    cube, row, col = lax.axis_index("cube"), lax.axis_index("row"), lax.axis_index("col")
    grid, columns = 32, 4
    position = cube * 4 + row
    sibling = position // (grid // 2)
    block = child_update[0]
    tiles, cols = block.shape[1], block.shape[3]
    rows = tiles * TB
    trade = [(i, i ^ 16) for i in range(grid)]

    raw = jnp.transpose(block[:, :, :, :2, :], (0, 3, 1, 2, 4)).reshape(2, 2, rows, TB)
    got = lax.ppermute(raw, ("cube", "row"), trade)
    maps = jnp.stack(
        [
            lax.dynamic_index_in_dim(child_map, sibling, 0, keepdims=False),
            lax.dynamic_index_in_dim(child_map, 1 - sibling, 0, keepdims=False),
        ]
    )
    within = position % 16
    pair_tiles = (
        grid * jnp.arange(tiles, dtype=jnp.int32)[None, :]
        + 16 * jnp.arange(2, dtype=jnp.int32)[:, None]
        + within
    )
    pair_maps = jnp.swapaxes(
        lax.dynamic_index_in_dim(
            maps.reshape(2, tiles, 2, 16, TB), within, 3, keepdims=False
        ),
        1,
        2,
    )
    pair_maps = pair_maps - TB * pair_tiles[None, :, :, None]
    row_maps = lax.dynamic_index_in_dim(pair_maps, sibling, 1, keepdims=False)
    col_maps = lax.dynamic_index_in_dim(
        maps.reshape(2, cols, columns, TB), col, 2, keepdims=False
    )
    col_tiles = columns * jnp.arange(cols, dtype=jnp.int32) + col
    col_maps = col_maps - TB * col_tiles[None, :, None]
    pair_diag = jnp.swapaxes(
        lax.dynamic_index_in_dim(
            parent_diag.reshape(tiles, 2, 16, TB), within, 2, keepdims=False
        ),
        0,
        1,
    )
    diag = lax.dynamic_index_in_dim(pair_diag, sibling, 0, keepdims=False)
    meets = pair_tiles[:, None, :] == col_tiles[None, :2, None]
    panel_diag = jnp.where(meets[..., None], pair_diag[:, None], 0.0)

    row_inverse = inverse(row_maps).reshape(2, rows)
    solved = jnp.arange(cols) < 2
    col_inverse = jnp.where(solved[None, :, None], -1, inverse(col_maps))
    here = jnp.logical_and(row == col, jnp.logical_or(jnp.arange(tiles) > 0, cube >= 2))
    trailing_diag = jnp.where(here[:, None], diag, 0.0)
    crossed = (row // 2 != col // 2).astype(jnp.int32)
    at = jnp.stack([sibling, cube, 2 * crossed]).astype(jnp.int32)
    whole = jax.ShapeDtypeStruct((1, tiles, TB, cols, TB), F32)
    all_maps = pl.BlockSpec((2, cols, TB), lambda i, *_: (0, 0, 0))
    result, main, thin = pl.pallas_call(
        keep_kernel,
        out_shape=[
            whole,
            jax.ShapeDtypeStruct((tiles, TB, cols - 8, TB), F32),
            jax.ShapeDtypeStruct((6, rows, TB), F32),
        ],
        grid_spec=pltpu.PrefetchScalarGridSpec(
            num_scalar_prefetch=2,
            grid=(tiles,),
            in_specs=[
                pl.BlockSpec(
                    (1, 1, 1, TB, cols, TB), lambda i, at, _: (0, at[0], i, 0, 0, 0)
                ),
                pl.BlockSpec((1, 1, 1, TB, cols, TB), lambda i, at, _: (0, 1 - at[0], i, 0, 0, 0)),
                all_maps,
            ],
            out_specs=[
                pl.BlockSpec((1, 1, TB, cols, TB), lambda i, *_: (0, i, 0, 0, 0)),
                pl.BlockSpec((1, TB, cols - 8, TB), lambda i, *_: (i, 0, 0, 0)),
                pl.BlockSpec((6, TB, TB), lambda i, *_: (0, i, 0)),
            ],
        ),
    )(at, row_inverse, child_update, child_update, col_inverse)
    main, thin, got = lax.optimization_barrier((main, thin, got))
    arrived = []
    for part in (thin, main):
        arrived.append(lax.ppermute(part, ("cube", "row"), trade))

    strip = jax.ShapeDtypeStruct((2, rows, TB), F32)
    own, even, odd, piece = pl.pallas_call(
        place_kernel,
        out_shape=[strip, strip, strip, jax.ShapeDtypeStruct((2, TB, TB), F32)],
        in_specs=[SMEM] + [VMEM] * 5,
        out_specs=[VMEM] * 4,
        scratch_shapes=[pltpu.VMEM((4, 2, rows, TB), F32)],
    )(
        jnp.stack([sibling, col % 2]).astype(jnp.int32),
        raw, got, pair_maps, col_maps[:, :2], panel_diag,
    )

    pivot, turned = pl.pallas_call(
        pivot_kernel,
        out_shape=[
            jax.ShapeDtypeStruct((4, 8, 2, TB, TB), F32),
            jax.ShapeDtypeStruct((4, 2, rows, TB), F32),
        ],
        in_specs=[VMEM, ANY, ANY],
        out_specs=[VMEM, ANY],
        scratch_shapes=[
            pltpu.SemaphoreType.DMA((33,)),
            pltpu.SemaphoreType.DMA((4, 8)),
            pltpu.SemaphoreType.DMA,
            pltpu.SemaphoreType.DMA((4,)),
            pltpu.SemaphoreType.DMA((4,)),
        ],
        compiler_params=pltpu.CompilerParams(collective_id=0, has_side_effects=True),
    )(piece, even, odd)

    groups = [
        [(s * 4 + z) * 4 + half * 2 + core for z in range(4) for core in range(2)]
        for s in range(2)
        for half in range(2)
    ]
    others = lax.all_gather(turned, ("cube", "row"), axis=0, axis_index_groups=groups)
    own, pivot = lax.optimization_barrier((own, pivot))
    strips = []
    for hop in (1, 3, 2):
        strips.append(lax.ppermute(own, "col", [(c, (c + hop) % 4) for c in range(4)]))

    lower, inverses = pl.pallas_call(
        factor_kernel,
        out_shape=[jax.ShapeDtypeStruct((K, K), F32), jax.ShapeDtypeStruct((K // TB, TB, TB), F32)],
        in_specs=[VMEM],
        out_specs=[VMEM, VMEM],
        scratch_shapes=[pltpu.VMEM((TB, TB), F32)],
    )(pivot)
    y, x = pl.pallas_call(
        solve_kernel,
        out_shape=[
            jax.ShapeDtypeStruct((2, rows, TB), F32),
            jax.ShapeDtypeStruct((rows, K), F32),
        ],
        in_specs=[SMEM] + [VMEM] * 6,
        out_specs=[VMEM, VMEM],
        scratch_shapes=[pltpu.VMEM((rows, K), F32)],
    )(col.reshape(1), lower, inverses, own, *strips)

    update = pl.pallas_call(
        update_kernel,
        out_shape=jax.ShapeDtypeStruct((tiles, cols * TB, TB), F32),
        grid_spec=pltpu.PrefetchScalarGridSpec(
            num_scalar_prefetch=1,
            grid=(cols // 8,),
            in_specs=[
                pl.BlockSpec((8, 4, 2, TB, TB), lambda i, *_: (0, 0, 0, i, 0)),
                VMEM,
                VMEM,
                VMEM,
            ],
            out_specs=pl.BlockSpec((tiles, 8 * TB, TB), lambda i, *_: (0, i, 0)),
            scratch_shapes=[
                pltpu.VMEM((8 * TB, K), jnp.bfloat16),
                pltpu.VMEM((8 * TB, K), jnp.bfloat16),
                pltpu.VMEM((rows, K), jnp.bfloat16),
                pltpu.VMEM((rows, K), jnp.bfloat16),
            ],
        ),
    )(at, others, x, y, trailing_diag)
    own_block = pl.BlockSpec((1, 1, TB // 2, cols, TB), lambda i, *_: (0, i // 2, i % 2, 0, 0))
    return pl.pallas_call(
        finish_kernel,
        out_shape=whole,
        grid_spec=pltpu.PrefetchScalarGridSpec(
            num_scalar_prefetch=1,
            grid=(2 * tiles,),
            in_specs=[
                pl.BlockSpec((1, TB, cols - 8, TB), lambda i, *_: (i // 2, 0, 0, 0)),
                pl.BlockSpec((6, TB, TB), lambda i, *_: (0, i // 2, 0)),
                all_maps,
                own_block,
                pl.BlockSpec((1, cols * TB, TB), lambda i, *_: (i // 2, 0, 0)),
            ],
            out_specs=own_block,
            scratch_shapes=[pltpu.VMEM((8 * TB, TB), F32)],
        ),
    )(row_inverse, arrived[1], arrived[0], col_inverse, result, update)


def solution(mesh):
    return jax.shard_map(
        on_device,
        mesh=mesh,
        in_specs=(P(("cube", "row"), None, None, None, "col", None), P(), P()),
        out_specs=P(("cube", "row"), None, None, "col", None),
        check_vma=False,
    )
```
